128 devices in a mesh: row: 16 (over z, y), col: 8 (over x, core).
Axes of the slice: x: 4, y: 4, z: 4, core: 2. Of those that a mesh axis runs over, the one named last changes fastest.
Arguments:
- x_blocks: bfloat16 [128, 16, 128, 128], P('row', 'col')
- x_cols: int32 [128, 16], P('row', 'col'), may hold values from 0 to 15, as said below
- x_count: int32 [128, 8], P('row', 'col'), may hold values from 0 to 2, as said below
- y_cols: int32 [128, 96], P('row', 'col'), may hold values from 0 to 15, as said below
- y_count: int32 [128, 8], P('row', 'col'), may hold values from 0 to 12, as said below
- branch_flag: int32 [128], P('row'), may hold values from 0 to 1
Outputs:
- new_blocks: bfloat16 [128, 96, 128, 128], P('row', 'col')
- new_trace: float32 [1], replicated
The draws below stay inside these ranges and needn't reach their ends.
Inputs may be any that keep to these rules, and one draw needn't show every extreme that they name: `x_cols`: within one block row and one column group, the first x_count slots name distinct block columns; other slots hold arbitrary valid columns. Slot 0 of block row I in group I // 16 names column I % 16. `x_count`: reaches 2; at least 1 for block row I in group I // 16. `y_cols`: within one block row and one column group, the first y_count slots name distinct block columns. Slot 0 of block row I in group I // 16 names column I % 16. `y_count`: reaches 12; at least 1 for block row I in group I // 16.
All inputs are finite; a program needn't handle non-finite values.
Results may differ from the reference program's by a relative error of at most 0.0004.
Values may be sent and summed in bfloat16 or wider, within the bound.
A program may use at most 128 MiB of HBM per device.

```python
import jax
import jax.numpy as jnp
from jax import lax

NB = 128
BS = 128
ROWCAP = 2
YCAP = 12
N_ROW = 16
N_COL = 8


def column_lists(key, slot_count):
    width = NB // N_COL
    scores = jax.random.randint(key, (NB, N_COL, width), 0, 2 ** 20) * width + jnp.arange(width, dtype=jnp.int32)
    rows = jnp.arange(NB, dtype=jnp.int32)
    own_group = (rows // width)[:, None, None] == jnp.arange(N_COL, dtype=jnp.int32)[None, :, None]
    own_col = (rows % width)[:, None, None] == jnp.arange(width, dtype=jnp.int32)[None, None, :]
    scores = jnp.where(own_group & own_col, -1, scores)
    order = jnp.argsort(scores, axis=-1, stable=True).astype(jnp.int32)
    return order[:, :, :slot_count].reshape((NB, N_COL * slot_count))


def diagonal_groups():
    width = NB // N_COL
    rows = jnp.arange(NB, dtype=jnp.int32)
    return (rows // width)[:, None] == jnp.arange(N_COL, dtype=jnp.int32)[None, :]


def draw_x_cols(key, part):
    return column_lists(jax.random.fold_in(key, 11), ROWCAP)


def draw_y_cols(key, part):
    return column_lists(jax.random.fold_in(key, 23), YCAP)


def draw_x_count(key, part):
    values = jax.random.randint(jax.random.fold_in(key, 37), (NB, N_COL), 0, ROWCAP + 2)
    values = jnp.minimum(values, ROWCAP)
    return jnp.where(diagonal_groups(), jnp.maximum(values, 1), values).astype(jnp.int32)


def draw_y_count(key, part):
    values = jax.random.randint(jax.random.fold_in(key, 41), (NB, N_COL), 0, YCAP + 2)
    values = jnp.minimum(values, YCAP)
    return jnp.where(diagonal_groups(), jnp.maximum(values, 1), values).astype(jnp.int32)


def draw_x_blocks(key, part):
    width = NB // N_COL
    shape = (NB, N_COL * ROWCAP, BS, BS)
    base = 0.3 * jax.random.normal(jax.random.fold_in(key, 51), shape, jnp.float32)
    noise = 0.3 * jax.random.normal(jax.random.fold_in(key, 53), (NB, BS, BS), jnp.float32)
    symmetric = (noise + jnp.swapaxes(noise, 1, 2)) * 0.7071
    diag_block = 0.5 * jnp.eye(BS, dtype=jnp.float32)[None] + symmetric
    rows = jnp.arange(NB, dtype=jnp.int32)
    slot_ids = jnp.arange(N_COL * ROWCAP, dtype=jnp.int32)
    is_diag = slot_ids[None, :] == (rows // width * ROWCAP)[:, None]
    mixed = jnp.where(is_diag[:, :, None, None], diag_block[:, None], base)
    return mixed.astype(jnp.bfloat16)


def touch_ends(result, stream_key, least, top_value):
    dims = result.shape
    place = [jax.random.randint(jax.random.fold_in(stream_key, axis), (), 0, dims[axis]) for axis in range(len(dims))]
    result = result.at[tuple(place)].set(least)
    longest = dims.index(max(dims))
    place[longest] = (place[longest] + 1) % dims[longest]
    return result.at[tuple(place)].set(top_value)


def setup_inputs(seed: int = 0) -> dict:
    splits = jax.random.split(jax.random.key(seed), 7)
    return {
        "x_blocks": draw_x_blocks(jax.random.fold_in(splits[6], 71), 0),
        "x_cols": draw_x_cols(jax.random.fold_in(splits[6], 71), 0),
        "x_count": draw_x_count(jax.random.fold_in(splits[6], 71), 0),
        "y_cols": draw_y_cols(jax.random.fold_in(splits[6], 71), 0),
        "y_count": draw_y_count(jax.random.fold_in(splits[6], 71), 0),
        "branch_flag": touch_ends(jax.random.randint(splits[5], (NB,), 0, 2), jax.random.fold_in(splits[5], 1), 0, 1).astype(jnp.int32),
    }


def reference(x_blocks, x_cols, x_count, y_cols, y_count, branch_flag):
    row_width = NB // N_ROW
    col_width = NB // N_COL
    pairs = N_COL * ROWCAP

    def window(index):
        row_group = index // N_COL
        col_group = index % N_COL
        row_start = row_group * row_width
        col_start = col_group * col_width
        row_blocks = lax.dynamic_slice_in_dim(x_blocks, row_start, row_width, 0)
        row_cols = lax.dynamic_slice_in_dim(x_cols, row_start, row_width, 0)
        row_count = lax.dynamic_slice_in_dim(x_count, row_start, row_width, 0)
        row_flags = lax.dynamic_slice_in_dim(branch_flag, row_start, row_width, 0)
        panel_blocks = lax.dynamic_slice_in_dim(x_blocks, col_group * ROWCAP, ROWCAP, 1)
        panel_cols = lax.dynamic_slice_in_dim(x_cols, col_group * ROWCAP, ROWCAP, 1)
        panel_count = lax.dynamic_slice_in_dim(x_count, col_group, 1, 1)[:, 0]
        own_blocks = lax.dynamic_slice_in_dim(row_blocks, col_group * ROWCAP, ROWCAP, 1)
        own_cols = lax.dynamic_slice_in_dim(row_cols, col_group * ROWCAP, ROWCAP, 1)
        own_count = lax.dynamic_slice_in_dim(row_count, col_group, 1, 1)
        win_rows = lax.dynamic_slice_in_dim(y_cols, row_start, row_width, 0)
        win_cols = lax.dynamic_slice_in_dim(win_rows, col_group * YCAP, YCAP, 1)
        count_rows = lax.dynamic_slice_in_dim(y_count, row_start, row_width, 0)
        win_count = lax.dynamic_slice_in_dim(count_rows, col_group, 1, 1)

        pair_ids = jnp.arange(pairs, dtype=jnp.int32)
        groups = pair_ids // ROWCAP
        inner_rows = (groups[None, :] * col_width + row_cols).astype(jnp.int32)
        live = (pair_ids % ROWCAP)[None, :] < jnp.take(row_count, groups, axis=1)
        inner_blocks = panel_blocks[inner_rows]
        inner_cols = panel_cols[inner_rows]
        inner_count = panel_count[inner_rows]
        slot_ids = jnp.arange(ROWCAP, dtype=jnp.int32)
        inner_live = slot_ids[None, None, :] < inner_count[..., None]
        partial_value = jnp.einsum("ipab,ipsbc->ipsac", row_blocks.astype(jnp.float32), inner_blocks.astype(jnp.float32))
        y_live = jnp.arange(YCAP, dtype=jnp.int32)[None, :] < win_count
        route = (inner_cols[:, None, :, :] == win_cols[:, :, None, None]) & inner_live[:, None, :, :]
        route = route & live[:, None, :, None] & y_live[:, :, None, None]
        product = jnp.einsum("iyps,ipsac->iyac", route.astype(jnp.float32), partial_value)

        own_ids = jnp.arange(ROWCAP, dtype=jnp.int32)
        own_match = (own_cols[:, None, :] == win_cols[:, :, None]) & (own_ids[None, None, :] < own_count[:, :, None])
        own_term = jnp.einsum("iyq,iqab->iyab", own_match.astype(jnp.float32), own_blocks.astype(jnp.float32))
        flip = (row_flags == 1)[:, None, None, None]
        updated = jnp.where(flip, 2.0 * own_term - product, product)
        updated = jnp.where(y_live[..., None, None], updated, jnp.zeros((), updated.dtype))
        rows_global = row_start + jnp.arange(row_width, dtype=jnp.int32)[:, None]
        diagonal = (rows_global == col_start + win_cols) & y_live
        traces = jnp.trace(updated, axis1=2, axis2=3)
        trace_part = jnp.sum(jnp.where(diagonal, traces, jnp.zeros((), traces.dtype)))
        return updated.astype(jnp.bfloat16), trace_part

    indices = jnp.arange(N_ROW * N_COL, dtype=jnp.int32)
    updated, traces = lax.map(window, indices)
    updated = updated.reshape((N_ROW, N_COL, row_width, YCAP, BS, BS))
    updated = updated.transpose((0, 2, 1, 3, 4, 5)).reshape((NB, N_COL * YCAP, BS, BS))
    return updated, jnp.sum(traces).reshape((1,))
```

```python
import jax
import jax.numpy as jnp
from jax import lax
from jax.experimental import pallas as pl
from jax.experimental.pallas import tpu as pltpu
from jax.sharding import Mesh
from jax.sharding import PartitionSpec as P

BS = 128
ROWS = 8
CAP = 2
YCAP = 12
OWN = ROWS * CAP
LINE = ("z", "y")
ALL = ("z", "y", "x", "core")
MESH_ID = pl.DeviceIdType.MESH
ZERO = 256


def gather_kernel(x_ref, m_ref, strip, panel, smeta, pmeta, psend, precv, xsend, xrecv, csend, crecv, lsem):
    place = {a: lax.axis_index(a) for a in ("z", "y", "x")}
    after = {a: lax.rem(v + 1, 4) for a, v in place.items()}
    before = {a: lax.rem(v + 3, 4) for a, v in place.items()}
    across = {a: lax.rem(v + 2, 4) for a, v in place.items()}
    core = lax.axis_index("core")
    z, y, x = place["z"], place["y"], place["x"]

    barrier = pltpu.get_barrier_semaphore()
    peers = [{a: to[a]} for a in ("z", "y", "x") for to in (after, before)] + [{"core": 1 - core}]
    for peer in peers:
        pl.semaphore_signal(barrier, inc=1, device_id=peer, device_id_type=MESH_ID)

    here = z * 4 + y
    local = [
        pltpu.make_async_copy(x_ref, panel.at[here], lsem.at[0]),
        pltpu.make_async_copy(x_ref, strip.at[x * 2 + core], lsem.at[1]),
        pltpu.make_async_copy(m_ref, pmeta.at[here], lsem.at[2]),
        pltpu.make_async_copy(m_ref, smeta.at[x * 2 + core], lsem.at[3]),
    ]
    for c in local:
        c.start()
    panel[16, 0] = jnp.zeros((BS, BS), jnp.bfloat16)
    pl.semaphore_wait(barrier, len(peers))

    sends = []

    def copy(src, dst, ss, rs, peer):
        return pltpu.make_async_remote_copy(
            src_ref=src, dst_ref=dst, send_sem=ss, recv_sem=rs, device_id=peer, device_id_type=MESH_ID
        )

    def start(*args):
        c = copy(*args)
        c.start()
        sends.append(c)

    class Ring:
        def __init__(self, axis, at, ssem, rsem, j, halves=2):
            self.axis, self.at, self.ssem, self.rsem, self.j, self.halves = axis, at, ssem, rsem, j, halves

        def own(self, src=None):
            dst = self.at(place[self.axis], None)
            src = dst if src is None else src
            for q, to in ((0, after), (1, before)):
                start(src, dst, self.ssem.at[self.j, q], self.rsem.at[self.j, q], {self.axis: to[self.axis]})

        def arrive(self, q):
            owner = (before, after)[q][self.axis]
            dst = self.at(owner, None)
            copy(dst, dst, self.ssem.at[self.j, q], self.rsem.at[self.j, q], {self.axis: owner}).wait_recv()
            if q < self.halves:
                half = self.at(owner, q if self.halves == 2 else None)
                to = (after, before)[q][self.axis]
                start(half, half, self.ssem.at[self.j, 2 + q], self.rsem.at[self.j, 2 + q], {self.axis: to})

        def arrive_across(self):
            for q in range(self.halves):
                half = self.at(across[self.axis], q if self.halves == 2 else None)
                copy(half, half, self.ssem.at[self.j, 2 + q], self.rsem.at[self.j, 2 + q],
                     {self.axis: before[self.axis]}).wait_recv()

    def panel_ring(axis, d, lo, j):
        def at(p, half):
            o = lax.rem((y if axis == "z" else z) + d, 4)
            g = p * 4 + o if axis == "z" else o * 4 + p
            return panel.at[g, pl.ds(lo, 8)] if half is None else panel.at[g, pl.ds(lo + 4 * half, 4)]

        return Ring(axis, at, psend, precv, j)

    def pmeta_ring(axis, d, j):
        def at(p, half):
            o = lax.rem((y if axis == "z" else z) + d, 4)
            return pmeta.at[p * 4 + o if axis == "z" else o * 4 + p]

        return Ring(axis, at, psend, precv, j, halves=1)

    def strip_at(p, half):
        g = p * 2 + core
        return strip.at[g] if half is None else strip.at[g, pl.ds(8 * half, 8)]

    az, by = panel_ring("z", 0, 0, 0), panel_ring("y", 0, 8, 1)
    ay = {d: panel_ring("y", d, 0, j) for d, j in ((0, 2), (3, 4), (1, 5), (2, 8))}
    bz = {d: panel_ring("z", d, 8, j) for d, j in ((0, 3), (3, 6), (1, 7), (2, 9))}
    mz = pmeta_ring("z", 0, 10)
    my = {d: pmeta_ring("y", d, j) for d, j in ((0, 11), (3, 12), (1, 13), (2, 14))}
    xs = Ring("x", strip_at, xsend, xrecv, 0)
    xm = Ring("x", lambda p, half: smeta.at[p * 2 + core], xsend, xrecv, 1, halves=1)

    def swap(p, j):
        g = p * 2 + core
        start(strip.at[g], strip.at[g], csend.at[0, j], crecv.at[0, j], {"core": 1 - core})
        start(smeta.at[g], smeta.at[g], csend.at[1, j], crecv.at[1, j], {"core": 1 - core})

    az.own(x_ref.at[pl.ds(0, 8)])
    by.own(x_ref.at[pl.ds(8, 8)])
    mz.own(m_ref)
    my[0].own(m_ref)
    ay[0].own(x_ref.at[pl.ds(0, 8)])
    bz[0].own(x_ref.at[pl.ds(8, 8)])
    xm.own(m_ref)
    xs.own(x_ref)
    for c in local:
        c.wait()
    swap(x, 0)
    for q, d in ((0, 3), (1, 1)):
        az.arrive(q)
        ay[d].own()
        by.arrive(q)
        bz[d].own()
        mz.arrive(q)
        my[d].own()
        my[0].arrive(q)
    for q in (0, 1):
        xs.arrive(q)
        xm.arrive(q)
        swap((before, after)[q]["x"], 1 + q)
    for q in (0, 1):
        ay[0].arrive(q)
        bz[0].arrive(q)
    az.arrive_across()
    ay[2].own()
    by.arrive_across()
    bz[2].own()
    mz.arrive_across()
    my[2].own()
    my[0].arrive_across()
    for d in (3, 1):
        for q in (0, 1):
            ay[d].arrive(q)
            bz[d].arrive(q)
            my[d].arrive(q)
    xs.arrive_across()
    xm.arrive_across()
    swap(across["x"], 3)
    for q in (0, 1):
        ay[2].arrive(q)
        bz[2].arrive(q)
        my[2].arrive(q)
    for d in (0, 3, 1, 2):
        ay[d].arrive_across()
        bz[d].arrive_across()
        if d:
            my[d].arrive_across()
    for p, j in ((x, 0), (before["x"], 1), (after["x"], 2), (across["x"], 3)):
        g = p * 2 + 1 - core
        copy(strip.at[g], strip.at[g], csend.at[0, j], crecv.at[0, j], {"core": 1 - core}).wait_recv()
        copy(smeta.at[g], smeta.at[g], csend.at[1, j], crecv.at[1, j], {"core": 1 - core}).wait_recv()
    for c in sends:
        c.wait_send()


def product_kernel(where, smeta, pmeta, y_cols, y_count, flag, strip, panel, out, part, obuf, diag,
                   slot, cnt, la, lb, own, osem):
    chunk, on_diag = where[0], where[1]
    diag[...] = jnp.zeros_like(diag)

    def row(i, carry):
        live_y = y_count[i, 0]
        for j in range(17):
            slot[j] = YCAP
        for t in range(YCAP):
            slot[jnp.where(t < live_y, y_cols[i, t], 16)] = t
        slot[16] = YCAP
        for t in range(YCAP + 1):
            cnt[t] = 0
            own[t] = ZERO
            la[t, 0] = 0
            la[t, 1] = 0
            lb[t, 0] = ZERO
            lb[t, 1] = ZERO
        for q in range(CAP):
            live = q < pmeta[chunk, 0, i * 4 + 2]
            t = slot[jnp.where(live, pmeta[chunk, 0, i * 4 + q], 16)]
            own[t] = chunk * OWN + i * CAP + q

        def pairs(g, c):
            n_live = smeta[g, 0, i * 4 + 2]
            for s in range(CAP):
                @pl.when(s < n_live)
                def _():
                    k = g * 16 + smeta[g, 0, i * 4 + s]
                    kc, kr = k // 8, k % 8
                    n_in = pmeta[kc, 0, kr * 4 + 2]
                    for w in range(CAP):
                        t = slot[jnp.where(w < n_in, pmeta[kc, 0, kr * 4 + w], 16)]
                        n = cnt[t]
                        la[t, n] = g * OWN + i * CAP + s
                        lb[t, n] = k * CAP + w
                        cnt[t] = n + 1
            return c

        lax.fori_loop(0, 8, pairs, 0)
        flip = flag[i] == 1
        sign = jnp.where(flip, -1.0, 1.0)
        twice = jnp.where(flip, 2.0, 0.0)

        def dot2(t, n):
            a = jnp.concatenate([strip[la[t, n]], strip[la[t, n + 1]]], axis=1)
            b = jnp.concatenate([panel[lb[t, n]], panel[lb[t, n + 1]]], axis=0)
            return jnp.dot(a, b, preferred_element_type=jnp.float32)

        def finish(t, product):
            return sign * product + twice * panel[own[t]].astype(jnp.float32)

        for t in range(YCAP):
            updated = finish(t, dot2(t, 0))
            obuf[i, t] = updated.astype(jnp.bfloat16)
            if t == 0:
                diag[1] = updated

        def more(t, c):
            n = cnt[t]

            @pl.when(n > 2)
            def _():
                la[t, n] = 0
                lb[t, n] = ZERO
                product = lax.fori_loop(
                    1, (n + 1) // 2, lambda h, acc: acc + dot2(t, h * 2), dot2(t, 0)
                )
                updated = finish(t, product)
                obuf[i, t] = updated.astype(jnp.bfloat16)

                @pl.when(t == 0)
                def _():
                    diag[1] = updated

            return c

        lax.fori_loop(0, YCAP, more, 0)
        diag[0] += diag[1]
        pltpu.make_async_copy(obuf.at[i], out.at[i], osem.at[i]).start()
        return carry

    lax.fori_loop(0, ROWS, row, 0)
    eye = lax.broadcasted_iota(jnp.int32, (BS, BS), 0) == lax.broadcasted_iota(jnp.int32, (BS, BS), 1)
    total = jnp.sum(jnp.where(eye & (on_diag == 1), diag[0], 0.0))
    part[...] = jnp.full(part.shape, total)
    for i in range(ROWS):
        pltpu.make_async_copy(obuf.at[i], out.at[i], osem.at[i]).wait()


def on_device(x_blocks, x_cols, x_count, y_cols, y_count, branch_flag):
    meta = jnp.concatenate([x_cols, x_count, branch_flag[:, None]], axis=1)
    meta = jnp.pad(meta.reshape(1, 32), ((0, 0), (0, 96)))
    vmem, anywhere, smem = (pl.BlockSpec(memory_space=m) for m in (pltpu.VMEM, pl.ANY, pltpu.SMEM))
    blocks = x_blocks.reshape(OWN, BS, BS)
    dma = pltpu.SemaphoreType.DMA
    strip, panel, smeta, pmeta = pl.pallas_call(
        gather_kernel,
        out_shape=[
            pltpu.VMEM((8, OWN, BS, BS), jnp.bfloat16),
            pltpu.VMEM((17, OWN, BS, BS), jnp.bfloat16),
            pltpu.VMEM((8, 1, BS), jnp.int32),
            pltpu.VMEM((16, 1, BS), jnp.int32),
        ],
        in_specs=[anywhere, vmem],
        out_specs=[vmem] * 4,
        scratch_shapes=[dma((15, 4)), dma((15, 4)), dma((2, 4)), dma((2, 4)), dma((2, 4)), dma((2, 4)), dma((4,))],
        compiler_params=pltpu.CompilerParams(
            collective_id=0, has_side_effects=True, vmem_limit_bytes=16 << 20
        ),
    )(blocks, meta)
    chunk = lax.axis_index("z") * 4 + lax.axis_index("y")
    group = lax.axis_index("x") * 2 + lax.axis_index("core")
    where = jnp.stack([chunk, (chunk // 2 == group).astype(jnp.int32)])
    out, part = pl.pallas_call(
        product_kernel,
        out_shape=[
            jax.ShapeDtypeStruct((ROWS, YCAP, BS, BS), jnp.bfloat16),
            jax.ShapeDtypeStruct((8, BS), jnp.float32),
        ],
        in_specs=[smem] * 6 + [vmem] * 2,
        out_specs=[anywhere, vmem],
        scratch_shapes=[
            pltpu.VMEM((ROWS, YCAP, BS, BS), jnp.bfloat16),
            pltpu.VMEM((2, BS, BS), jnp.float32),
            pltpu.SMEM((17,), jnp.int32),
            pltpu.SMEM((YCAP + 1,), jnp.int32),
            pltpu.SMEM((YCAP + 1, 40), jnp.int32),
            pltpu.SMEM((YCAP + 1, 40), jnp.int32),
            pltpu.SMEM((YCAP + 1,), jnp.int32),
            dma((ROWS,)),
        ],
        compiler_params=pltpu.CompilerParams(vmem_limit_bytes=16 << 20),
    )(where, smeta, pmeta, y_cols, y_count, branch_flag,
      strip.reshape(8 * OWN, BS, BS), panel.reshape(17 * OWN, BS, BS))
    total = lax.psum(part[0, 0], ALL)
    return out, total.reshape((1,))


def solution(mesh):
    finer = Mesh(mesh.devices.reshape(4, 4, 4, 2), ALL)
    placed = (
        P(LINE, ("x", "core"), None, None),
        P(LINE, ("x", "core")),
        P(LINE, ("x", "core")),
        P(LINE, ("x", "core")),
        P(LINE, ("x", "core")),
        P(LINE),
    )
    return jax.shard_map(
        on_device,
        mesh=finer,
        in_specs=placed,
        out_specs=(P(LINE, ("x", "core"), None, None), P()),
        check_vma=False,
    )
```

```python
import jax
import jax.numpy as jnp
from jax import lax
from jax.experimental import pallas as pl
from jax.experimental.pallas import tpu as pltpu
from jax.sharding import Mesh
from jax.sharding import PartitionSpec as P

BS = 128
ROWS = 8
CAP = 2
YCAP = 12
OWN = ROWS * CAP
LINE = ("z", "y")
ALL = ("z", "y", "x", "core")
MESH_ID = pl.DeviceIdType.MESH
ZERO = 256


def gather_kernel(x_ref, m_ref, strip, panel, smeta, pmeta, trace, s_idx, p_idx, acc, mine, plane_tr, line_tr,
                  psend, precv, xsend, xrecv, csend, crecv, lsem, asend, arecv, bsend, brecv):
    place = {a: lax.axis_index(a) for a in ("z", "y", "x")}
    after = {a: lax.rem(v + 1, 4) for a, v in place.items()}
    before = {a: lax.rem(v + 3, 4) for a, v in place.items()}
    across = {a: lax.rem(v + 2, 4) for a, v in place.items()}
    core = lax.axis_index("core")
    z, y, x = place["z"], place["y"], place["x"]
    here, line = z * 4 + y, x * 2 + core

    barrier = pltpu.get_barrier_semaphore()
    peers = [{a: to[a]} for a in ("z", "y", "x") for to in (after, before)] + [{"core": 1 - core}]
    for peer in peers:
        pl.semaphore_signal(barrier, inc=1, device_id=peer, device_id_type=MESH_ID)

    local = [
        pltpu.make_async_copy(x_ref, panel.at[here], lsem.at[0]),
        pltpu.make_async_copy(x_ref, strip.at[line], lsem.at[1]),
        pltpu.make_async_copy(m_ref, pmeta.at[here], lsem.at[2]),
        pltpu.make_async_copy(m_ref, smeta.at[line], lsem.at[3]),
    ]
    for c in local:
        c.start()
    panel[16, 0] = jnp.zeros((BS, BS), jnp.bfloat16)
    acc[...] = jnp.zeros_like(acc)
    pl.semaphore_wait(barrier, len(peers))

    sends = []

    def copy(src, dst, ss, rs, peer):
        return pltpu.make_async_remote_copy(
            src_ref=src, dst_ref=dst, send_sem=ss, recv_sem=rs, device_id=peer, device_id_type=MESH_ID
        )

    def start(*args):
        c = copy(*args)
        c.start()
        sends.append(c)

    class Ring:
        def __init__(self, axis, at, ssem, rsem, j, via=(0, 1), src=None):
            self.axis, self.at, self.ssem, self.rsem, self.j, self.via = axis, at, ssem, rsem, j, via
            self.src = src or (lambda h: at(place[axis], h))

        def order(self, q):
            return sorted(range(len(self.via)), key=lambda h: self.via[h] != q)

        def own(self, qs=(0, 1)):
            for q in qs:
                to = (after, before)[q][self.axis]
                for h in self.order(q):
                    n = q * 2 + h
                    start(self.src(h), self.at(place[self.axis], h), self.ssem.at[self.j, n], self.rsem.at[self.j, n],
                          {self.axis: to})

        def arrive(self, q):
            owner, to = (before, after)[q][self.axis], (after, before)[q][self.axis]
            for h in self.order(q):
                n, piece = q * 2 + h, self.at(owner, h)
                copy(piece, piece, self.ssem.at[self.j, n], self.rsem.at[self.j, n], {self.axis: owner}).wait_recv()
                if self.via[h] == q:
                    start(piece, piece, self.ssem.at[self.j, 4 + h], self.rsem.at[self.j, 4 + h], {self.axis: to})

        def arrive_across(self):
            for h in range(len(self.via)):
                piece = self.at(across[self.axis], h)
                copy(piece, piece, self.ssem.at[self.j, 4 + h], self.rsem.at[self.j, 4 + h],
                     {self.axis: before[self.axis]}).wait_recv()

    def chunk_of(axis, d, p):
        o = lax.rem((y if axis == "z" else z) + d, 4)
        return p * 4 + o if axis == "z" else o * 4 + p

    def panel_ring(axis, d, lo, j, via=(0, 1)):
        src = (lambda h: x_ref.at[pl.ds(lo + 4 * h, 4)]) if d == 0 else None
        return Ring(axis, lambda p, h: panel.at[chunk_of(axis, d, p), pl.ds(lo + 4 * h, 4)], psend, precv, j, via, src)

    def pmeta_ring(axis, d, j):
        src = (lambda h: m_ref) if d == 0 else None
        return Ring(axis, lambda p, h: pmeta.at[chunk_of(axis, d, p)], psend, precv, j, (0,), src)

    az, by = panel_ring("z", 0, 0, 0), panel_ring("y", 0, 8, 1)
    ay = {d: panel_ring("y", d, 0, j, v) for d, j, v in ((0, 2, (0, 1)), (1, 3, (0, 0)), (2, 4, (0, 1)), (3, 5, (1, 1)))}
    bz = {d: panel_ring("z", d, 8, j) for d, j in ((0, 6), (1, 7), (2, 8), (3, 9))}
    mz = pmeta_ring("z", 0, 10)
    my = {d: pmeta_ring("y", d, j) for d, j in ((0, 11), (1, 12), (2, 13), (3, 14))}
    xs = Ring("x", lambda p, h: strip.at[p * 2 + core, pl.ds(8 * h, 8)], xsend, xrecv, 0, (0, 1),
              lambda h: x_ref.at[pl.ds(8 * h, 8)])
    xm = Ring("x", lambda p, h: smeta.at[p * 2 + core], xsend, xrecv, 1, (0,), lambda h: m_ref)

    def swap(what, p, j, n):
        g = p * 2 + core
        start(what.at[g], what.at[g], csend.at[n, j], crecv.at[n, j], {"core": 1 - core})

    def swapped(what, p, j, n):
        g = p * 2 + 1 - core
        copy(what.at[g], what.at[g], csend.at[n, j], crecv.at[n, j], {"core": 1 - core}).wait_recv()

    source = (x == z) & (core == y // 2)
    low = lax.rem(y, 2) * 8

    def add_chunk(dz, dy):
        both = (dz, dy) not in ((0, 0), (0, 2), (2, 0), (2, 2))
        g = lax.rem(z + dz, 4) * 4 + lax.rem(y + dy, 4)
        group, base = g // 2, lax.rem(g, 2) * 8

        @pl.when(source)
        def _():
            def step(n, c):
                lefts, rights = [], []
                for u in range(4):
                    k, w = n * 2 + u // 2, u % 2
                    i = p_idx[g, 0, k * 4 + w] - low
                    ok = (w < p_idx[g, 0, k * 4 + 2]) & (i >= 0) & (i < ROWS)
                    i = jnp.clip(i, 0, ROWS - 1)
                    stored = s_idx[group, 0, i * 4 + 2]
                    first = (s_idx[group, 0, i * 4] == base + k) & (stored > 0)
                    second = (s_idx[group, 0, i * 4 + 1] == base + k) & (stored > 1)
                    sign = 1 - 2 * lax.rem(p_idx[here, 0, i * 4 + 3], 2)
                    if both:
                        sign = sign + 1 - 2 * lax.rem(p_idx[g, 0, k * 4 + 3], 2)
                    weight = jnp.where(ok & (first | second), sign, 0).astype(jnp.float32)
                    left = strip[group, i * 2 + jnp.where(second, 1, 0)]
                    lefts.append((left.astype(jnp.float32) * weight).astype(jnp.bfloat16))
                    rights.append(panel[g, k * 2 + w])
                acc[...] += jnp.dot(jnp.concatenate(lefts, axis=1), jnp.concatenate(rights, axis=0),
                                    preferred_element_type=jnp.float32)
                return c

            lax.fori_loop(0, 4, step, 0)

    mz.own()
    my[0].own()
    xm.own()
    az.own()
    by.own()
    xs.own()
    for c in local:
        c.wait()
    swap(smeta, x, 0, 1)
    swap(strip, x, 0, 0)
    for q in (0, 1):
        mz.arrive(q)
        my[0].arrive(q)
    my[1].own()
    my[3].own()
    ay[0].own()
    bz[0].own()
    for q in (0, 1):
        xm.arrive(q)
        swap(smeta, (before, after)[q]["x"], 1 + q, 1)
    for q in (0, 1):
        az.arrive(q)
        by.arrive(q)
    ay[1].own()
    bz[1].own()
    mz.arrive_across()
    my[2].own()
    my[0].arrive_across()
    xm.arrive_across()
    swap(smeta, across["x"], 3, 1)
    for d in (1, 3):
        for q in (0, 1):
            my[d].arrive(q)
    for q in (0, 1):
        xs.arrive(q)
        swap(strip, (before, after)[q]["x"], 1 + q, 0)
    az.arrive_across()
    by.arrive_across()
    ay[2].own()
    bz[2].own()
    xs.arrive_across()
    swap(strip, across["x"], 3, 0)
    ay[3].own((1,))
    ay[1].arrive(0)
    ay[1].arrive(1)
    ay[0].arrive(0)
    ay[0].arrive(1)
    for q in (0, 1):
        bz[0].arrive(q)
    for q in (0, 1):
        bz[1].arrive(q)
    for d in (1, 3):
        my[d].arrive_across()
    for q in (0, 1):
        my[2].arrive(q)
    for p, j in ((x, 0), (before["x"], 1), (after["x"], 2), (across["x"], 3)):
        swapped(smeta, p, j, 1)
        swapped(strip, p, j, 0)
    my[2].arrive_across()
    index_copies = [pltpu.make_async_copy(pmeta, p_idx, lsem.at[4]), pltpu.make_async_copy(smeta, s_idx, lsem.at[5])]
    for c in index_copies:
        c.start()
    for c in index_copies:
        c.wait()
    add_chunk(0, 0)
    add_chunk(1, 0)
    for q in (0, 1):
        ay[2].arrive(q)
        bz[2].arrive(q)
    ay[3].own((0,))
    bz[3].own()
    add_chunk(0, 1)
    add_chunk(1, 1)
    bz[0].arrive_across()
    add_chunk(2, 0)
    ay[3].arrive(1)
    add_chunk(3, 1)
    bz[1].arrive_across()
    add_chunk(2, 1)
    ay[1].arrive_across()
    add_chunk(1, 2)
    ay[0].arrive_across()
    add_chunk(0, 2)
    bz[2].arrive_across()
    ay[2].arrive_across()
    add_chunk(2, 2)

    @pl.when(source)
    def _():
        for i in range(ROWS):
            flag = lax.rem(p_idx[here, 0, i * 4 + 3], 2)
            acc[...] += (2 * flag).astype(jnp.float32) * strip[line, i * 2].astype(jnp.float32)
        eye = lax.broadcasted_iota(jnp.int32, (BS, BS), 0) == lax.broadcasted_iota(jnp.int32, (BS, BS), 1)
        total = jnp.full((1, BS), jnp.sum(jnp.where(eye, acc[...], 0.0)))
        mine[0] = total
        plane_tr[lax.rem(y, 2)] = total

    far = [(dz, dy) for dz in range(4) for dy in range(4) if dz or dy]

    def tell_plane(n):
        dz, dy = far[n]
        return copy(mine.at[0], plane_tr.at[lax.rem(y, 2)], asend.at[n], arecv.at[lax.rem(y, 2)],
                    {"z": lax.rem(z + dz, 4), "y": lax.rem(y + dy, 4)})

    @pl.when(source)
    def _():
        for n in range(len(far)):
            tell_plane(n).start()

    bz[3].arrive(0)
    bz[3].arrive(1)
    for t in range(2):
        @pl.when(jnp.logical_not(source & (lax.rem(y, 2) == t)))
        def _():
            copy(mine.at[0], plane_tr.at[t], asend.at[0], arecv.at[t], {"core": 1 - core}).wait_recv()

    total = plane_tr[0] + plane_tr[1]
    mine[1] = total
    line_tr[line] = total
    others = [(dx, dc) for dx in range(4) for dc in range(2) if dx or dc]
    for n, (dx, dc) in enumerate(others):
        start(mine.at[1], line_tr.at[line], bsend.at[n], brecv.at[line],
              {"x": lax.rem(x + dx, 4), "core": lax.rem(core + dc, 2)})
    ay[3].arrive(0)
    ay[3].arrive_across()
    bz[3].arrive_across()
    for dx, dc in others:
        g = lax.rem(x + dx, 4) * 2 + lax.rem(core + dc, 2)
        copy(mine.at[1], line_tr.at[g], bsend.at[0], brecv.at[g], {"core": 1 - core}).wait_recv()
    result = line_tr[0]
    for g in range(1, 8):
        result = result + line_tr[g]
    trace[...] = result

    @pl.when(source)
    def _():
        for n in range(len(far)):
            tell_plane(n).wait_send()

    for c in sends:
        c.wait_send()


def product_kernel(smeta, pmeta, strip, panel, out, obuf, slot, cnt, la, lb, own, osem):
    chunk = lax.axis_index("z") * 4 + lax.axis_index("y")
    mine = lax.axis_index("x") * 2 + lax.axis_index("core")

    def row(i, carry):
        packed = pmeta[chunk, 0, i * 4 + 3]
        live_y = packed // 2
        for j in range(17):
            slot[j] = YCAP
        for t in range(YCAP):
            slot[jnp.where(t < live_y, smeta[mine, 0, 32 + i * YCAP + t], 16)] = t
        slot[16] = YCAP
        for t in range(YCAP + 1):
            cnt[t] = 0
            own[t] = ZERO
            la[t, 0] = 0
            la[t, 1] = 0
            lb[t, 0] = ZERO
            lb[t, 1] = ZERO
        for q in range(CAP):
            live = q < pmeta[chunk, 0, i * 4 + 2]
            t = slot[jnp.where(live, pmeta[chunk, 0, i * 4 + q], 16)]
            own[t] = chunk * OWN + i * CAP + q

        def pairs(g, c):
            n_live = smeta[g, 0, i * 4 + 2]
            for s in range(CAP):
                @pl.when(s < n_live)
                def _():
                    k = g * 16 + smeta[g, 0, i * 4 + s]
                    kc, kr = k // 8, k % 8
                    n_in = pmeta[kc, 0, kr * 4 + 2]
                    for w in range(CAP):
                        t = slot[jnp.where(w < n_in, pmeta[kc, 0, kr * 4 + w], 16)]
                        n = cnt[t]
                        la[t, n] = g * OWN + i * CAP + s
                        lb[t, n] = k * CAP + w
                        cnt[t] = n + 1
            return c

        lax.fori_loop(0, 8, pairs, 0)
        flip = packed % 2 == 1
        sign = jnp.where(flip, -1.0, 1.0)
        twice = jnp.where(flip, 2.0, 0.0)

        def dot2(t, n):
            a = jnp.concatenate([strip[la[t, n]], strip[la[t, n + 1]]], axis=1)
            b = jnp.concatenate([panel[lb[t, n]], panel[lb[t, n + 1]]], axis=0)
            return jnp.dot(a, b, preferred_element_type=jnp.float32)

        def finish(t, product):
            return sign * product + twice * panel[own[t]].astype(jnp.float32)

        for t in range(YCAP):
            updated = finish(t, dot2(t, 0))
            obuf[i, t] = updated.astype(jnp.bfloat16)

        def more(t, c):
            n = cnt[t]

            @pl.when(n > 2)
            def _():
                la[t, n] = 0
                lb[t, n] = ZERO
                product = lax.fori_loop(
                    1, (n + 1) // 2, lambda h, acc: acc + dot2(t, h * 2), dot2(t, 0)
                )
                updated = finish(t, product)
                obuf[i, t] = updated.astype(jnp.bfloat16)

            return c

        lax.fori_loop(0, YCAP, more, 0)
        pltpu.make_async_copy(obuf.at[i], out.at[i], osem.at[i]).start()
        return carry

    lax.fori_loop(0, ROWS, row, 0)
    for i in range(ROWS):
        pltpu.make_async_copy(obuf.at[i], out.at[i], osem.at[i]).wait()


def on_device(x_blocks, x_cols, x_count, y_cols, y_count, branch_flag):
    rows = jnp.concatenate([x_cols, x_count, 2 * y_count + branch_flag[:, None]], axis=1)
    meta = jnp.concatenate([rows.reshape(1, 4 * ROWS), y_cols.reshape(1, YCAP * ROWS)], axis=1)
    vmem, hbm, smem = (pl.BlockSpec(memory_space=m) for m in (pltpu.VMEM, pltpu.HBM, pltpu.SMEM))
    dma = pltpu.SemaphoreType.DMA
    strip, panel, smeta, pmeta, trace = pl.pallas_call(
        gather_kernel,
        out_shape=[
            pltpu.VMEM((8, OWN, BS, BS), jnp.bfloat16),
            pltpu.VMEM((17, OWN, BS, BS), jnp.bfloat16),
            pltpu.VMEM((8, 1, BS), jnp.int32),
            pltpu.VMEM((16, 1, BS), jnp.int32),
            jax.ShapeDtypeStruct((1, BS), jnp.float32),
        ],
        in_specs=[hbm, vmem],
        out_specs=[vmem] * 5,
        scratch_shapes=[
            pltpu.SMEM((8, 1, BS), jnp.int32),
            pltpu.SMEM((16, 1, BS), jnp.int32),
            pltpu.VMEM((BS, BS), jnp.float32),
            pltpu.VMEM((2, 1, BS), jnp.float32),
            pltpu.VMEM((2, 1, BS), jnp.float32),
            pltpu.VMEM((8, 1, BS), jnp.float32),
            dma((15, 6)),
            dma((15, 6)),
            dma((2, 6)),
            dma((2, 6)),
            dma((2, 4)),
            dma((2, 4)),
            dma((6,)),
            dma((15,)),
            dma((2,)),
            dma((7,)),
            dma((8,)),
        ],
        compiler_params=pltpu.CompilerParams(collective_id=0, has_side_effects=True, vmem_limit_bytes=16 << 20),
    )(x_blocks.reshape(OWN, BS, BS), meta)
    out = pl.pallas_call(
        product_kernel,
        out_shape=jax.ShapeDtypeStruct((ROWS, YCAP, BS, BS), jnp.bfloat16),
        in_specs=[smem] * 2 + [vmem] * 2,
        out_specs=hbm,
        scratch_shapes=[
            pltpu.VMEM((ROWS, YCAP, BS, BS), jnp.bfloat16),
            pltpu.SMEM((17,), jnp.int32),
            pltpu.SMEM((YCAP + 1,), jnp.int32),
            pltpu.SMEM((YCAP + 1, 40), jnp.int32),
            pltpu.SMEM((YCAP + 1, 40), jnp.int32),
            pltpu.SMEM((YCAP + 1,), jnp.int32),
            dma((ROWS,)),
        ],
        compiler_params=pltpu.CompilerParams(vmem_limit_bytes=16 << 20),
    )(smeta, pmeta, strip.reshape(8 * OWN, BS, BS), panel.reshape(17 * OWN, BS, BS))
    return out, trace[0, :1]


def solution(mesh):
    finer = Mesh(mesh.devices.reshape(4, 4, 4, 2), ALL)
    placed = (
        P(LINE, ("x", "core"), None, None),
        P(LINE, ("x", "core")),
        P(LINE, ("x", "core")),
        P(LINE, ("x", "core")),
        P(LINE, ("x", "core")),
        P(LINE),
    )
    return jax.shard_map(
        on_device,
        mesh=finer,
        in_specs=placed,
        out_specs=(P(LINE, ("x", "core"), None, None), P()),
        check_vma=False,
    )
```

```python
import jax
import jax.numpy as jnp
from jax import lax
from jax.experimental import pallas as pl
from jax.experimental.pallas import tpu as pltpu
from jax.sharding import Mesh
from jax.sharding import PartitionSpec as P

BS = 128
ROWS = 8
CAP = 2
YCAP = 12
OWN = ROWS * CAP
LINE = ("z", "y")
ALL = ("z", "y", "x", "core")
MESH_ID = pl.DeviceIdType.MESH
ZERO = 256
NONE = ZERO * 128 * 32 + 16


def gather_kernel(x_ref, m_ref, y_ref, strip, panel, trace, table, entries, smeta, pmeta, y_mem, s_idx, p_idx, e_idx, acc, mine, plane_tr, line_tr,
                  psend, precv, xsend, xrecv, csend, crecv, lsem, asend, arecv, bsend, brecv):
    place = {a: lax.axis_index(a) for a in ("z", "y", "x")}
    after = {a: lax.rem(v + 1, 4) for a, v in place.items()}
    before = {a: lax.rem(v + 3, 4) for a, v in place.items()}
    across = {a: lax.rem(v + 2, 4) for a, v in place.items()}
    core = lax.axis_index("core")
    z, y, x = place["z"], place["y"], place["x"]
    here, line = z * 4 + y, x * 2 + core

    barrier = pltpu.get_barrier_semaphore()
    peers = [{a: to[a]} for a in ("z", "y", "x") for to in (after, before)] + [{"core": 1 - core}]
    for peer in peers:
        pl.semaphore_signal(barrier, inc=1, device_id=peer, device_id_type=MESH_ID)

    local = [
        pltpu.make_async_copy(x_ref, panel.at[here], lsem.at[0]),
        pltpu.make_async_copy(x_ref, strip.at[line], lsem.at[1]),
        pltpu.make_async_copy(m_ref, pmeta.at[here], lsem.at[2]),
        pltpu.make_async_copy(m_ref, smeta.at[line], lsem.at[3]),
        pltpu.make_async_copy(y_ref, y_mem, lsem.at[7]),
    ]
    for c in local:
        c.start()
    panel[16, 0] = jnp.zeros((BS, BS), jnp.bfloat16)
    acc[...] = jnp.zeros_like(acc)
    pl.semaphore_wait(barrier, len(peers))

    sends = []

    def copy(src, dst, ss, rs, peer):
        return pltpu.make_async_remote_copy(
            src_ref=src, dst_ref=dst, send_sem=ss, recv_sem=rs, device_id=peer, device_id_type=MESH_ID
        )

    def start(*args):
        c = copy(*args)
        c.start()
        sends.append(c)

    class Ring:
        def __init__(self, axis, at, ssem, rsem, j, via=(0, 1), src=None):
            self.axis, self.at, self.ssem, self.rsem, self.j, self.via = axis, at, ssem, rsem, j, via
            self.src = src or (lambda h: at(place[axis], h))

        def order(self, q):
            return sorted(range(len(self.via)), key=lambda h: self.via[h] != q)

        def own(self, qs=(0, 1), part=slice(None)):
            for q in qs:
                to = (after, before)[q][self.axis]
                for h in self.order(q)[part]:
                    n = q * 2 + h
                    start(self.src(h), self.at(place[self.axis], h), self.ssem.at[self.j, n], self.rsem.at[self.j, n],
                          {self.axis: to})

        def arrive(self, q, part=slice(None)):
            owner, to = (before, after)[q][self.axis], (after, before)[q][self.axis]
            for h in self.order(q)[part]:
                n, piece = q * 2 + h, self.at(owner, h)
                copy(piece, piece, self.ssem.at[self.j, n], self.rsem.at[self.j, n], {self.axis: owner}).wait_recv()
                if self.via[h] == q:
                    start(piece, piece, self.ssem.at[self.j, 4 + h], self.rsem.at[self.j, 4 + h], {self.axis: to})

        def arrive_across(self):
            for h in range(len(self.via)):
                piece = self.at(across[self.axis], h)
                copy(piece, piece, self.ssem.at[self.j, 4 + h], self.rsem.at[self.j, 4 + h],
                     {self.axis: before[self.axis]}).wait_recv()

    def chunk_of(axis, d, p):
        o = lax.rem((y if axis == "z" else z) + d, 4)
        return p * 4 + o if axis == "z" else o * 4 + p

    def panel_ring(axis, d, lo, j, via=(0, 1)):
        src = (lambda h: x_ref.at[pl.ds(lo + 4 * h, 4)]) if d == 0 else None
        return Ring(axis, lambda p, h: panel.at[chunk_of(axis, d, p), pl.ds(lo + 4 * h, 4)], psend, precv, j, via, src)

    def pmeta_ring(axis, d, j):
        src = (lambda h: m_ref) if d == 0 else None
        return Ring(axis, lambda p, h: pmeta.at[chunk_of(axis, d, p)], psend, precv, j, (0,), src)

    az, by = panel_ring("z", 0, 0, 0), panel_ring("y", 0, 8, 1)
    ay = {d: panel_ring("y", d, 0, j, v) for d, j, v in ((0, 2, (0, 1)), (1, 3, (0, 0)), (2, 4, (0, 1)), (3, 5, (1, 1)))}
    bz = {d: panel_ring("z", d, 8, j) for d, j in ((0, 6), (1, 7), (2, 8), (3, 9))}
    mz = pmeta_ring("z", 0, 10)
    my = {d: pmeta_ring("y", d, j) for d, j in ((0, 11), (1, 12), (2, 13), (3, 14))}
    xs = Ring("x", lambda p, h: strip.at[p * 2 + core, pl.ds(8 * h, 8)], xsend, xrecv, 0, (0, 1),
              lambda h: x_ref.at[pl.ds(8 * h, 8)])
    xm = Ring("x", lambda p, h: smeta.at[p * 2 + core], xsend, xrecv, 1, (0,), lambda h: m_ref)

    def swap(what, p, j, n):
        g = p * 2 + core
        start(what.at[g], what.at[g], csend.at[n, j], crecv.at[n, j], {"core": 1 - core})

    def swapped(what, p, j, n):
        g = p * 2 + 1 - core
        copy(what.at[g], what.at[g], csend.at[n, j], crecv.at[n, j], {"core": 1 - core}).wait_recv()

    source = (x == z) & (core == y // 2)
    low = lax.rem(y, 2) * 8

    def add_chunk(dz, dy):
        both = (dz, dy) not in ((0, 0), (0, 2), (2, 0), (2, 2))
        g = lax.rem(z + dz, 4) * 4 + lax.rem(y + dy, 4)
        group, base = g // 2, lax.rem(g, 2) * 8

        @pl.when(source)
        def _():
            def step(n, c):
                lefts, rights = [], []
                for u in range(4):
                    k, w = n * 2 + u // 2, u % 2
                    i = p_idx[g, w, k] - low
                    ok = (w < p_idx[g, 2, k]) & (i >= 0) & (i < ROWS)
                    i = jnp.clip(i, 0, ROWS - 1)
                    stored = s_idx[group, 2, i]
                    first = (s_idx[group, 0, i] == base + k) & (stored > 0)
                    second = (s_idx[group, 1, i] == base + k) & (stored > 1)
                    sign = 1 - 2 * p_idx[here, 4, i]
                    if both:
                        sign = sign + 1 - 2 * p_idx[g, 4, k]
                    weight = jnp.where(ok & (first | second), sign, 0).astype(jnp.float32)
                    left = strip[group, i * 2 + jnp.where(second, 1, 0)]
                    lefts.append((left.astype(jnp.float32) * weight).astype(jnp.bfloat16))
                    rights.append(panel[g, k * 2 + w])
                acc[...] += jnp.dot(jnp.concatenate(lefts, axis=1), jnp.concatenate(rights, axis=0),
                                    preferred_element_type=jnp.float32)
                return c

            lax.fori_loop(0, 4, step, 0)

    def list_pairs():
        def row(i, c):
            for g in range(8):
                stored = s_idx[g, 2, i]
                for u in range(CAP):
                    k = s_idx[g, u, i]
                    chunk, r = 2 * g + k // 8, k % 8
                    inner = jnp.where(u < stored, p_idx[chunk, 2, r], 0)
                    for w in range(CAP):
                        col = jnp.where(w < inner, p_idx[chunk, w, r], 16)
                        place_b = (16 * g + k) * CAP + w
                        e_idx[i, (g * CAP + u) * CAP + w] = (place_b * 128 + g * OWN + i * CAP + u) * 32 + col
            return c

        lax.fori_loop(0, ROWS, row, 0)
        c = pltpu.make_async_copy(e_idx, entries, lsem.at[6])
        c.start()
        c.wait()

    def list_slots():
        lane = lax.broadcasted_iota(jnp.int32, (ROWS, BS), 1)
        sub = lax.broadcasted_iota(jnp.int32, (ROWS, BS), 0)
        entry = entries[...]
        col = jnp.where(lane < 32, entry % 32, 16)
        tab = jnp.zeros((ROWS, BS), jnp.int32)
        most = jnp.zeros((ROWS, 1), jnp.int32)
        by_row = [
            jnp.sum(jnp.where(lane == sub, jnp.broadcast_to(m_ref[f : f + 1, :], (ROWS, BS)), 0), axis=1, keepdims=True)
            for f in range(5)
        ]
        live = by_row[3]
        for t in range(YCAP):
            want = jnp.where(t < live, y_mem[:, t : t + 1], 17)
            hit = (col == want).astype(jnp.int32)
            upto = hit
            for shift in (1, 2, 4, 8, 16):
                upto = upto + jnp.where(lane >= shift, pltpu.roll(upto, shift, 1), 0)
            count = jnp.sum(hit, axis=1, keepdims=True)
            most = jnp.maximum(most, count)
            own = jnp.full((ROWS, 1), ZERO, jnp.int32)
            for u in range(CAP):
                mine_u = (by_row[u] == want) & (u < by_row[2])
                own = jnp.where(mine_u, here * OWN + sub[:, :1] * CAP + u, own)
            values = []
            for n in range(2):
                found = jnp.sum(jnp.where((hit == 1) & (upto == n + 1), entry, 0), axis=1, keepdims=True)
                values.append(jnp.where(count > n, found, NONE))
            for f, v in enumerate((*values, count, own)):
                tab = jnp.where(lane == t * 4 + f, v, tab)
        tab = jnp.where(lane == 48, by_row[4], tab)
        table[...] = jnp.where(lane == 49, most, tab)

    one, two = slice(0, 1), slice(1, 2)
    mz.own()
    my[0].own()
    xm.own()
    az.own(part=one)
    by.own(part=one)
    xs.own(part=one)
    for c in local:
        c.wait()
    swap(smeta, x, 0, 1)
    for q in (0, 1):
        mz.arrive(q)
    my[1].own()
    my[3].own()
    for q in (0, 1):
        my[0].arrive(q)
        xm.arrive(q)
    az.own(part=two)
    by.own(part=two)
    xs.own(part=two)
    for q in (0, 1):
        swap(smeta, (before, after)[q]["x"], 1 + q, 1)
    swap(strip, x, 0, 0)
    for part in (one, two):
        ay[0].own(part=part)
        bz[0].own(part=part)
        if part == one:
            mz.arrive_across()
            my[2].own()
            for q in (0, 1):
                az.arrive(q, one)
                by.arrive(q, one)
            for d in (1, 3):
                for q in (0, 1):
                    my[d].arrive(q)
    for q in (0, 1):
        az.arrive(q, two)
        by.arrive(q, two)
    ay[1].own()
    bz[1].own()
    my[0].arrive_across()
    for q in (0, 1):
        my[2].arrive(q)
    xm.arrive_across()
    swap(smeta, across["x"], 3, 1)
    for q in (0, 1):
        xs.arrive(q)
        swap(strip, (before, after)[q]["x"], 1 + q, 0)
    az.arrive_across()
    by.arrive_across()
    ay[2].own()
    bz[2].own()
    ay[3].own((1,))
    for d in (1, 3):
        my[d].arrive_across()
    xs.arrive_across()
    swap(strip, across["x"], 3, 0)
    for q in (0, 1):
        bz[0].arrive(q)
    ay[1].arrive(0)
    ay[1].arrive(1)
    ay[0].arrive(0)
    ay[0].arrive(1)
    for q in (0, 1):
        bz[1].arrive(q)
    my[2].arrive_across()
    for p, j in ((x, 0), (before["x"], 1), (after["x"], 2), (across["x"], 3)):
        swapped(smeta, p, j, 1)
        swapped(strip, p, j, 0)
    index_copies = [pltpu.make_async_copy(pmeta, p_idx, lsem.at[4]), pltpu.make_async_copy(smeta, s_idx, lsem.at[5])]
    for c in index_copies:
        c.start()
    for c in index_copies:
        c.wait()
    list_pairs()
    add_chunk(0, 0)
    add_chunk(1, 0)
    for q in (0, 1):
        ay[2].arrive(q)
        bz[2].arrive(q)
    ay[3].own((0,))
    bz[3].own()
    list_slots()
    add_chunk(0, 1)
    add_chunk(1, 1)
    bz[0].arrive_across()
    add_chunk(2, 0)
    ay[3].arrive(1)
    add_chunk(3, 1)
    bz[1].arrive_across()
    add_chunk(2, 1)
    ay[1].arrive_across()
    add_chunk(1, 2)
    ay[0].arrive_across()
    add_chunk(0, 2)
    bz[2].arrive_across()
    ay[2].arrive_across()
    add_chunk(2, 2)

    @pl.when(source)
    def _():
        for i in range(ROWS):
            flag = p_idx[here, 4, i]
            acc[...] += (2 * flag).astype(jnp.float32) * strip[line, i * 2].astype(jnp.float32)
        eye = lax.broadcasted_iota(jnp.int32, (BS, BS), 0) == lax.broadcasted_iota(jnp.int32, (BS, BS), 1)
        total = jnp.full((1, BS), jnp.sum(jnp.where(eye, acc[...], 0.0)))
        mine[0] = total
        plane_tr[lax.rem(y, 2)] = total

    far = [(dz, dy) for dz in range(4) for dy in range(4) if dz or dy]

    def tell_plane(n):
        dz, dy = far[n]
        return copy(mine.at[0], plane_tr.at[lax.rem(y, 2)], asend.at[n], arecv.at[lax.rem(y, 2)],
                    {"z": lax.rem(z + dz, 4), "y": lax.rem(y + dy, 4)})

    @pl.when(source)
    def _():
        for n in range(len(far)):
            tell_plane(n).start()

    for part in (one, two):
        for q in (0, 1):
            bz[3].arrive(q, part)
    for t in range(2):
        @pl.when(jnp.logical_not(source & (lax.rem(y, 2) == t)))
        def _():
            copy(mine.at[0], plane_tr.at[t], asend.at[0], arecv.at[t], {"core": 1 - core}).wait_recv()

    total = plane_tr[0] + plane_tr[1]
    mine[1] = total
    line_tr[line] = total
    others = [(dx, dc) for dx in range(4) for dc in range(2) if dx or dc]
    for n, (dx, dc) in enumerate(others):
        start(mine.at[1], line_tr.at[line], bsend.at[n], brecv.at[line],
              {"x": lax.rem(x + dx, 4), "core": lax.rem(core + dc, 2)})
    ay[3].arrive(0)
    ay[3].arrive_across()
    bz[3].arrive_across()
    for dx, dc in others:
        g = lax.rem(x + dx, 4) * 2 + lax.rem(core + dc, 2)
        copy(mine.at[1], line_tr.at[g], bsend.at[0], brecv.at[g], {"core": 1 - core}).wait_recv()
    result = line_tr[0]
    for g in range(1, 8):
        result = result + line_tr[g]
    trace[...] = result

    @pl.when(source)
    def _():
        for n in range(len(far)):
            tell_plane(n).wait_send()

    for c in sends:
        c.wait_send()


def product_kernel(table, entries, strip, panel, out, obuf, found, osem):
    def row(i, carry):
        flip = table[i, 48] == 1
        sign = jnp.where(flip, -1.0, 1.0)
        twice = jnp.where(flip, 2.0, 0.0)

        def dot2(c0, c1):
            a = jnp.concatenate([strip[(c0 >> 5) & 127], strip[(c1 >> 5) & 127]], axis=1)
            b = jnp.concatenate([panel[c0 >> 12], panel[c1 >> 12]], axis=0)
            return jnp.dot(a, b, preferred_element_type=jnp.float32)

        def finish(t, product):
            updated = sign * product + twice * panel[table[i, t * 4 + 3]].astype(jnp.float32)
            obuf[i, t] = updated.astype(jnp.bfloat16)

        for t in range(YCAP):
            finish(t, dot2(table[i, t * 4], table[i, t * 4 + 1]))

        @pl.when(table[i, 49] > 2)
        def _():
            def more(t, c):
                @pl.when(table[i, t * 4 + 2] > 2)
                def _():
                    col = table[i, t * 4] & 31
                    n = 0
                    for e in range(32):
                        entry = entries[i, e]
                        found[n] = entry
                        n = n + jnp.where((entry & 31) == col, 1, 0)
                    found[n] = NONE
                    finish(t, lax.fori_loop(
                        1, (n + 1) // 2, lambda h, p: p + dot2(found[2 * h], found[2 * h + 1]),
                        dot2(found[0], found[1])))

                return c

            lax.fori_loop(0, YCAP, more, 0)

        pltpu.make_async_copy(obuf.at[i], out.at[i], osem.at[i]).start()
        return carry

    lax.fori_loop(0, ROWS, row, 0)
    for i in range(ROWS):
        pltpu.make_async_copy(obuf.at[i], out.at[i], osem.at[i]).wait()


def on_device(x_blocks, x_cols, x_count, y_cols, y_count, branch_flag):
    meta = jnp.concatenate([x_cols.T, x_count.T, y_count.T, branch_flag[None, :]], axis=0)
    meta = jnp.pad(meta, ((0, 3), (0, BS - ROWS)))
    x_blocks = pltpu.with_memory_space_constraint(x_blocks.reshape(OWN, BS, BS), pltpu.HBM)
    y_cols = pltpu.with_memory_space_constraint(y_cols, pltpu.HBM)
    vmem, hbm, smem = (pl.BlockSpec(memory_space=m) for m in (pltpu.VMEM, pltpu.HBM, pltpu.SMEM))
    dma = pltpu.SemaphoreType.DMA
    strip, panel, trace, table, entries = pl.pallas_call(
        gather_kernel,
        out_shape=[
            pltpu.VMEM((8, OWN, BS, BS), jnp.bfloat16),
            pltpu.VMEM((17, OWN, BS, BS), jnp.bfloat16),
            jax.ShapeDtypeStruct((1, BS), jnp.float32),
            pltpu.VMEM((ROWS, BS), jnp.int32),
            pltpu.VMEM((ROWS, BS), jnp.int32),
        ],
        in_specs=[hbm, vmem, hbm],
        out_specs=[vmem] * 5,
        scratch_shapes=[
            pltpu.VMEM((8, ROWS, BS), jnp.int32),
            pltpu.VMEM((16, ROWS, BS), jnp.int32),
            pltpu.VMEM((ROWS, YCAP), jnp.int32),
            pltpu.SMEM((8, ROWS, BS), jnp.int32),
            pltpu.SMEM((16, ROWS, BS), jnp.int32),
            pltpu.SMEM((ROWS, BS), jnp.int32),
            pltpu.VMEM((BS, BS), jnp.float32),
            pltpu.VMEM((2, 1, BS), jnp.float32),
            pltpu.VMEM((2, 1, BS), jnp.float32),
            pltpu.VMEM((8, 1, BS), jnp.float32),
            dma((15, 6)),
            dma((15, 6)),
            dma((2, 6)),
            dma((2, 6)),
            dma((2, 4)),
            dma((2, 4)),
            dma((8,)),
            dma((15,)),
            dma((2,)),
            dma((7,)),
            dma((8,)),
        ],
        compiler_params=pltpu.CompilerParams(collective_id=0, has_side_effects=True, vmem_limit_bytes=16 << 20),
    )(x_blocks, meta, y_cols)
    out = pl.pallas_call(
        product_kernel,
        out_shape=jax.ShapeDtypeStruct((ROWS, YCAP, BS, BS), jnp.bfloat16),
        in_specs=[smem] * 2 + [vmem] * 2,
        out_specs=hbm,
        scratch_shapes=[
            pltpu.VMEM((ROWS, YCAP, BS, BS), jnp.bfloat16),
            pltpu.SMEM((40,), jnp.int32),
            dma((ROWS,)),
        ],
        compiler_params=pltpu.CompilerParams(vmem_limit_bytes=16 << 20),
    )(table, entries, strip.reshape(8 * OWN, BS, BS), panel.reshape(17 * OWN, BS, BS))
    return out, trace[0, :1]


def solution(mesh):
    finer = Mesh(mesh.devices.reshape(4, 4, 4, 2), ALL)
    placed = (
        P(LINE, ("x", "core"), None, None),
        P(LINE, ("x", "core")),
        P(LINE, ("x", "core")),
        P(LINE, ("x", "core")),
        P(LINE, ("x", "core")),
        P(LINE),
    )
    return jax.shard_map(
        on_device,
        mesh=finer,
        in_specs=placed,
        out_specs=(P(LINE, ("x", "core"), None, None), P()),
        check_vma=False,
    )
```

```python
import jax
import jax.numpy as jnp
from jax import lax
from jax.experimental import pallas as pl
from jax.experimental.pallas import tpu as pltpu
from jax.sharding import Mesh
from jax.sharding import PartitionSpec as P

BS = 128
ROWS = 8
CAP = 2
YCAP = 12
OWN = ROWS * CAP
LINE = ("z", "y")
ALL = ("z", "y", "x", "core")
MESH_ID = pl.DeviceIdType.MESH
ZERO = 256
NONE = ZERO * 128 * 32 + 16
PAIRS = 4
WIDTH = PAIRS + 2
FLAG = YCAP * WIDTH
BIG = FLAG + 1


def signs(table, i):
    flip = table[i, FLAG] == 1
    return jnp.where(flip, -1.0, 1.0), jnp.where(flip, 2.0, 0.0)


def dot_pairs(strip, panel, entries):
    a = jnp.concatenate([strip[(e >> 9) & 7, (e >> 5) & 15] for e in entries], axis=1)
    b = jnp.concatenate([panel[e >> 16, (e >> 12) & 15] for e in entries], axis=0)
    return jnp.dot(a, b, preferred_element_type=jnp.float32)


def gather_kernel(x_ref, m_ref, y_ref, strip, panel, slots, trace, table, entries, smeta, pmeta, y_mem, s_idx, p_idx, e_idx, t_idx, acc, mine, plane_tr, line_tr,
                  psend, precv, xsend, xrecv, csend, crecv, lsem, asend, arecv, bsend, brecv):
    place = {a: lax.axis_index(a) for a in ("z", "y", "x")}
    after = {a: lax.rem(v + 1, 4) for a, v in place.items()}
    before = {a: lax.rem(v + 3, 4) for a, v in place.items()}
    across = {a: lax.rem(v + 2, 4) for a, v in place.items()}
    core = lax.axis_index("core")
    z, y, x = place["z"], place["y"], place["x"]
    here, line = z * 4 + y, x * 2 + core

    barrier = pltpu.get_barrier_semaphore()
    peers = [{a: to[a]} for a in ("z", "y", "x") for to in (after, before)] + [{"core": 1 - core}]
    for peer in peers:
        pl.semaphore_signal(barrier, inc=1, device_id=peer, device_id_type=MESH_ID)

    local = [
        pltpu.make_async_copy(x_ref, panel.at[here], lsem.at[0]),
        pltpu.make_async_copy(x_ref, strip.at[line], lsem.at[1]),
        pltpu.make_async_copy(m_ref, pmeta.at[here], lsem.at[2]),
        pltpu.make_async_copy(m_ref, smeta.at[line], lsem.at[3]),
        pltpu.make_async_copy(y_ref, y_mem, lsem.at[7]),
    ]
    for c in local:
        c.start()
    panel[16, 0] = jnp.zeros((BS, BS), jnp.bfloat16)
    acc[...] = jnp.zeros_like(acc)
    pl.semaphore_wait(barrier, len(peers))

    sends = []

    def copy(src, dst, ss, rs, peer):
        return pltpu.make_async_remote_copy(
            src_ref=src, dst_ref=dst, send_sem=ss, recv_sem=rs, device_id=peer, device_id_type=MESH_ID
        )

    def start(*args):
        c = copy(*args)
        c.start()
        sends.append(c)

    class Ring:
        def __init__(self, axis, at, ssem, rsem, j, via=(0, 1), src=None):
            self.axis, self.at, self.ssem, self.rsem, self.j, self.via = axis, at, ssem, rsem, j, via
            self.src = src or (lambda h: at(place[axis], h))

        def order(self, q):
            return sorted(range(len(self.via)), key=lambda h: self.via[h] != q)

        def own(self, qs=(0, 1), part=slice(None)):
            for q in qs:
                to = (after, before)[q][self.axis]
                for h in self.order(q)[part]:
                    n = q * 2 + h
                    start(self.src(h), self.at(place[self.axis], h), self.ssem.at[self.j, n], self.rsem.at[self.j, n],
                          {self.axis: to})

        def arrive(self, q, part=slice(None), hold=()):
            owner = (before, after)[q][self.axis]
            for h in self.order(q)[part]:
                n, piece = q * 2 + h, self.at(owner, h)
                copy(piece, piece, self.ssem.at[self.j, n], self.rsem.at[self.j, n], {self.axis: owner}).wait_recv()
                if self.via[h] == q and h not in hold:
                    self.pass_on(q, h)

        def pass_on(self, q, h):
            piece = self.at((before, after)[q][self.axis], h)
            start(piece, piece, self.ssem.at[self.j, 4 + h], self.rsem.at[self.j, 4 + h],
                  {self.axis: (after, before)[q][self.axis]})

        def arrive_across(self):
            for h in range(len(self.via)):
                piece = self.at(across[self.axis], h)
                copy(piece, piece, self.ssem.at[self.j, 4 + h], self.rsem.at[self.j, 4 + h],
                     {self.axis: before[self.axis]}).wait_recv()

    def chunk_of(axis, d, p):
        o = lax.rem((y if axis == "z" else z) + d, 4)
        return p * 4 + o if axis == "z" else o * 4 + p

    def panel_ring(axis, d, lo, j, via=(0, 1)):
        src = (lambda h: x_ref.at[pl.ds(lo + 4 * h, 4)]) if d == 0 else None
        return Ring(axis, lambda p, h: panel.at[chunk_of(axis, d, p), pl.ds(lo + 4 * h, 4)], psend, precv, j, via, src)

    def pmeta_ring(axis, d, j):
        src = (lambda h: m_ref) if d == 0 else None
        return Ring(axis, lambda p, h: pmeta.at[chunk_of(axis, d, p)], psend, precv, j, (0,), src)

    az, by = panel_ring("z", 0, 0, 0), panel_ring("y", 0, 8, 1)
    ay = {d: panel_ring("y", d, 0, j, v) for d, j, v in ((0, 2, (0, 1)), (1, 3, (0, 0)), (2, 4, (0, 1)), (3, 5, (1, 1)))}
    bz = {d: panel_ring("z", d, 8, j) for d, j in ((0, 6), (1, 7), (2, 8), (3, 9))}
    mz = pmeta_ring("z", 0, 10)
    my = {d: pmeta_ring("y", d, j) for d, j in ((0, 11), (1, 12), (2, 13), (3, 14))}
    xs = Ring("x", lambda p, h: strip.at[p * 2 + core, pl.ds(8 * h, 8)], xsend, xrecv, 0, (0, 1),
              lambda h: x_ref.at[pl.ds(8 * h, 8)])
    xm = Ring("x", lambda p, h: smeta.at[p * 2 + core], xsend, xrecv, 1, (0,), lambda h: m_ref)

    def swap(what, p, j, n):
        g = p * 2 + core
        start(what.at[g], what.at[g], csend.at[n, j], crecv.at[n, j], {"core": 1 - core})

    def swapped(what, p, j, n):
        g = p * 2 + 1 - core
        copy(what.at[g], what.at[g], csend.at[n, j], crecv.at[n, j], {"core": 1 - core}).wait_recv()

    source = (x == z) & (core == y // 2)
    low = lax.rem(y, 2) * 8

    def add_chunk(dz, dy):
        both = (dz, dy) not in ((0, 0), (0, 2), (2, 0), (2, 2))
        g = lax.rem(z + dz, 4) * 4 + lax.rem(y + dy, 4)
        group, base = g // 2, lax.rem(g, 2) * 8

        @pl.when(source)
        def _():
            def step(n, c):
                lefts, rights = [], []
                for u in range(4):
                    k, w = n * 2 + u // 2, u % 2
                    i = p_idx[g, w, k] - low
                    ok = (w < p_idx[g, 2, k]) & (i >= 0) & (i < ROWS)
                    i = jnp.clip(i, 0, ROWS - 1)
                    stored = s_idx[group, 2, i]
                    first = (s_idx[group, 0, i] == base + k) & (stored > 0)
                    second = (s_idx[group, 1, i] == base + k) & (stored > 1)
                    sign = 1 - 2 * p_idx[here, 4, i]
                    if both:
                        sign = sign + 1 - 2 * p_idx[g, 4, k]
                    weight = jnp.where(ok & (first | second), sign, 0).astype(jnp.float32)
                    left = strip[group, i * 2 + jnp.where(second, 1, 0)]
                    lefts.append((left.astype(jnp.float32) * weight).astype(jnp.bfloat16))
                    rights.append(panel[g, k * 2 + w])
                acc[...] += jnp.dot(jnp.concatenate(lefts, axis=1), jnp.concatenate(rights, axis=0),
                                    preferred_element_type=jnp.float32)
                return c

            lax.fori_loop(0, 4, step, 0)

    def list_pairs():
        def row(i, c):
            for g in range(8):
                stored = s_idx[g, 2, i]
                for u in range(CAP):
                    k = s_idx[g, u, i]
                    chunk, r = 2 * g + k // 8, k % 8
                    inner = jnp.where(u < stored, p_idx[chunk, 2, r], 0)
                    for w in range(CAP):
                        col = jnp.where(w < inner, p_idx[chunk, w, r], 16)
                        place_b = (16 * g + k) * CAP + w
                        e_idx[i, (g * CAP + u) * CAP + w] = (place_b * 128 + g * OWN + i * CAP + u) * 32 + col
            return c

        lax.fori_loop(0, ROWS, row, 0)
        c = pltpu.make_async_copy(e_idx, entries, lsem.at[6])
        c.start()
        c.wait()

    def list_slots():
        lane = lax.broadcasted_iota(jnp.int32, (ROWS, BS), 1)
        sub = lax.broadcasted_iota(jnp.int32, (ROWS, BS), 0)
        entry = entries[...]
        col = jnp.where(lane < 32, entry % 32, 16)
        tab = jnp.zeros((ROWS, BS), jnp.int32)
        big = jnp.zeros((ROWS, 1), jnp.int32)
        by_row = [
            jnp.sum(jnp.where(lane == sub, jnp.broadcast_to(m_ref[f : f + 1, :], (ROWS, BS)), 0), axis=1, keepdims=True)
            for f in range(5)
        ]
        live = by_row[3]
        for t in range(YCAP):
            want = jnp.where(t < live, y_mem[:, t : t + 1], 17)
            hit = (col == want).astype(jnp.int32)
            upto = hit
            for shift in (1, 2, 4, 8, 16):
                upto = upto + jnp.where(lane >= shift, pltpu.roll(upto, shift, 1), 0)
            count = jnp.sum(hit, axis=1, keepdims=True)
            own = jnp.full((ROWS, 1), ZERO, jnp.int32)
            for u in range(CAP):
                mine_u = (by_row[u] == want) & (u < by_row[2])
                own = jnp.where(mine_u, here * OWN + sub[:, :1] * CAP + u, own)
            for n in range(PAIRS):
                found = jnp.sum(jnp.where((hit == 1) & (upto == n + 1), entry, 0), axis=1, keepdims=True)
                tab = jnp.where(lane == t * WIDTH + n, jnp.where(count > n, found, NONE), tab)
            tab = jnp.where(lane == t * WIDTH + PAIRS, count, tab)
            tab = jnp.where(lane == t * WIDTH + PAIRS + 1, own, tab)
            tab = jnp.where((lane == BIG + 1 + big) & (count > 2), t, tab)
            big = big + jnp.where(count > 2, 1, 0)
        tab = jnp.where(lane == FLAG, by_row[4], tab)
        table[...] = jnp.where(lane == BIG, big, tab)
        c = pltpu.make_async_copy(table, t_idx, lsem.at[8])
        c.start()
        c.wait()

    def multiply(first, last):
        def row(i, c):
            sign, twice = signs(t_idx, i)
            for t in range(YCAP):
                product = dot_pairs(strip, panel, [t_idx[i, t * WIDTH + n] for n in range(2)])
                own = t_idx[i, t * WIDTH + PAIRS + 1]
                updated = sign * product + twice * panel[own >> 4, own & 15].astype(jnp.float32)
                slots[i, t] = updated.astype(jnp.bfloat16)
            return c

        lax.fori_loop(first, last, row, 0)

    one, two = slice(0, 1), slice(1, 2)
    mz.own()
    my[0].own()
    xm.own()
    az.own(part=one)
    by.own(part=one)
    xs.own(part=one)
    for c in local:
        c.wait()
    swap(smeta, x, 0, 1)
    for q in (0, 1):
        mz.arrive(q)
    my[1].own()
    my[3].own()
    for q in (0, 1):
        my[0].arrive(q)
        xm.arrive(q)
    az.own(part=two)
    by.own(part=two)
    xs.own(part=two)
    for q in (0, 1):
        swap(smeta, (before, after)[q]["x"], 1 + q, 1)
    swap(strip, x, 0, 0)
    for part in (one, two):
        ay[0].own(part=part)
        bz[0].own(part=part)
        if part == one:
            mz.arrive_across()
            my[2].own()
            for q in (0, 1):
                az.arrive(q, one)
                by.arrive(q, one)
            for d in (1, 3):
                for q in (0, 1):
                    my[d].arrive(q)
    for q in (0, 1):
        az.arrive(q, two)
        by.arrive(q, two)
    ay[1].own()
    bz[1].own()
    my[0].arrive_across()
    for q in (0, 1):
        my[2].arrive(q)
    xm.arrive_across()
    swap(smeta, across["x"], 3, 1)
    for q in (0, 1):
        xs.arrive(q)
        swap(strip, (before, after)[q]["x"], 1 + q, 0)
    az.arrive_across()
    by.arrive_across()
    ay[2].own()
    bz[2].own()
    ay[3].own((1,))
    for d in (1, 3):
        my[d].arrive_across()
    xs.arrive_across()
    swap(strip, across["x"], 3, 0)
    for q in (0, 1):
        bz[0].arrive(q)
    ay[1].arrive(0)
    ay[1].arrive(1)
    ay[0].arrive(0)
    ay[0].arrive(1)
    for q in (0, 1):
        bz[1].arrive(q)
    my[2].arrive_across()
    for p, j in ((x, 0), (before["x"], 1), (after["x"], 2), (across["x"], 3)):
        swapped(smeta, p, j, 1)
        swapped(strip, p, j, 0)
    index_copies = [pltpu.make_async_copy(pmeta, p_idx, lsem.at[4]), pltpu.make_async_copy(smeta, s_idx, lsem.at[5])]
    for c in index_copies:
        c.start()
    for c in index_copies:
        c.wait()
    list_pairs()
    add_chunk(0, 0)
    add_chunk(1, 0)
    for q in (0, 1):
        ay[2].arrive(q)
        bz[2].arrive(q)
    ay[3].own((0,), one)
    bz[3].own()
    list_slots()
    add_chunk(0, 1)
    add_chunk(1, 1)
    bz[0].arrive_across()
    add_chunk(2, 0)
    ay[3].arrive(1, hold=(1,))
    add_chunk(3, 1)
    bz[1].arrive_across()
    add_chunk(2, 1)
    ay[1].arrive_across()
    add_chunk(1, 2)
    ay[0].arrive_across()
    add_chunk(0, 2)
    bz[2].arrive_across()
    ay[2].arrive_across()
    add_chunk(2, 2)

    @pl.when(source)
    def _():
        for i in range(ROWS):
            flag = p_idx[here, 4, i]
            acc[...] += (2 * flag).astype(jnp.float32) * strip[line, i * 2].astype(jnp.float32)
        eye = lax.broadcasted_iota(jnp.int32, (BS, BS), 0) == lax.broadcasted_iota(jnp.int32, (BS, BS), 1)
        total = jnp.full((1, BS), jnp.sum(jnp.where(eye, acc[...], 0.0)))
        mine[0] = total
        plane_tr[lax.rem(y, 2)] = total

    far = [(dz, dy) for dz in range(4) for dy in range(4) if dz or dy]

    def tell_plane(n):
        dz, dy = far[n]
        return copy(mine.at[0], plane_tr.at[lax.rem(y, 2)], asend.at[n], arecv.at[lax.rem(y, 2)],
                    {"z": lax.rem(z + dz, 4), "y": lax.rem(y + dy, 4)})

    @pl.when(source)
    def _():
        for n in range(len(far)):
            tell_plane(n).start()

    ay[3].own((0,), two)
    ay[3].pass_on(1, 1)

    for part in (one, two):
        for q in (0, 1):
            bz[3].arrive(q, part)
    for t in range(2):
        @pl.when(jnp.logical_not(source & (lax.rem(y, 2) == t)))
        def _():
            copy(mine.at[0], plane_tr.at[t], asend.at[0], arecv.at[t], {"core": 1 - core}).wait_recv()

    total = plane_tr[0] + plane_tr[1]
    mine[1] = total
    line_tr[line] = total
    others = [(dx, dc) for dx in range(4) for dc in range(2) if dx or dc]
    for n, (dx, dc) in enumerate(others):
        start(mine.at[1], line_tr.at[line], bsend.at[n], brecv.at[line],
              {"x": lax.rem(x + dx, 4), "core": lax.rem(core + dc, 2)})
    ay[3].arrive(0)
    ay[3].arrive_across()
    bz[3].arrive_across()
    multiply(0, ROWS)
    for dx, dc in others:
        g = lax.rem(x + dx, 4) * 2 + lax.rem(core + dc, 2)
        copy(mine.at[1], line_tr.at[g], bsend.at[0], brecv.at[g], {"core": 1 - core}).wait_recv()
    result = line_tr[0]
    for g in range(1, 8):
        result = result + line_tr[g]
    trace[...] = result

    @pl.when(source)
    def _():
        for n in range(len(far)):
            tell_plane(n).wait_send()

    for c in sends:
        c.wait_send()


def finish_kernel(table, entries, strip, panel, slots, out, redone, found, osem):
    for i in range(ROWS):
        @pl.when(table[i, BIG] == 0)
        def _():
            pltpu.make_async_copy(slots.at[i], out.at[i], osem.at[i]).start()

    def redo(i, t):
        count = table[i, t * WIDTH + PAIRS]
        sign, twice = signs(table, i)
        own = table[i, t * WIDTH + PAIRS + 1]

        def store(product):
            updated = sign * product + twice * panel[own >> 4, own & 15].astype(jnp.float32)
            redone[i, t] = updated.astype(jnp.bfloat16)

        @pl.when(count <= PAIRS)
        def _():
            store(dot_pairs(strip, panel, [table[i, t * WIDTH + n] for n in range(PAIRS)]))

        @pl.when(count > PAIRS)
        def _():
            col = table[i, t * WIDTH] & 31
            n = 0
            for e in range(32):
                entry = entries[i, e]
                found[n] = entry
                n = n + jnp.where((entry & 31) == col, 1, 0)
            found[n] = NONE
            store(lax.fori_loop(
                1, (n + 1) // 2, lambda h, p: p + dot_pairs(strip, panel, [found[2 * h], found[2 * h + 1]]),
                dot_pairs(strip, panel, [found[0], found[1]])))

    def row(i, carry):
        @pl.when(table[i, BIG] > 0)
        def _():
            def again(n, c):
                redo(i, table[i, BIG + 1 + n])
                return c

            lax.fori_loop(0, table[i, BIG], again, 0)

            def send(t, c):
                big = table[i, t * WIDTH + PAIRS] > 2

                @pl.when(big)
                def _():
                    pltpu.make_async_copy(redone.at[i, t], out.at[i, t], osem.at[i]).start()

                @pl.when(jnp.logical_not(big))
                def _():
                    pltpu.make_async_copy(slots.at[i, t], out.at[i, t], osem.at[i]).start()

                return c

            lax.fori_loop(0, YCAP, send, 0)

        return carry

    lax.fori_loop(0, ROWS, row, 0)
    for i in range(ROWS):
        pltpu.make_async_copy(slots.at[i], out.at[i], osem.at[i]).wait()


def on_device(x_blocks, x_cols, x_count, y_cols, y_count, branch_flag):
    meta = jnp.concatenate([x_cols.T, x_count.T, y_count.T, branch_flag[None, :]], axis=0)
    meta = jnp.pad(meta, ((0, 3), (0, BS - ROWS)))
    x_blocks = pltpu.with_memory_space_constraint(x_blocks.reshape(OWN, BS, BS), pltpu.HBM)
    y_cols = pltpu.with_memory_space_constraint(y_cols, pltpu.HBM)
    vmem, hbm, smem = (pl.BlockSpec(memory_space=m) for m in (pltpu.VMEM, pltpu.HBM, pltpu.SMEM))
    dma = pltpu.SemaphoreType.DMA
    strip, panel, slots, trace, table, entries = pl.pallas_call(
        gather_kernel,
        out_shape=[
            pltpu.VMEM((8, OWN, BS, BS), jnp.bfloat16),
            pltpu.VMEM((17, OWN, BS, BS), jnp.bfloat16),
            pltpu.VMEM((ROWS, YCAP, BS, BS), jnp.bfloat16),
            jax.ShapeDtypeStruct((1, BS), jnp.float32),
            pltpu.VMEM((ROWS, BS), jnp.int32),
            pltpu.VMEM((ROWS, BS), jnp.int32),
        ],
        in_specs=[hbm, vmem, hbm],
        out_specs=[vmem] * 6,
        scratch_shapes=[
            pltpu.VMEM((8, ROWS, BS), jnp.int32),
            pltpu.VMEM((16, ROWS, BS), jnp.int32),
            pltpu.VMEM((ROWS, YCAP), jnp.int32),
            pltpu.SMEM((8, ROWS, BS), jnp.int32),
            pltpu.SMEM((16, ROWS, BS), jnp.int32),
            pltpu.SMEM((ROWS, BS), jnp.int32),
            pltpu.SMEM((ROWS, BS), jnp.int32),
            pltpu.VMEM((BS, BS), jnp.float32),
            pltpu.VMEM((2, 1, BS), jnp.float32),
            pltpu.VMEM((2, 1, BS), jnp.float32),
            pltpu.VMEM((8, 1, BS), jnp.float32),
            dma((15, 6)),
            dma((15, 6)),
            dma((2, 6)),
            dma((2, 6)),
            dma((2, 4)),
            dma((2, 4)),
            dma((9,)),
            dma((15,)),
            dma((2,)),
            dma((7,)),
            dma((8,)),
        ],
        compiler_params=pltpu.CompilerParams(collective_id=0, has_side_effects=True, vmem_limit_bytes=16 << 20),
    )(x_blocks, meta, y_cols)
    out = pl.pallas_call(
        finish_kernel,
        out_shape=jax.ShapeDtypeStruct((ROWS, YCAP, BS, BS), jnp.bfloat16),
        in_specs=[smem] * 2 + [vmem] * 3,
        out_specs=hbm,
        scratch_shapes=[
            pltpu.VMEM((ROWS, YCAP, BS, BS), jnp.bfloat16),
            pltpu.SMEM((40,), jnp.int32),
            dma((ROWS,)),
        ],
        compiler_params=pltpu.CompilerParams(vmem_limit_bytes=16 << 20),
    )(table, entries, strip, panel, slots)
    return out, trace[0, :1]


def solution(mesh):
    finer = Mesh(mesh.devices.reshape(4, 4, 4, 2), ALL)
    placed = (
        P(LINE, ("x", "core"), None, None),
        P(LINE, ("x", "core")),
        P(LINE, ("x", "core")),
        P(LINE, ("x", "core")),
        P(LINE, ("x", "core")),
        P(LINE),
    )
    return jax.shard_map(
        on_device,
        mesh=finer,
        in_specs=placed,
        out_specs=(P(LINE, ("x", "core"), None, None), P()),
        check_vma=False,
    )
```

```python
import jax
import jax.numpy as jnp
from jax import lax
from jax.experimental import pallas as pl
from jax.experimental.pallas import tpu as pltpu
from jax.sharding import Mesh
from jax.sharding import PartitionSpec as P

BS = 128
ROWS = 8
CAP = 2
YCAP = 12
OWN = ROWS * CAP
LINE = ("z", "y")
ALL = ("z", "y", "x", "core")
MESH_ID = pl.DeviceIdType.MESH
ZERO = 256
NONE = ZERO * 128 * 32 + 16
PAIRS = 4
WIDTH = PAIRS + 2
FLAG = YCAP * WIDTH
BIG = FLAG + 1


def signs(table, i):
    flip = table[i, FLAG] == 1
    return jnp.where(flip, -1.0, 1.0), jnp.where(flip, 2.0, 0.0)


def dot_pairs(strip, panel, entries):
    a = jnp.concatenate([strip[(e >> 9) & 7, (e >> 5) & 15] for e in entries], axis=1)
    b = jnp.concatenate([panel[e >> 16, (e >> 12) & 15] for e in entries], axis=0)
    return jnp.dot(a, b, preferred_element_type=jnp.float32)


def gather_kernel(x_ref, *refs):
    (cols_ref, x_count_ref, y_count_ref, flag_ref, y_ref, strip, panel, slots, trace, table, entries, smeta, pmeta,
     m_ref, cols_mem, x_count_mem, y_count_mem, flag_mem, y_mem, s_idx, p_idx, e_idx, t_idx, acc, mine, plane_tr, line_tr,
     psend, precv, xsend, xrecv, csend, crecv, lsem, msem, asend, arecv, bsend, brecv) = refs
    place = {a: lax.axis_index(a) for a in ("z", "y", "x")}
    after = {a: lax.rem(v + 1, 4) for a, v in place.items()}
    before = {a: lax.rem(v + 3, 4) for a, v in place.items()}
    across = {a: lax.rem(v + 2, 4) for a, v in place.items()}
    core = lax.axis_index("core")
    z, y, x = place["z"], place["y"], place["x"]
    here, line = z * 4 + y, x * 2 + core

    barrier = pltpu.get_barrier_semaphore()
    peers = [{a: to[a]} for a in ("z", "y", "x") for to in (after, before)] + [{"core": 1 - core}]
    for peer in peers:
        pl.semaphore_signal(barrier, inc=1, device_id=peer, device_id_type=MESH_ID)

    local = [
        pltpu.make_async_copy(x_ref, panel.at[here], lsem.at[0]),
        pltpu.make_async_copy(x_ref, strip.at[line], lsem.at[1]),
        pltpu.make_async_copy(y_ref, y_mem, lsem.at[7]),
    ]
    fields = ((cols_ref, cols_mem), (x_count_ref, x_count_mem), (y_count_ref, y_count_mem), (flag_ref, flag_mem))
    small = [pltpu.make_async_copy(a, b, msem.at[n]) for n, (a, b) in enumerate(fields)]
    for c in small + local:
        c.start()
    for c in small:
        c.wait()
    for row, (_, b) in zip((0, 2, 3, 4), fields):
        for tile in (m_ref, smeta.at[line], pmeta.at[here]):
            tile[row : row + b.shape[0], :ROWS] = b[...]
    panel[16, 0] = jnp.zeros((BS, BS), jnp.bfloat16)
    acc[...] = jnp.zeros_like(acc)
    pl.semaphore_wait(barrier, len(peers))

    sends = []

    def copy(src, dst, ss, rs, peer):
        return pltpu.make_async_remote_copy(
            src_ref=src, dst_ref=dst, send_sem=ss, recv_sem=rs, device_id=peer, device_id_type=MESH_ID
        )

    def start(*args):
        c = copy(*args)
        c.start()
        sends.append(c)

    class Ring:
        def __init__(self, axis, at, ssem, rsem, j, via=(0, 1), src=None):
            self.axis, self.at, self.ssem, self.rsem, self.j, self.via = axis, at, ssem, rsem, j, via
            self.src = src or (lambda h: at(place[axis], h))

        def order(self, q):
            return sorted(range(len(self.via)), key=lambda h: self.via[h] != q)

        def own(self, qs=(0, 1), part=slice(None)):
            for q in qs:
                to = (after, before)[q][self.axis]
                for h in self.order(q)[part]:
                    n = q * 2 + h
                    start(self.src(h), self.at(place[self.axis], h), self.ssem.at[self.j, n], self.rsem.at[self.j, n],
                          {self.axis: to})

        def arrive(self, q, part=slice(None), hold=()):
            owner = (before, after)[q][self.axis]
            for h in self.order(q)[part]:
                n, piece = q * 2 + h, self.at(owner, h)
                copy(piece, piece, self.ssem.at[self.j, n], self.rsem.at[self.j, n], {self.axis: owner}).wait_recv()
                if self.via[h] == q and h not in hold:
                    self.pass_on(q, h)

        def pass_on(self, q, h):
            piece = self.at((before, after)[q][self.axis], h)
            start(piece, piece, self.ssem.at[self.j, 4 + h], self.rsem.at[self.j, 4 + h],
                  {self.axis: (after, before)[q][self.axis]})

        def arrive_across(self):
            for h in range(len(self.via)):
                piece = self.at(across[self.axis], h)
                copy(piece, piece, self.ssem.at[self.j, 4 + h], self.rsem.at[self.j, 4 + h],
                     {self.axis: before[self.axis]}).wait_recv()

    def chunk_of(axis, d, p):
        o = lax.rem((y if axis == "z" else z) + d, 4)
        return p * 4 + o if axis == "z" else o * 4 + p

    def panel_ring(axis, d, lo, j, via=(0, 1)):
        src = (lambda h: x_ref.at[pl.ds(lo + 4 * h, 4)]) if d == 0 else None
        return Ring(axis, lambda p, h: panel.at[chunk_of(axis, d, p), pl.ds(lo + 4 * h, 4)], psend, precv, j, via, src)

    def pmeta_ring(axis, d, j):
        src = (lambda h: m_ref) if d == 0 else None
        return Ring(axis, lambda p, h: pmeta.at[chunk_of(axis, d, p)], psend, precv, j, (0,), src)

    az, by = panel_ring("z", 0, 0, 0), panel_ring("y", 0, 8, 1)
    ay = {d: panel_ring("y", d, 0, j, v) for d, j, v in ((0, 2, (0, 1)), (1, 3, (0, 0)), (2, 4, (0, 1)), (3, 5, (1, 1)))}
    bz = {d: panel_ring("z", d, 8, j) for d, j in ((0, 6), (1, 7), (2, 8), (3, 9))}
    mz = pmeta_ring("z", 0, 10)
    my = {d: pmeta_ring("y", d, j) for d, j in ((0, 11), (1, 12), (2, 13), (3, 14))}
    xs = Ring("x", lambda p, h: strip.at[p * 2 + core, pl.ds(8 * h, 8)], xsend, xrecv, 0, (0, 1),
              lambda h: x_ref.at[pl.ds(8 * h, 8)])
    xm = Ring("x", lambda p, h: smeta.at[p * 2 + core], xsend, xrecv, 1, (0,), lambda h: m_ref)

    def swap(what, p, j, n):
        g = p * 2 + core
        start(what.at[g], what.at[g], csend.at[n, j], crecv.at[n, j], {"core": 1 - core})

    def swapped(what, p, j, n):
        g = p * 2 + 1 - core
        copy(what.at[g], what.at[g], csend.at[n, j], crecv.at[n, j], {"core": 1 - core}).wait_recv()

    source = (x == z) & (core == y // 2)
    low = lax.rem(y, 2) * 8

    def add_chunk(dz, dy):
        both = (dz, dy) not in ((0, 0), (0, 2), (2, 0), (2, 2))
        g = lax.rem(z + dz, 4) * 4 + lax.rem(y + dy, 4)
        group, base = g // 2, lax.rem(g, 2) * 8

        @pl.when(source)
        def _():
            def step(n, c):
                lefts, rights = [], []
                for u in range(4):
                    k, w = n * 2 + u // 2, u % 2
                    i = p_idx[g, w, k] - low
                    ok = (w < p_idx[g, 2, k]) & (i >= 0) & (i < ROWS)
                    i = jnp.clip(i, 0, ROWS - 1)
                    stored = s_idx[group, 2, i]
                    first = (s_idx[group, 0, i] == base + k) & (stored > 0)
                    second = (s_idx[group, 1, i] == base + k) & (stored > 1)
                    sign = 1 - 2 * p_idx[here, 4, i]
                    if both:
                        sign = sign + 1 - 2 * p_idx[g, 4, k]
                    weight = jnp.where(ok & (first | second), sign, 0).astype(jnp.float32)
                    left = strip[group, i * 2 + jnp.where(second, 1, 0)]
                    lefts.append((left.astype(jnp.float32) * weight).astype(jnp.bfloat16))
                    rights.append(panel[g, k * 2 + w])
                acc[...] += jnp.dot(jnp.concatenate(lefts, axis=1), jnp.concatenate(rights, axis=0),
                                    preferred_element_type=jnp.float32)
                return c

            lax.fori_loop(0, 4, step, 0)

    def list_pairs():
        def row(i, c):
            for g in range(8):
                stored = s_idx[g, 2, i]
                for u in range(CAP):
                    k = s_idx[g, u, i]
                    chunk, r = 2 * g + k // 8, k % 8
                    inner = jnp.where(u < stored, p_idx[chunk, 2, r], 0)
                    for w in range(CAP):
                        col = jnp.where(w < inner, p_idx[chunk, w, r], 16)
                        place_b = (16 * g + k) * CAP + w
                        e_idx[i, (g * CAP + u) * CAP + w] = (place_b * 128 + g * OWN + i * CAP + u) * 32 + col
            return c

        lax.fori_loop(0, ROWS, row, 0)
        c = pltpu.make_async_copy(e_idx, entries, lsem.at[6])
        c.start()
        c.wait()

    def list_slots():
        lane = lax.broadcasted_iota(jnp.int32, (ROWS, BS), 1)
        sub = lax.broadcasted_iota(jnp.int32, (ROWS, BS), 0)
        entry = entries[...]
        col = jnp.where(lane < 32, entry % 32, 16)
        tab = jnp.zeros((ROWS, BS), jnp.int32)
        big = jnp.zeros((ROWS, 1), jnp.int32)
        by_row = [
            jnp.sum(jnp.where(lane == sub, jnp.broadcast_to(m_ref[f : f + 1, :], (ROWS, BS)), 0), axis=1, keepdims=True)
            for f in range(5)
        ]
        live = by_row[3]
        for t in range(YCAP):
            want = jnp.where(t < live, y_mem[:, t : t + 1], 17)
            hit = (col == want).astype(jnp.int32)
            upto = hit
            for shift in (1, 2, 4, 8, 16):
                upto = upto + jnp.where(lane >= shift, pltpu.roll(upto, shift, 1), 0)
            count = jnp.sum(hit, axis=1, keepdims=True)
            own = jnp.full((ROWS, 1), ZERO, jnp.int32)
            for u in range(CAP):
                mine_u = (by_row[u] == want) & (u < by_row[2])
                own = jnp.where(mine_u, here * OWN + sub[:, :1] * CAP + u, own)
            for n in range(PAIRS):
                found = jnp.sum(jnp.where((hit == 1) & (upto == n + 1), entry, 0), axis=1, keepdims=True)
                tab = jnp.where(lane == t * WIDTH + n, jnp.where(count > n, found, NONE), tab)
            tab = jnp.where(lane == t * WIDTH + PAIRS, count, tab)
            tab = jnp.where(lane == t * WIDTH + PAIRS + 1, own, tab)
            tab = jnp.where((lane == BIG + 1 + big) & (count > 2), t, tab)
            big = big + jnp.where(count > 2, 1, 0)
        tab = jnp.where(lane == FLAG, by_row[4], tab)
        table[...] = jnp.where(lane == BIG, big, tab)
        c = pltpu.make_async_copy(table, t_idx, lsem.at[8])
        c.start()
        c.wait()

    def multiply(first, last):
        def row(i, c):
            sign, twice = signs(t_idx, i)
            for t in range(YCAP):
                product = dot_pairs(strip, panel, [t_idx[i, t * WIDTH + n] for n in range(2)])
                own = t_idx[i, t * WIDTH + PAIRS + 1]
                updated = sign * product + twice * panel[own >> 4, own & 15].astype(jnp.float32)
                slots[i, t] = updated.astype(jnp.bfloat16)
            return c

        lax.fori_loop(first, last, row, 0)

    one, two = slice(0, 1), slice(1, 2)
    mz.own()
    my[0].own()
    xm.own()
    az.own(part=one)
    by.own(part=one)
    xs.own(part=one)
    for c in local:
        c.wait()
    swap(smeta, x, 0, 1)
    for q in (0, 1):
        mz.arrive(q)
    my[1].own()
    my[3].own()
    for q in (0, 1):
        my[0].arrive(q)
        xm.arrive(q)
    az.own(part=two)
    by.own(part=two)
    xs.own(part=two)
    for q in (0, 1):
        swap(smeta, (before, after)[q]["x"], 1 + q, 1)
    swap(strip, x, 0, 0)
    for part in (one, two):
        ay[0].own(part=part)
        bz[0].own(part=part)
        if part == one:
            mz.arrive_across()
            my[2].own()
            for q in (0, 1):
                az.arrive(q, one)
                by.arrive(q, one)
            for d in (1, 3):
                for q in (0, 1):
                    my[d].arrive(q)
    for q in (0, 1):
        az.arrive(q, two)
        by.arrive(q, two)
    ay[1].own()
    bz[1].own()
    my[0].arrive_across()
    for q in (0, 1):
        my[2].arrive(q)
    xm.arrive_across()
    swap(smeta, across["x"], 3, 1)
    for q in (0, 1):
        xs.arrive(q)
        swap(strip, (before, after)[q]["x"], 1 + q, 0)
    az.arrive_across()
    by.arrive_across()
    ay[2].own()
    bz[2].own()
    ay[3].own((1,))
    for d in (1, 3):
        my[d].arrive_across()
    xs.arrive_across()
    swap(strip, across["x"], 3, 0)
    for q in (0, 1):
        bz[0].arrive(q)
    ay[1].arrive(0)
    ay[1].arrive(1)
    ay[0].arrive(0)
    ay[0].arrive(1)
    for q in (0, 1):
        bz[1].arrive(q)
    my[2].arrive_across()
    for p, j in ((x, 0), (before["x"], 1), (after["x"], 2), (across["x"], 3)):
        swapped(smeta, p, j, 1)
        swapped(strip, p, j, 0)
    index_copies = [pltpu.make_async_copy(pmeta, p_idx, lsem.at[4]), pltpu.make_async_copy(smeta, s_idx, lsem.at[5])]
    for c in index_copies:
        c.start()
    for c in index_copies:
        c.wait()
    list_pairs()

    @pl.when(source)
    def _():
        for i in range(ROWS):
            flag = p_idx[here, 4, i]
            acc[...] += (2 * flag).astype(jnp.float32) * strip[line, i * 2].astype(jnp.float32)

    add_chunk(0, 0)
    add_chunk(1, 0)
    for q in (0, 1):
        ay[2].arrive(q)
        bz[2].arrive(q)
    ay[3].own((0,), one)
    bz[3].own()
    list_slots()
    add_chunk(0, 1)
    add_chunk(1, 1)
    bz[0].arrive_across()
    add_chunk(2, 0)
    ay[3].arrive(1, hold=(1,))
    add_chunk(3, 1)
    bz[1].arrive_across()
    add_chunk(2, 1)
    ay[1].arrive_across()
    add_chunk(1, 2)
    ay[0].arrive_across()
    add_chunk(0, 2)
    bz[2].arrive_across()
    ay[2].arrive_across()
    add_chunk(2, 2)

    @pl.when(source)
    def _():
        eye = lax.broadcasted_iota(jnp.int32, (BS, BS), 0) == lax.broadcasted_iota(jnp.int32, (BS, BS), 1)
        total = jnp.full((1, BS), jnp.sum(jnp.where(eye, acc[...], 0.0)))
        mine[0] = total
        plane_tr[lax.rem(y, 2)] = total

    far = [(dz, dy) for dz in (2, 1, 3, 0) for dy in (2, 1, 3, 0) if dz or dy]

    def tell_plane(n):
        dz, dy = far[n]
        return copy(mine.at[0], plane_tr.at[lax.rem(y, 2)], asend.at[n], arecv.at[lax.rem(y, 2)],
                    {"z": lax.rem(z + dz, 4), "y": lax.rem(y + dy, 4)})

    @pl.when(source)
    def _():
        for n in range(len(far)):
            tell_plane(n).start()

    ay[3].own((0,), two)
    ay[3].pass_on(1, 1)

    for part in (one, two):
        for q in (0, 1):
            bz[3].arrive(q, part)
    for t in range(2):
        @pl.when(jnp.logical_not(source & (lax.rem(y, 2) == t)))
        def _():
            copy(mine.at[0], plane_tr.at[t], asend.at[0], arecv.at[t], {"core": 1 - core}).wait_recv()

    total = plane_tr[0] + plane_tr[1]
    mine[1] = total
    line_tr[line] = total
    others = [(dx, dc) for dx in (2, 1, 3, 0) for dc in (1, 0) if dx or dc]
    for n, (dx, dc) in enumerate(others):
        start(mine.at[1], line_tr.at[line], bsend.at[n], brecv.at[line],
              {"x": lax.rem(x + dx, 4), "core": lax.rem(core + dc, 2)})
    ay[3].arrive(0)
    ay[3].arrive_across()
    bz[3].arrive_across()
    multiply(0, ROWS)
    for dx, dc in others:
        g = lax.rem(x + dx, 4) * 2 + lax.rem(core + dc, 2)
        copy(mine.at[1], line_tr.at[g], bsend.at[0], brecv.at[g], {"core": 1 - core}).wait_recv()
    result = line_tr[0]
    for g in range(1, 8):
        result = result + line_tr[g]
    trace[...] = result

    @pl.when(source)
    def _():
        for n in range(len(far)):
            tell_plane(n).wait_send()

    for c in sends:
        c.wait_send()


def finish_kernel(table, entries, strip, panel, slots, out, redone, found, osem):
    for i in range(ROWS):
        @pl.when(table[i, BIG] == 0)
        def _():
            pltpu.make_async_copy(slots.at[i], out.at[i], osem.at[i]).start()

    def redo(i, t):
        count = table[i, t * WIDTH + PAIRS]
        sign, twice = signs(table, i)
        own = table[i, t * WIDTH + PAIRS + 1]

        def store(product):
            updated = sign * product + twice * panel[own >> 4, own & 15].astype(jnp.float32)
            redone[i, t] = updated.astype(jnp.bfloat16)

        @pl.when(count <= PAIRS)
        def _():
            store(dot_pairs(strip, panel, [table[i, t * WIDTH + n] for n in range(PAIRS)]))

        @pl.when(count > PAIRS)
        def _():
            col = table[i, t * WIDTH] & 31
            n = 0
            for e in range(32):
                entry = entries[i, e]
                found[n] = entry
                n = n + jnp.where((entry & 31) == col, 1, 0)
            found[n] = NONE
            store(lax.fori_loop(
                1, (n + 1) // 2, lambda h, p: p + dot_pairs(strip, panel, [found[2 * h], found[2 * h + 1]]),
                dot_pairs(strip, panel, [found[0], found[1]])))

    def row(i, carry):
        @pl.when(table[i, BIG] > 0)
        def _():
            def again(n, c):
                redo(i, table[i, BIG + 1 + n])
                return c

            lax.fori_loop(0, table[i, BIG], again, 0)

            def send(t, c):
                big = table[i, t * WIDTH + PAIRS] > 2

                @pl.when(big)
                def _():
                    pltpu.make_async_copy(redone.at[i, t], out.at[i, t], osem.at[i]).start()

                @pl.when(jnp.logical_not(big))
                def _():
                    pltpu.make_async_copy(slots.at[i, t], out.at[i, t], osem.at[i]).start()

                return c

            lax.fori_loop(0, YCAP, send, 0)

        return carry

    lax.fori_loop(0, ROWS, row, 0)
    for i in range(ROWS):
        pltpu.make_async_copy(slots.at[i], out.at[i], osem.at[i]).wait()


def on_device(x_blocks, x_cols, x_count, y_cols, y_count, branch_flag):
    x_blocks = pltpu.with_memory_space_constraint(x_blocks.reshape(OWN, BS, BS), pltpu.HBM)
    indices = [
        pltpu.with_memory_space_constraint(a, pltpu.HBM)
        for a in (x_cols.T, x_count.T, y_count.T, branch_flag[None, :], y_cols)
    ]
    vmem, hbm, smem = (pl.BlockSpec(memory_space=m) for m in (pltpu.VMEM, pltpu.HBM, pltpu.SMEM))
    dma = pltpu.SemaphoreType.DMA
    strip, panel, slots, trace, table, entries = pl.pallas_call(
        gather_kernel,
        out_shape=[
            pltpu.VMEM((8, OWN, BS, BS), jnp.bfloat16),
            pltpu.VMEM((17, OWN, BS, BS), jnp.bfloat16),
            pltpu.VMEM((ROWS, YCAP, BS, BS), jnp.bfloat16),
            jax.ShapeDtypeStruct((1, BS), jnp.float32),
            pltpu.VMEM((ROWS, BS), jnp.int32),
            pltpu.VMEM((ROWS, BS), jnp.int32),
        ],
        in_specs=[hbm] * 6,
        out_specs=[vmem] * 6,
        scratch_shapes=[
            pltpu.VMEM((8, ROWS, BS), jnp.int32),
            pltpu.VMEM((16, ROWS, BS), jnp.int32),
            pltpu.VMEM((ROWS, BS), jnp.int32),
            pltpu.VMEM((CAP, ROWS), jnp.int32),
            pltpu.VMEM((1, ROWS), jnp.int32),
            pltpu.VMEM((1, ROWS), jnp.int32),
            pltpu.VMEM((1, ROWS), jnp.int32),
            pltpu.VMEM((ROWS, YCAP), jnp.int32),
            pltpu.SMEM((8, ROWS, BS), jnp.int32),
            pltpu.SMEM((16, ROWS, BS), jnp.int32),
            pltpu.SMEM((ROWS, BS), jnp.int32),
            pltpu.SMEM((ROWS, BS), jnp.int32),
            pltpu.VMEM((BS, BS), jnp.float32),
            pltpu.VMEM((2, 1, BS), jnp.float32),
            pltpu.VMEM((2, 1, BS), jnp.float32),
            pltpu.VMEM((8, 1, BS), jnp.float32),
            dma((15, 6)),
            dma((15, 6)),
            dma((2, 6)),
            dma((2, 6)),
            dma((2, 4)),
            dma((2, 4)),
            dma((9,)),
            dma((4,)),
            dma((15,)),
            dma((2,)),
            dma((7,)),
            dma((8,)),
        ],
        compiler_params=pltpu.CompilerParams(collective_id=0, has_side_effects=True, vmem_limit_bytes=16 << 20),
    )(x_blocks, *indices)
    out = pl.pallas_call(
        finish_kernel,
        out_shape=jax.ShapeDtypeStruct((ROWS, YCAP, BS, BS), jnp.bfloat16),
        in_specs=[smem] * 2 + [vmem] * 3,
        out_specs=hbm,
        scratch_shapes=[
            pltpu.VMEM((ROWS, YCAP, BS, BS), jnp.bfloat16),
            pltpu.SMEM((40,), jnp.int32),
            dma((ROWS,)),
        ],
        compiler_params=pltpu.CompilerParams(vmem_limit_bytes=16 << 20),
    )(table, entries, strip, panel, slots)
    return out, trace[0, :1]


def solution(mesh):
    finer = Mesh(mesh.devices.reshape(4, 4, 4, 2), ALL)
    placed = (
        P(LINE, ("x", "core"), None, None),
        P(LINE, ("x", "core")),
        P(LINE, ("x", "core")),
        P(LINE, ("x", "core")),
        P(LINE, ("x", "core")),
        P(LINE),
    )
    return jax.shard_map(
        on_device,
        mesh=finer,
        in_specs=placed,
        out_specs=(P(LINE, ("x", "core"), None, None), P()),
        check_vma=False,
    )
```

```python
import jax
import jax.numpy as jnp
from jax import lax
from jax.experimental import pallas as pl
from jax.experimental.pallas import tpu as pltpu
from jax.sharding import Mesh
from jax.sharding import PartitionSpec as P

BS = 128
ROWS = 8
CAP = 2
YCAP = 12
OWN = ROWS * CAP
LINE = ("z", "y")
ALL = ("z", "y", "x", "core")
MESH_ID = pl.DeviceIdType.MESH
ZERO = 256
NONE = ZERO * 128 * 32 + 16
PAIRS = 4
WIDTH = PAIRS + 2
FLAG = YCAP * WIDTH
BIG = FLAG + 1


def signs(table, i):
    flip = table[i, FLAG] == 1
    return jnp.where(flip, -1.0, 1.0), jnp.where(flip, 2.0, 0.0)


def dot_pairs(strip, panel, entries):
    a = jnp.concatenate([strip[(e >> 9) & 7, (e >> 5) & 15] for e in entries], axis=1)
    b = jnp.concatenate([panel[e >> 16, (e >> 12) & 15] for e in entries], axis=0)
    return jnp.dot(a, b, preferred_element_type=jnp.float32)


def gather_kernel(x_ref, *refs):
    (cols_ref, x_count_ref, y_count_ref, flag_ref, y_ref, strip, panel, slots, trace, table, entries, smeta, pmeta,
     m_ref, cols_mem, x_count_mem, y_count_mem, flag_mem, y_mem, s_idx, p_idx, e_idx, t_idx, acc, mine, plane_tr, line_tr,
     psend, precv, xsend, xrecv, csend, crecv, lsem, msem, asend, arecv, bsend, brecv) = refs
    place = {a: lax.axis_index(a) for a in ("z", "y", "x")}
    after = {a: lax.rem(v + 1, 4) for a, v in place.items()}
    before = {a: lax.rem(v + 3, 4) for a, v in place.items()}
    across = {a: lax.rem(v + 2, 4) for a, v in place.items()}
    core = lax.axis_index("core")
    z, y, x = place["z"], place["y"], place["x"]
    here, line = z * 4 + y, x * 2 + core

    barrier = pltpu.get_barrier_semaphore()
    peers = [{a: to[a]} for a in ("z", "y", "x") for to in (after, before)] + [{"core": 1 - core}]
    for peer in peers:
        pl.semaphore_signal(barrier, inc=1, device_id=peer, device_id_type=MESH_ID)

    local = [
        pltpu.make_async_copy(x_ref, panel.at[here], lsem.at[0]),
        pltpu.make_async_copy(x_ref, strip.at[line], lsem.at[1]),
        pltpu.make_async_copy(y_ref, y_mem, lsem.at[7]),
    ]
    fields = ((cols_ref, cols_mem), (x_count_ref, x_count_mem), (y_count_ref, y_count_mem), (flag_ref, flag_mem))
    small = [pltpu.make_async_copy(a, b, msem.at[n]) for n, (a, b) in enumerate(fields)]
    for c in small + local:
        c.start()
    for c in small:
        c.wait()
    for row, (_, b) in zip((0, 2, 3, 4), fields):
        for tile in (m_ref, smeta.at[line], pmeta.at[here]):
            tile[row : row + b.shape[0], :ROWS] = b[...]
    panel[16, 0] = jnp.zeros((BS, BS), jnp.bfloat16)
    acc[...] = jnp.zeros_like(acc)
    pl.semaphore_wait(barrier, len(peers))

    sends = []

    def copy(src, dst, ss, rs, peer):
        return pltpu.make_async_remote_copy(
            src_ref=src, dst_ref=dst, send_sem=ss, recv_sem=rs, device_id=peer, device_id_type=MESH_ID
        )

    def start(*args):
        c = copy(*args)
        c.start()
        sends.append(c)

    class Ring:
        def __init__(self, axis, at, ssem, rsem, j, via=(0, 1), src=None):
            self.axis, self.at, self.ssem, self.rsem, self.j, self.via = axis, at, ssem, rsem, j, via
            self.src = src or (lambda h: at(place[axis], h))

        def order(self, q):
            return sorted(range(len(self.via)), key=lambda h: self.via[h] != q)

        def own(self, qs=(0, 1), part=slice(None)):
            for q in qs:
                to = (after, before)[q][self.axis]
                for h in self.order(q)[part]:
                    n = q * 2 + h
                    start(self.src(h), self.at(place[self.axis], h), self.ssem.at[self.j, n], self.rsem.at[self.j, n],
                          {self.axis: to})

        def arrive(self, q, part=slice(None), hold=()):
            owner = (before, after)[q][self.axis]
            for h in self.order(q)[part]:
                n, piece = q * 2 + h, self.at(owner, h)
                copy(piece, piece, self.ssem.at[self.j, n], self.rsem.at[self.j, n], {self.axis: owner}).wait_recv()
                if self.via[h] == q and h not in hold:
                    self.pass_on(q, h)

        def pass_on(self, q, h):
            piece = self.at((before, after)[q][self.axis], h)
            start(piece, piece, self.ssem.at[self.j, 4 + h], self.rsem.at[self.j, 4 + h],
                  {self.axis: (after, before)[q][self.axis]})

        def arrive_across(self):
            for h in range(len(self.via)):
                piece = self.at(across[self.axis], h)
                copy(piece, piece, self.ssem.at[self.j, 4 + h], self.rsem.at[self.j, 4 + h],
                     {self.axis: before[self.axis]}).wait_recv()

    def chunk_of(axis, d, p):
        o = lax.rem((y if axis == "z" else z) + d, 4)
        return p * 4 + o if axis == "z" else o * 4 + p

    def panel_ring(axis, d, lo, j, via=(0, 1)):
        src = (lambda h: x_ref.at[pl.ds(lo + 4 * h, 4)]) if d == 0 else None
        return Ring(axis, lambda p, h: panel.at[chunk_of(axis, d, p), pl.ds(lo + 4 * h, 4)], psend, precv, j, via, src)

    def pmeta_ring(axis, d, j):
        src = (lambda h: m_ref) if d == 0 else None
        return Ring(axis, lambda p, h: pmeta.at[chunk_of(axis, d, p)], psend, precv, j, (0,), src)

    az, by = panel_ring("z", 0, 0, 0), panel_ring("y", 0, 8, 1)
    ay = {d: panel_ring("y", d, 0, j, v) for d, j, v in ((0, 2, (0, 1)), (1, 3, (0, 0)), (2, 4, (0, 1)), (3, 5, (1, 1)))}
    bz = {d: panel_ring("z", d, 8, j) for d, j in ((0, 6), (1, 7), (2, 8), (3, 9))}
    mz = pmeta_ring("z", 0, 10)
    my = {d: pmeta_ring("y", d, j) for d, j in ((0, 11), (1, 12), (2, 13), (3, 14))}
    xs = Ring("x", lambda p, h: strip.at[p * 2 + core, pl.ds(8 * h, 8)], xsend, xrecv, 0, (0, 1),
              lambda h: x_ref.at[pl.ds(8 * h, 8)])
    xm = Ring("x", lambda p, h: smeta.at[p * 2 + core], xsend, xrecv, 1, (0,), lambda h: m_ref)

    def swap(what, p, j, n):
        g = p * 2 + core
        start(what.at[g], what.at[g], csend.at[n, j], crecv.at[n, j], {"core": 1 - core})

    def swapped(what, p, j, n):
        g = p * 2 + 1 - core
        copy(what.at[g], what.at[g], csend.at[n, j], crecv.at[n, j], {"core": 1 - core}).wait_recv()

    source = (x == z) & (core == y // 2)
    low = lax.rem(y, 2) * 8

    def add_chunk(dz, dy):
        both = (dz, dy) not in ((0, 0), (0, 2), (2, 0), (2, 2))
        g = lax.rem(z + dz, 4) * 4 + lax.rem(y + dy, 4)
        group, base = g // 2, lax.rem(g, 2) * 8

        @pl.when(source)
        def _():
            def step(n, c):
                lefts, rights = [], []
                for u in range(4):
                    k, w = n * 2 + u // 2, u % 2
                    i = p_idx[g, w, k] - low
                    ok = (w < p_idx[g, 2, k]) & (i >= 0) & (i < ROWS)
                    i = jnp.clip(i, 0, ROWS - 1)
                    stored = s_idx[group, 2, i]
                    first = (s_idx[group, 0, i] == base + k) & (stored > 0)
                    second = (s_idx[group, 1, i] == base + k) & (stored > 1)
                    sign = 1 - 2 * p_idx[here, 4, i]
                    if both:
                        sign = jnp.where(p_idx[g, 4, k] == p_idx[here, 4, i], sign, 0)
                    weight = jnp.where(ok & (first | second), sign, 0).astype(jnp.float32)
                    left = strip[group, i * 2 + jnp.where(second, 1, 0)]
                    lefts.append((left.astype(jnp.float32) * weight).astype(jnp.bfloat16))
                    rights.append(panel[g, k * 2 + w])
                product = jnp.dot(jnp.concatenate(lefts, axis=1), jnp.concatenate(rights, axis=0),
                                  preferred_element_type=jnp.float32)
                acc[...] += 2.0 * product if both else product
                return c

            lax.fori_loop(0, 4, step, 0)

    def list_pairs():
        def row(i, c):
            for g in range(8):
                stored = s_idx[g, 2, i]
                for u in range(CAP):
                    k = s_idx[g, u, i]
                    chunk, r = 2 * g + k // 8, k % 8
                    inner = jnp.where(u < stored, p_idx[chunk, 2, r], 0)
                    for w in range(CAP):
                        col = jnp.where(w < inner, p_idx[chunk, w, r], 16)
                        place_b = (16 * g + k) * CAP + w
                        e_idx[i, (g * CAP + u) * CAP + w] = (place_b * 128 + g * OWN + i * CAP + u) * 32 + col
            return c

        lax.fori_loop(0, ROWS, row, 0)
        c = pltpu.make_async_copy(e_idx, entries, lsem.at[6])
        c.start()
        c.wait()

    def list_slots():
        lane = lax.broadcasted_iota(jnp.int32, (ROWS, BS), 1)
        sub = lax.broadcasted_iota(jnp.int32, (ROWS, BS), 0)
        entry = entries[...]
        col = jnp.where(lane < 32, entry % 32, 16)
        tab = jnp.zeros((ROWS, BS), jnp.int32)
        big = jnp.zeros((ROWS, 1), jnp.int32)
        by_row = [
            jnp.sum(jnp.where(lane == sub, jnp.broadcast_to(m_ref[f : f + 1, :], (ROWS, BS)), 0), axis=1, keepdims=True)
            for f in range(5)
        ]
        live = by_row[3]
        for t in range(YCAP):
            want = jnp.where(t < live, y_mem[:, t : t + 1], 17)
            hit = (col == want).astype(jnp.int32)
            upto = hit
            for shift in (1, 2, 4, 8, 16):
                upto = upto + jnp.where(lane >= shift, pltpu.roll(upto, shift, 1), 0)
            count = jnp.sum(hit, axis=1, keepdims=True)
            own = jnp.full((ROWS, 1), ZERO, jnp.int32)
            for u in range(CAP):
                mine_u = (by_row[u] == want) & (u < by_row[2])
                own = jnp.where(mine_u, here * OWN + sub[:, :1] * CAP + u, own)
            for n in range(PAIRS):
                found = jnp.sum(jnp.where((hit == 1) & (upto == n + 1), entry, 0), axis=1, keepdims=True)
                tab = jnp.where(lane == t * WIDTH + n, jnp.where(count > n, found, NONE), tab)
            tab = jnp.where(lane == t * WIDTH + PAIRS, count, tab)
            tab = jnp.where(lane == t * WIDTH + PAIRS + 1, own, tab)
            tab = jnp.where((lane == BIG + 1 + big) & (count > 2), t, tab)
            big = big + jnp.where(count > 2, 1, 0)
        tab = jnp.where(lane == FLAG, by_row[4], tab)
        table[...] = jnp.where(lane == BIG, big, tab)
        c = pltpu.make_async_copy(table, t_idx, lsem.at[8])
        c.start()
        c.wait()

    def multiply(first, last):
        def row(i, c):
            sign, twice = signs(t_idx, i)
            for t in range(YCAP):
                product = dot_pairs(strip, panel, [t_idx[i, t * WIDTH + n] for n in range(2)])
                own = t_idx[i, t * WIDTH + PAIRS + 1]
                updated = sign * product + twice * panel[own >> 4, own & 15].astype(jnp.float32)
                slots[i, t] = updated.astype(jnp.bfloat16)
            return c

        lax.fori_loop(first, last, row, 0)

    one, two = slice(0, 1), slice(1, 2)
    mz.own()
    my[0].own()
    xm.own()
    az.own(part=one)
    by.own(part=one)
    xs.own(part=one)
    for c in local:
        c.wait()
    swap(smeta, x, 0, 1)
    for q in (0, 1):
        mz.arrive(q)
    my[1].own()
    my[3].own()
    for q in (0, 1):
        my[0].arrive(q)
        xm.arrive(q)
    az.own(part=two)
    by.own(part=two)
    xs.own(part=two)
    for q in (0, 1):
        swap(smeta, (before, after)[q]["x"], 1 + q, 1)
    swap(strip, x, 0, 0)
    for part in (one, two):
        ay[0].own(part=part)
        bz[0].own(part=part)
        if part == one:
            mz.arrive_across()
            my[2].own()
            for q in (0, 1):
                az.arrive(q, one)
                by.arrive(q, one)
            for d in (1, 3):
                for q in (0, 1):
                    my[d].arrive(q)
    for q in (0, 1):
        az.arrive(q, two)
        by.arrive(q, two)
    ay[1].own()
    bz[1].own()
    my[0].arrive_across()
    for q in (0, 1):
        my[2].arrive(q)
    xm.arrive_across()
    swap(smeta, across["x"], 3, 1)
    for q in (0, 1):
        xs.arrive(q)
        swap(strip, (before, after)[q]["x"], 1 + q, 0)
    az.arrive_across()
    by.arrive_across()
    ay[2].own()
    bz[2].own()
    ay[3].own((1,))
    for d in (1, 3):
        my[d].arrive_across()
    xs.arrive_across()
    swap(strip, across["x"], 3, 0)
    for q in (0, 1):
        bz[0].arrive(q)
    ay[1].arrive(0)
    ay[1].arrive(1)
    ay[0].arrive(0)
    ay[0].arrive(1)
    for q in (0, 1):
        bz[1].arrive(q)
    my[2].arrive_across()
    for p, j in ((x, 0), (before["x"], 1), (after["x"], 2), (across["x"], 3)):
        swapped(smeta, p, j, 1)
        swapped(strip, p, j, 0)
    index_copies = [pltpu.make_async_copy(pmeta, p_idx, lsem.at[4]), pltpu.make_async_copy(smeta, s_idx, lsem.at[5])]
    for c in index_copies:
        c.start()
    for c in index_copies:
        c.wait()
    list_pairs()

    @pl.when(source)
    def _():
        for i in range(ROWS):
            flag = p_idx[here, 4, i]
            acc[...] += (2 * flag).astype(jnp.float32) * strip[line, i * 2].astype(jnp.float32)

    add_chunk(0, 0)
    add_chunk(1, 0)
    for q in (0, 1):
        ay[2].arrive(q)
        bz[2].arrive(q)
    ay[3].own((0,), one)
    bz[3].own()
    list_slots()
    add_chunk(0, 1)
    add_chunk(1, 1)
    bz[0].arrive_across()
    add_chunk(2, 0)
    ay[3].arrive(1, hold=(1,))
    add_chunk(3, 1)
    bz[1].arrive_across()
    add_chunk(2, 1)
    ay[1].arrive_across()
    add_chunk(1, 2)
    ay[0].arrive_across()
    add_chunk(0, 2)
    bz[2].arrive_across()
    ay[2].arrive_across()
    add_chunk(2, 2)

    @pl.when(source)
    def _():
        eye = lax.broadcasted_iota(jnp.int32, (BS, BS), 0) == lax.broadcasted_iota(jnp.int32, (BS, BS), 1)
        total = jnp.full((1, BS), jnp.sum(jnp.where(eye, acc[...], 0.0)))
        mine[0] = total
        plane_tr[lax.rem(y, 2)] = total

    far = [(dz, dy) for dz in (2, 1, 3, 0) for dy in (2, 1, 3, 0) if dz or dy]

    def tell_plane(n):
        dz, dy = far[n]
        return copy(mine.at[0], plane_tr.at[lax.rem(y, 2)], asend.at[n], arecv.at[lax.rem(y, 2)],
                    {"z": lax.rem(z + dz, 4), "y": lax.rem(y + dy, 4)})

    @pl.when(source)
    def _():
        for n in range(len(far)):
            tell_plane(n).start()

    ay[3].own((0,), two)
    ay[3].pass_on(1, 1)

    for part in (one, two):
        for q in (0, 1):
            bz[3].arrive(q, part)
    for t in range(2):
        @pl.when(jnp.logical_not(source & (lax.rem(y, 2) == t)))
        def _():
            copy(mine.at[0], plane_tr.at[t], asend.at[0], arecv.at[t], {"core": 1 - core}).wait_recv()

    total = plane_tr[0] + plane_tr[1]
    mine[1] = total
    line_tr[line] = total
    others = [(dx, dc) for dx in (2, 1, 3, 0) for dc in (1, 0) if dx or dc]
    for n, (dx, dc) in enumerate(others):
        start(mine.at[1], line_tr.at[line], bsend.at[n], brecv.at[line],
              {"x": lax.rem(x + dx, 4), "core": lax.rem(core + dc, 2)})
    ay[3].arrive(0)
    ay[3].arrive_across()
    bz[3].arrive_across()
    multiply(0, ROWS)
    @pl.when(source)
    def _():
        for n in range(len(far)):
            tell_plane(n).wait_send()

    for c in sends:
        c.wait_send()

    for dx, dc in others:
        g = lax.rem(x + dx, 4) * 2 + lax.rem(core + dc, 2)
        copy(mine.at[1], line_tr.at[g], bsend.at[0], brecv.at[g], {"core": 1 - core}).wait_recv()
    result = line_tr[0]
    for g in range(1, 8):
        result = result + line_tr[g]
    trace[...] = result


def finish_kernel(table, entries, strip, panel, slots, out, redone, found, osem):
    for i in range(ROWS):
        @pl.when(table[i, BIG] == 0)
        def _():
            pltpu.make_async_copy(slots.at[i], out.at[i], osem.at[i]).start()

    def redo(i, t):
        count = table[i, t * WIDTH + PAIRS]
        sign, twice = signs(table, i)
        own = table[i, t * WIDTH + PAIRS + 1]

        def store(product):
            updated = sign * product + twice * panel[own >> 4, own & 15].astype(jnp.float32)
            redone[i, t] = updated.astype(jnp.bfloat16)

        @pl.when(count <= PAIRS)
        def _():
            store(dot_pairs(strip, panel, [table[i, t * WIDTH + n] for n in range(PAIRS)]))

        @pl.when(count > PAIRS)
        def _():
            col = table[i, t * WIDTH] & 31
            n = 0
            for e in range(32):
                entry = entries[i, e]
                found[n] = entry
                n = n + jnp.where((entry & 31) == col, 1, 0)
            found[n] = NONE
            store(lax.fori_loop(
                1, (n + 1) // 2, lambda h, p: p + dot_pairs(strip, panel, [found[2 * h], found[2 * h + 1]]),
                dot_pairs(strip, panel, [found[0], found[1]])))

    def row(i, carry):
        @pl.when(table[i, BIG] > 0)
        def _():
            def again(n, c):
                redo(i, table[i, BIG + 1 + n])
                return c

            lax.fori_loop(0, table[i, BIG], again, 0)

            def send(t, c):
                big = table[i, t * WIDTH + PAIRS] > 2

                @pl.when(big)
                def _():
                    pltpu.make_async_copy(redone.at[i, t], out.at[i, t], osem.at[i]).start()

                @pl.when(jnp.logical_not(big))
                def _():
                    pltpu.make_async_copy(slots.at[i, t], out.at[i, t], osem.at[i]).start()

                return c

            lax.fori_loop(0, YCAP, send, 0)

        return carry

    lax.fori_loop(0, ROWS, row, 0)
    for i in range(ROWS):
        pltpu.make_async_copy(slots.at[i], out.at[i], osem.at[i]).wait()


def on_device(x_blocks, x_cols, x_count, y_cols, y_count, branch_flag):
    x_blocks = pltpu.with_memory_space_constraint(x_blocks.reshape(OWN, BS, BS), pltpu.HBM)
    indices = [
        pltpu.with_memory_space_constraint(a, pltpu.HBM)
        for a in (x_cols.T, x_count.T, y_count.T, branch_flag[None, :], y_cols)
    ]
    vmem, hbm, smem = (pl.BlockSpec(memory_space=m) for m in (pltpu.VMEM, pltpu.HBM, pltpu.SMEM))
    dma = pltpu.SemaphoreType.DMA
    strip, panel, slots, trace, table, entries = pl.pallas_call(
        gather_kernel,
        out_shape=[
            pltpu.VMEM((8, OWN, BS, BS), jnp.bfloat16),
            pltpu.VMEM((17, OWN, BS, BS), jnp.bfloat16),
            pltpu.VMEM((ROWS, YCAP, BS, BS), jnp.bfloat16),
            jax.ShapeDtypeStruct((1, BS), jnp.float32),
            pltpu.VMEM((ROWS, BS), jnp.int32),
            pltpu.VMEM((ROWS, BS), jnp.int32),
        ],
        in_specs=[hbm] * 6,
        out_specs=[vmem] * 6,
        scratch_shapes=[
            pltpu.VMEM((8, ROWS, BS), jnp.int32),
            pltpu.VMEM((16, ROWS, BS), jnp.int32),
            pltpu.VMEM((ROWS, BS), jnp.int32),
            pltpu.VMEM((CAP, ROWS), jnp.int32),
            pltpu.VMEM((1, ROWS), jnp.int32),
            pltpu.VMEM((1, ROWS), jnp.int32),
            pltpu.VMEM((1, ROWS), jnp.int32),
            pltpu.VMEM((ROWS, YCAP), jnp.int32),
            pltpu.SMEM((8, ROWS, BS), jnp.int32),
            pltpu.SMEM((16, ROWS, BS), jnp.int32),
            pltpu.SMEM((ROWS, BS), jnp.int32),
            pltpu.SMEM((ROWS, BS), jnp.int32),
            pltpu.VMEM((BS, BS), jnp.float32),
            pltpu.VMEM((2, 1, BS), jnp.float32),
            pltpu.VMEM((2, 1, BS), jnp.float32),
            pltpu.VMEM((8, 1, BS), jnp.float32),
            dma((15, 6)),
            dma((15, 6)),
            dma((2, 6)),
            dma((2, 6)),
            dma((2, 4)),
            dma((2, 4)),
            dma((9,)),
            dma((4,)),
            dma((15,)),
            dma((2,)),
            dma((7,)),
            dma((8,)),
        ],
        compiler_params=pltpu.CompilerParams(collective_id=0, has_side_effects=True, vmem_limit_bytes=16 << 20),
    )(x_blocks, *indices)
    out = pl.pallas_call(
        finish_kernel,
        out_shape=jax.ShapeDtypeStruct((ROWS, YCAP, BS, BS), jnp.bfloat16),
        in_specs=[smem] * 2 + [vmem] * 3,
        out_specs=hbm,
        scratch_shapes=[
            pltpu.VMEM((ROWS, YCAP, BS, BS), jnp.bfloat16),
            pltpu.SMEM((40,), jnp.int32),
            dma((ROWS,)),
        ],
        compiler_params=pltpu.CompilerParams(vmem_limit_bytes=16 << 20),
    )(table, entries, strip, panel, slots)
    return out, trace[0, :1]


def solution(mesh):
    finer = Mesh(mesh.devices.reshape(4, 4, 4, 2), ALL)
    placed = (
        P(LINE, ("x", "core"), None, None),
        P(LINE, ("x", "core")),
        P(LINE, ("x", "core")),
        P(LINE, ("x", "core")),
        P(LINE, ("x", "core")),
        P(LINE),
    )
    return jax.shard_map(
        on_device,
        mesh=finer,
        in_specs=placed,
        out_specs=(P(LINE, ("x", "core"), None, None), P()),
        check_vma=False,
    )
```

```python
import jax
import jax.numpy as jnp
from jax import lax
from jax.experimental import pallas as pl
from jax.experimental.pallas import tpu as pltpu
from jax.sharding import Mesh
from jax.sharding import PartitionSpec as P

BS = 128
ROWS = 8
CAP = 2
YCAP = 12
OWN = ROWS * CAP
LINE = ("z", "y")
ALL = ("z", "y", "x", "core")
MESH_ID = pl.DeviceIdType.MESH
ZERO = 256
NONE = ZERO * 128 * 32 + 16
DIRECT = 3
PAIRS = 4
WIDTH = PAIRS + 2
FLAG = YCAP * WIDTH
BIG = FLAG + 1


def signs(table, i):
    flip = table[i, FLAG] == 1
    return jnp.where(flip, -1.0, 1.0), jnp.where(flip, 2.0, 0.0)


def dot_pairs(strip, panel, entries):
    a = jnp.concatenate([strip[(e >> 9) & 7, (e >> 5) & 15] for e in entries], axis=1)
    b = jnp.concatenate([panel[e >> 16, (e >> 12) & 15] for e in entries], axis=0)
    return jnp.dot(a, b, preferred_element_type=jnp.float32)


def gather_kernel(x_ref, *refs):
    (cols_ref, x_count_ref, y_count_ref, flag_ref, y_ref, strip, panel, slots, trace, table, entries, smeta, pmeta,
     m_ref, cols_mem, x_count_mem, y_count_mem, flag_mem, y_mem, s_idx, p_idx, e_idx, t_idx, acc, mine, plane_tr, line_tr,
     psend, precv, xsend, xrecv, csend, crecv, lsem, msem, asend, arecv, bsend, brecv) = refs
    place = {a: lax.axis_index(a) for a in ("z", "y", "x")}
    after = {a: lax.rem(v + 1, 4) for a, v in place.items()}
    before = {a: lax.rem(v + 3, 4) for a, v in place.items()}
    across = {a: lax.rem(v + 2, 4) for a, v in place.items()}
    core = lax.axis_index("core")
    z, y, x = place["z"], place["y"], place["x"]
    here, line = z * 4 + y, x * 2 + core

    barrier = pltpu.get_barrier_semaphore()
    peers = [{a: to[a]} for a in ("z", "y", "x") for to in (after, before)] + [{"core": 1 - core}]
    for peer in peers:
        pl.semaphore_signal(barrier, inc=1, device_id=peer, device_id_type=MESH_ID)

    local = [
        pltpu.make_async_copy(x_ref, panel.at[here], lsem.at[0]),
        pltpu.make_async_copy(x_ref, strip.at[line], lsem.at[1]),
        pltpu.make_async_copy(y_ref, y_mem, lsem.at[7]),
    ]
    fields = ((cols_ref, cols_mem), (x_count_ref, x_count_mem), (y_count_ref, y_count_mem), (flag_ref, flag_mem))
    small = [pltpu.make_async_copy(a, b, msem.at[n]) for n, (a, b) in enumerate(fields)]
    for c in small + local:
        c.start()
    for c in small:
        c.wait()
    for row, (_, b) in zip((0, 2, 3, 4), fields):
        for tile in (m_ref, smeta.at[line], pmeta.at[here]):
            tile[row : row + b.shape[0], :ROWS] = b[...]
    panel[16, 0] = jnp.zeros((BS, BS), jnp.bfloat16)
    acc[...] = jnp.zeros_like(acc)
    pl.semaphore_wait(barrier, len(peers))

    sends = []

    def copy(src, dst, ss, rs, peer):
        return pltpu.make_async_remote_copy(
            src_ref=src, dst_ref=dst, send_sem=ss, recv_sem=rs, device_id=peer, device_id_type=MESH_ID
        )

    def start(*args):
        c = copy(*args)
        c.start()
        sends.append(c)

    class Ring:
        def __init__(self, axis, at, ssem, rsem, j, via=(0, 1), src=None):
            self.axis, self.at, self.ssem, self.rsem, self.j, self.via = axis, at, ssem, rsem, j, via
            self.src = src or (lambda h: at(place[axis], h))

        def order(self, q):
            return sorted(range(len(self.via)), key=lambda h: self.via[h] != q)

        def own(self, qs=(0, 1), part=slice(None)):
            for q in qs:
                to = (after, before)[q][self.axis]
                for h in self.order(q)[part]:
                    n = q * 2 + h
                    start(self.src(h), self.at(place[self.axis], h), self.ssem.at[self.j, n], self.rsem.at[self.j, n],
                          {self.axis: to})

        def arrive(self, q, part=slice(None), hold=()):
            owner = (before, after)[q][self.axis]
            for h in self.order(q)[part]:
                n, piece = q * 2 + h, self.at(owner, h)
                copy(piece, piece, self.ssem.at[self.j, n], self.rsem.at[self.j, n], {self.axis: owner}).wait_recv()
                if self.via[h] == q and h not in hold:
                    self.pass_on(q, h)

        def pass_on(self, q, h):
            piece = self.at((before, after)[q][self.axis], h)
            start(piece, piece, self.ssem.at[self.j, 4 + h], self.rsem.at[self.j, 4 + h],
                  {self.axis: (after, before)[q][self.axis]})

        def arrive_across(self):
            for h in range(len(self.via)):
                piece = self.at(across[self.axis], h)
                copy(piece, piece, self.ssem.at[self.j, 4 + h], self.rsem.at[self.j, 4 + h],
                     {self.axis: before[self.axis]}).wait_recv()

    def chunk_of(axis, d, p):
        o = lax.rem((y if axis == "z" else z) + d, 4)
        return p * 4 + o if axis == "z" else o * 4 + p

    def panel_ring(axis, d, lo, j, via=(0, 1)):
        src = (lambda h: x_ref.at[pl.ds(lo + 4 * h, 4)]) if d == 0 else None
        return Ring(axis, lambda p, h: panel.at[chunk_of(axis, d, p), pl.ds(lo + 4 * h, 4)], psend, precv, j, via, src)

    def pmeta_ring(axis, d, j):
        src = (lambda h: m_ref) if d == 0 else None
        return Ring(axis, lambda p, h: pmeta.at[chunk_of(axis, d, p)], psend, precv, j, (0,), src)

    az, by = panel_ring("z", 0, 0, 0), panel_ring("y", 0, 8, 1)
    ay = {d: panel_ring("y", d, 0, j, v) for d, j, v in ((0, 2, (0, 1)), (1, 3, (0, 0)), (2, 4, (0, 1)), (3, 5, (1, 1)))}
    bz = {d: panel_ring("z", d, 8, j) for d, j in ((0, 6), (1, 7), (2, 8), (3, 9))}
    mz = pmeta_ring("z", 0, 10)
    my = {d: pmeta_ring("y", d, j) for d, j in ((0, 11), (1, 12), (2, 13), (3, 14))}
    xs = Ring("x", lambda p, h: strip.at[p * 2 + core, pl.ds(8 * h, 8)], xsend, xrecv, 0, (0, 1),
              lambda h: x_ref.at[pl.ds(8 * h, 8)])
    xm = Ring("x", lambda p, h: smeta.at[p * 2 + core], xsend, xrecv, 1, (0,), lambda h: m_ref)

    def swap(what, p, j, n):
        g = p * 2 + core
        start(what.at[g], what.at[g], csend.at[n, j], crecv.at[n, j], {"core": 1 - core})

    def swapped(what, p, j, n):
        g = p * 2 + 1 - core
        copy(what.at[g], what.at[g], csend.at[n, j], crecv.at[n, j], {"core": 1 - core}).wait_recv()

    source = (x == z) & (core == y // 2)
    low = lax.rem(y, 2) * 8

    def add_chunk(dz, dy):
        both = (dz, dy) not in ((0, 0), (0, 2), (2, 0), (2, 2))
        g = lax.rem(z + dz, 4) * 4 + lax.rem(y + dy, 4)
        group, base = g // 2, lax.rem(g, 2) * 8

        @pl.when(source)
        def _():
            def step(n, c):
                lefts, rights = [], []
                for u in range(4):
                    k, w = n * 2 + u // 2, u % 2
                    i = p_idx[g, w, k] - low
                    ok = (w < p_idx[g, 2, k]) & (i >= 0) & (i < ROWS)
                    i = jnp.clip(i, 0, ROWS - 1)
                    stored = s_idx[group, 2, i]
                    first = (s_idx[group, 0, i] == base + k) & (stored > 0)
                    second = (s_idx[group, 1, i] == base + k) & (stored > 1)
                    sign = 1 - 2 * p_idx[here, 4, i]
                    if both:
                        sign = jnp.where(p_idx[g, 4, k] == p_idx[here, 4, i], sign, 0)
                    weight = jnp.where(ok & (first | second), sign, 0).astype(jnp.float32)
                    left = strip[group, i * 2 + jnp.where(second, 1, 0)]
                    lefts.append((left.astype(jnp.float32) * weight).astype(jnp.bfloat16))
                    rights.append(panel[g, k * 2 + w])
                product = jnp.dot(jnp.concatenate(lefts, axis=1), jnp.concatenate(rights, axis=0),
                                  preferred_element_type=jnp.float32)
                acc[...] += 2.0 * product if both else product
                return c

            lax.fori_loop(0, 4, step, 0)

    def list_pairs():
        def row(i, c):
            for g in range(8):
                stored = s_idx[g, 2, i]
                for u in range(CAP):
                    k = s_idx[g, u, i]
                    chunk, r = 2 * g + k // 8, k % 8
                    inner = jnp.where(u < stored, p_idx[chunk, 2, r], 0)
                    for w in range(CAP):
                        col = jnp.where(w < inner, p_idx[chunk, w, r], 16)
                        place_b = (16 * g + k) * CAP + w
                        e_idx[i, (g * CAP + u) * CAP + w] = (place_b * 128 + g * OWN + i * CAP + u) * 32 + col
            return c

        lax.fori_loop(0, ROWS, row, 0)
        c = pltpu.make_async_copy(e_idx, entries, lsem.at[6])
        c.start()
        c.wait()

    def list_slots():
        lane = lax.broadcasted_iota(jnp.int32, (ROWS, BS), 1)
        sub = lax.broadcasted_iota(jnp.int32, (ROWS, BS), 0)
        entry = entries[...]
        col = jnp.where(lane < 32, entry % 32, 16)
        tab = jnp.zeros((ROWS, BS), jnp.int32)
        big = jnp.zeros((ROWS, 1), jnp.int32)
        by_row = [
            jnp.sum(jnp.where(lane == sub, jnp.broadcast_to(m_ref[f : f + 1, :], (ROWS, BS)), 0), axis=1, keepdims=True)
            for f in range(5)
        ]
        live = by_row[3]
        for t in range(YCAP):
            want = jnp.where(t < live, y_mem[:, t : t + 1], 17)
            hit = (col == want).astype(jnp.int32)
            upto = hit
            for shift in (1, 2, 4, 8, 16):
                upto = upto + jnp.where(lane >= shift, pltpu.roll(upto, shift, 1), 0)
            count = jnp.sum(hit, axis=1, keepdims=True)
            own = jnp.full((ROWS, 1), ZERO, jnp.int32)
            for u in range(CAP):
                mine_u = (by_row[u] == want) & (u < by_row[2])
                own = jnp.where(mine_u, here * OWN + sub[:, :1] * CAP + u, own)
            for n in range(PAIRS):
                found = jnp.sum(jnp.where((hit == 1) & (upto == n + 1), entry, 0), axis=1, keepdims=True)
                tab = jnp.where(lane == t * WIDTH + n, jnp.where(count > n, found, NONE), tab)
            tab = jnp.where(lane == t * WIDTH + PAIRS, count, tab)
            tab = jnp.where(lane == t * WIDTH + PAIRS + 1, own, tab)
            tab = jnp.where((lane == BIG + 1 + big) & (count > DIRECT), t, tab)
            big = big + jnp.where(count > DIRECT, 1, 0)
        tab = jnp.where(lane == FLAG, by_row[4], tab)
        table[...] = jnp.where(lane == BIG, big, tab)
        c = pltpu.make_async_copy(table, t_idx, lsem.at[8])
        c.start()
        c.wait()

    def multiply(first, last):
        def row(i, c):
            sign, twice = signs(t_idx, i)
            for t in range(YCAP):
                product = dot_pairs(strip, panel, [t_idx[i, t * WIDTH + n] for n in range(DIRECT)])
                own = t_idx[i, t * WIDTH + PAIRS + 1]
                updated = sign * product + twice * panel[own >> 4, own & 15].astype(jnp.float32)
                slots[i, t] = updated.astype(jnp.bfloat16)
            return c

        def rows(n, c):
            for u in range(4):
                row(n * 4 + u, c)
            return c

        lax.fori_loop(first // 4, last // 4, rows, 0)

    one, two = slice(0, 1), slice(1, 2)
    mz.own()
    my[0].own()
    xm.own()
    az.own(part=one)
    by.own(part=one)
    xs.own(part=one)
    for c in local:
        c.wait()
    swap(smeta, x, 0, 1)
    for q in (0, 1):
        mz.arrive(q)
    my[1].own()
    my[3].own()
    for q in (0, 1):
        my[0].arrive(q)
        xm.arrive(q)
    az.own(part=two)
    by.own(part=two)
    xs.own(part=two)
    for q in (0, 1):
        swap(smeta, (before, after)[q]["x"], 1 + q, 1)
    swap(strip, x, 0, 0)
    for part in (one, two):
        ay[0].own(part=part)
        bz[0].own(part=part)
        if part == one:
            mz.arrive_across()
            my[2].own()
            for q in (0, 1):
                az.arrive(q, one)
                by.arrive(q, one)
            for d in (1, 3):
                for q in (0, 1):
                    my[d].arrive(q)
    for q in (0, 1):
        az.arrive(q, two)
        by.arrive(q, two)
    ay[1].own()
    bz[1].own()
    my[0].arrive_across()
    for q in (0, 1):
        my[2].arrive(q)
    xm.arrive_across()
    swap(smeta, across["x"], 3, 1)
    for q in (0, 1):
        xs.arrive(q)
        swap(strip, (before, after)[q]["x"], 1 + q, 0)
    az.arrive_across()
    by.arrive_across()
    ay[2].own()
    bz[2].own()
    ay[3].own((1,))
    for d in (1, 3):
        my[d].arrive_across()
    xs.arrive_across()
    swap(strip, across["x"], 3, 0)
    for q in (0, 1):
        bz[0].arrive(q)
    ay[1].arrive(0)
    ay[1].arrive(1)
    ay[0].arrive(0)
    ay[0].arrive(1)
    for q in (0, 1):
        bz[1].arrive(q)
    my[2].arrive_across()
    for p, j in ((x, 0), (before["x"], 1), (after["x"], 2), (across["x"], 3)):
        swapped(smeta, p, j, 1)
        swapped(strip, p, j, 0)
    index_copies = [pltpu.make_async_copy(pmeta, p_idx, lsem.at[4]), pltpu.make_async_copy(smeta, s_idx, lsem.at[5])]
    for c in index_copies:
        c.start()
    for c in index_copies:
        c.wait()
    list_pairs()

    @pl.when(source)
    def _():
        for i in range(ROWS):
            flag = p_idx[here, 4, i]
            acc[...] += (2 * flag).astype(jnp.float32) * strip[line, i * 2].astype(jnp.float32)

    add_chunk(0, 0)
    add_chunk(1, 0)
    for q in (0, 1):
        ay[2].arrive(q)
        bz[2].arrive(q)
    ay[3].own((0,), one)
    bz[3].own()
    list_slots()
    add_chunk(0, 1)
    add_chunk(1, 1)
    bz[0].arrive_across()
    add_chunk(2, 0)
    ay[3].arrive(1, hold=(1,))
    add_chunk(3, 1)
    bz[1].arrive_across()
    add_chunk(2, 1)
    ay[1].arrive_across()
    add_chunk(1, 2)
    ay[0].arrive_across()
    add_chunk(0, 2)
    bz[2].arrive_across()
    ay[2].arrive_across()
    add_chunk(2, 2)

    @pl.when(source)
    def _():
        eye = lax.broadcasted_iota(jnp.int32, (BS, BS), 0) == lax.broadcasted_iota(jnp.int32, (BS, BS), 1)
        total = jnp.full((1, BS), jnp.sum(jnp.where(eye, acc[...], 0.0)))
        mine[0] = total
        plane_tr[lax.rem(y, 2)] = total

    far = [(dz, dy) for dz in (2, 1, 3, 0) for dy in (2, 1, 3, 0) if dz or dy]

    def tell_plane(n):
        dz, dy = far[n]
        return copy(mine.at[0], plane_tr.at[lax.rem(y, 2)], asend.at[n], arecv.at[lax.rem(y, 2)],
                    {"z": lax.rem(z + dz, 4), "y": lax.rem(y + dy, 4)})

    @pl.when(source)
    def _():
        for n in range(len(far)):
            tell_plane(n).start()

    ay[3].own((0,), two)
    ay[3].pass_on(1, 1)

    for part in (one, two):
        for q in (0, 1):
            bz[3].arrive(q, part)
    for t in range(2):
        @pl.when(jnp.logical_not(source & (lax.rem(y, 2) == t)))
        def _():
            copy(mine.at[0], plane_tr.at[t], asend.at[0], arecv.at[t], {"core": 1 - core}).wait_recv()

    total = plane_tr[0] + plane_tr[1]
    mine[1] = total
    line_tr[line] = total
    others = [(dx, dc) for dx in (2, 1, 3, 0) for dc in (1, 0) if dx or dc]
    for n, (dx, dc) in enumerate(others):
        start(mine.at[1], line_tr.at[line], bsend.at[n], brecv.at[line],
              {"x": lax.rem(x + dx, 4), "core": lax.rem(core + dc, 2)})
    ay[3].arrive(0)
    ay[3].arrive_across()
    bz[3].arrive_across()
    multiply(0, ROWS)
    @pl.when(source)
    def _():
        for n in range(len(far)):
            tell_plane(n).wait_send()

    for c in sends:
        c.wait_send()

    for dx, dc in others:
        g = lax.rem(x + dx, 4) * 2 + lax.rem(core + dc, 2)
        copy(mine.at[1], line_tr.at[g], bsend.at[0], brecv.at[g], {"core": 1 - core}).wait_recv()
    result = line_tr[0]
    for g in range(1, 8):
        result = result + line_tr[g]
    trace[...] = result


def finish_kernel(table, entries, strip, panel, slots, out, redone, found, osem):
    for i in range(ROWS):
        @pl.when(table[i, BIG] == 0)
        def _():
            pltpu.make_async_copy(slots.at[i], out.at[i], osem.at[i]).start()

    def redo(i, t):
        count = table[i, t * WIDTH + PAIRS]
        sign, twice = signs(table, i)
        own = table[i, t * WIDTH + PAIRS + 1]

        def store(product):
            updated = sign * product + twice * panel[own >> 4, own & 15].astype(jnp.float32)
            redone[i, t] = updated.astype(jnp.bfloat16)

        @pl.when(count <= PAIRS)
        def _():
            store(dot_pairs(strip, panel, [table[i, t * WIDTH + n] for n in range(PAIRS)]))

        @pl.when(count > PAIRS)
        def _():
            col = table[i, t * WIDTH] & 31
            n = 0
            for e in range(32):
                entry = entries[i, e]
                found[n] = entry
                n = n + jnp.where((entry & 31) == col, 1, 0)
            found[n] = NONE
            store(lax.fori_loop(
                1, (n + 1) // 2, lambda h, p: p + dot_pairs(strip, panel, [found[2 * h], found[2 * h + 1]]),
                dot_pairs(strip, panel, [found[0], found[1]])))

    def row(i, carry):
        @pl.when(table[i, BIG] > 0)
        def _():
            def again(n, c):
                redo(i, table[i, BIG + 1 + n])
                return c

            lax.fori_loop(0, table[i, BIG], again, 0)

            def send(t, c):
                big = table[i, t * WIDTH + PAIRS] > DIRECT

                @pl.when(big)
                def _():
                    pltpu.make_async_copy(redone.at[i, t], out.at[i, t], osem.at[i]).start()

                @pl.when(jnp.logical_not(big))
                def _():
                    pltpu.make_async_copy(slots.at[i, t], out.at[i, t], osem.at[i]).start()

                return c

            lax.fori_loop(0, YCAP, send, 0)

        return carry

    lax.fori_loop(0, ROWS, row, 0)
    for i in range(ROWS):
        pltpu.make_async_copy(slots.at[i], out.at[i], osem.at[i]).wait()


def on_device(x_blocks, x_cols, x_count, y_cols, y_count, branch_flag):
    x_blocks = pltpu.with_memory_space_constraint(x_blocks.reshape(OWN, BS, BS), pltpu.HBM)
    indices = [
        pltpu.with_memory_space_constraint(a, pltpu.HBM)
        for a in (x_cols.T, x_count.T, y_count.T, branch_flag[None, :], y_cols)
    ]
    vmem, hbm, smem = (pl.BlockSpec(memory_space=m) for m in (pltpu.VMEM, pltpu.HBM, pltpu.SMEM))
    dma = pltpu.SemaphoreType.DMA
    strip, panel, slots, trace, table, entries = pl.pallas_call(
        gather_kernel,
        out_shape=[
            pltpu.VMEM((8, OWN, BS, BS), jnp.bfloat16),
            pltpu.VMEM((17, OWN, BS, BS), jnp.bfloat16),
            pltpu.VMEM((ROWS, YCAP, BS, BS), jnp.bfloat16),
            jax.ShapeDtypeStruct((1, BS), jnp.float32),
            pltpu.VMEM((ROWS, BS), jnp.int32),
            pltpu.VMEM((ROWS, BS), jnp.int32),
        ],
        in_specs=[hbm] * 6,
        out_specs=[vmem] * 6,
        scratch_shapes=[
            pltpu.VMEM((8, ROWS, BS), jnp.int32),
            pltpu.VMEM((16, ROWS, BS), jnp.int32),
            pltpu.VMEM((ROWS, BS), jnp.int32),
            pltpu.VMEM((CAP, ROWS), jnp.int32),
            pltpu.VMEM((1, ROWS), jnp.int32),
            pltpu.VMEM((1, ROWS), jnp.int32),
            pltpu.VMEM((1, ROWS), jnp.int32),
            pltpu.VMEM((ROWS, YCAP), jnp.int32),
            pltpu.SMEM((8, ROWS, BS), jnp.int32),
            pltpu.SMEM((16, ROWS, BS), jnp.int32),
            pltpu.SMEM((ROWS, BS), jnp.int32),
            pltpu.SMEM((ROWS, BS), jnp.int32),
            pltpu.VMEM((BS, BS), jnp.float32),
            pltpu.VMEM((2, 1, BS), jnp.float32),
            pltpu.VMEM((2, 1, BS), jnp.float32),
            pltpu.VMEM((8, 1, BS), jnp.float32),
            dma((15, 6)),
            dma((15, 6)),
            dma((2, 6)),
            dma((2, 6)),
            dma((2, 4)),
            dma((2, 4)),
            dma((9,)),
            dma((4,)),
            dma((15,)),
            dma((2,)),
            dma((7,)),
            dma((8,)),
        ],
        compiler_params=pltpu.CompilerParams(collective_id=0, has_side_effects=True, vmem_limit_bytes=16 << 20),
    )(x_blocks, *indices)
    out = pl.pallas_call(
        finish_kernel,
        out_shape=jax.ShapeDtypeStruct((ROWS, YCAP, BS, BS), jnp.bfloat16),
        in_specs=[smem] * 2 + [vmem] * 3,
        out_specs=hbm,
        scratch_shapes=[
            pltpu.VMEM((ROWS, YCAP, BS, BS), jnp.bfloat16),
            pltpu.SMEM((40,), jnp.int32),
            dma((ROWS,)),
        ],
        compiler_params=pltpu.CompilerParams(vmem_limit_bytes=16 << 20),
    )(table, entries, strip, panel, slots)
    return out, trace[0, :1]


def solution(mesh):
    finer = Mesh(mesh.devices.reshape(4, 4, 4, 2), ALL)
    placed = (
        P(LINE, ("x", "core"), None, None),
        P(LINE, ("x", "core")),
        P(LINE, ("x", "core")),
        P(LINE, ("x", "core")),
        P(LINE, ("x", "core")),
        P(LINE),
    )
    return jax.shard_map(
        on_device,
        mesh=finer,
        in_specs=placed,
        out_specs=(P(LINE, ("x", "core"), None, None), P()),
        check_vma=False,
    )
```

```python
import jax
import jax.numpy as jnp
from jax import lax
from jax.experimental import pallas as pl
from jax.experimental.pallas import tpu as pltpu
from jax.sharding import Mesh
from jax.sharding import PartitionSpec as P

BS = 128
ROWS = 8
CAP = 2
YCAP = 12
OWN = ROWS * CAP
LINE = ("z", "y")
ALL = ("z", "y", "x", "core")
MESH_ID = pl.DeviceIdType.MESH
ZERO = 256
NONE = ZERO * 128 * 32 + 16
DIRECT = 3
PAIRS = 4
WIDTH = PAIRS + 2
FLAG = YCAP * WIDTH
BIG = FLAG + 1


def signs(table, i):
    flip = table[i, FLAG] == 1
    return jnp.where(flip, -1.0, 1.0), jnp.where(flip, 2.0, 0.0)


def dot_pairs(strip, panel, entries):
    a = jnp.concatenate([strip[(e >> 9) & 7, (e >> 5) & 15] for e in entries], axis=1)
    b = jnp.concatenate([panel[e >> 16, (e >> 12) & 15] for e in entries], axis=0)
    return jnp.dot(a, b, preferred_element_type=jnp.float32)


def gather_kernel(x_ref, *refs):
    (cols_ref, x_count_ref, y_count_ref, flag_ref, y_ref, strip, panel, slots, trace, table, entries, smeta, pmeta,
     m_ref, cols_mem, x_count_mem, y_count_mem, flag_mem, y_mem, s_idx, p_idx, e_idx, t_idx, acc, mine, plane_tr, line_tr,
     psend, precv, xsend, xrecv, csend, crecv, lsem, msem, asend, arecv, bsend, brecv) = refs
    place = {a: lax.axis_index(a) for a in ("z", "y", "x")}
    after = {a: lax.rem(v + 1, 4) for a, v in place.items()}
    before = {a: lax.rem(v + 3, 4) for a, v in place.items()}
    across = {a: lax.rem(v + 2, 4) for a, v in place.items()}
    core = lax.axis_index("core")
    z, y, x = place["z"], place["y"], place["x"]
    here, line = z * 4 + y, x * 2 + core

    barrier = pltpu.get_barrier_semaphore()
    peers = [{a: to[a]} for a in ("z", "y", "x") for to in (after, before)] + [{"core": 1 - core}]
    for peer in peers:
        pl.semaphore_signal(barrier, inc=1, device_id=peer, device_id_type=MESH_ID)

    local = [
        pltpu.make_async_copy(x_ref, panel.at[here], lsem.at[0]),
        pltpu.make_async_copy(x_ref, strip.at[line], lsem.at[1]),
        pltpu.make_async_copy(y_ref, y_mem, lsem.at[7]),
    ]
    fields = ((cols_ref, cols_mem), (x_count_ref, x_count_mem), (y_count_ref, y_count_mem), (flag_ref, flag_mem))
    small = [pltpu.make_async_copy(a, b, msem.at[n]) for n, (a, b) in enumerate(fields)]
    for c in small + local:
        c.start()
    for c in small:
        c.wait()
    for row, (_, b) in zip((0, 2, 3, 4), fields):
        for tile in (m_ref, smeta.at[line], pmeta.at[here]):
            tile[row : row + b.shape[0], :ROWS] = b[...]
    panel[16, 0] = jnp.zeros((BS, BS), jnp.bfloat16)
    acc[...] = jnp.zeros_like(acc)
    pl.semaphore_wait(barrier, len(peers))

    sends = []

    def copy(src, dst, ss, rs, peer):
        return pltpu.make_async_remote_copy(
            src_ref=src, dst_ref=dst, send_sem=ss, recv_sem=rs, device_id=peer, device_id_type=MESH_ID
        )

    def start(*args):
        c = copy(*args)
        c.start()
        sends.append(c)

    class Ring:
        def __init__(self, axis, at, ssem, rsem, j, via=(0, 1), src=None):
            self.axis, self.at, self.ssem, self.rsem, self.j, self.via = axis, at, ssem, rsem, j, via
            self.src = src or (lambda h: at(place[axis], h))

        def order(self, q):
            return sorted(range(len(self.via)), key=lambda h: self.via[h] != q)

        def own(self, qs=(0, 1), part=slice(None)):
            for q in qs:
                to = (after, before)[q][self.axis]
                for h in self.order(q)[part]:
                    n = q * 2 + h
                    start(self.src(h), self.at(place[self.axis], h), self.ssem.at[self.j, n], self.rsem.at[self.j, n],
                          {self.axis: to})

        def arrive(self, q, part=slice(None), hold=()):
            owner = (before, after)[q][self.axis]
            for h in self.order(q)[part]:
                n, piece = q * 2 + h, self.at(owner, h)
                copy(piece, piece, self.ssem.at[self.j, n], self.rsem.at[self.j, n], {self.axis: owner}).wait_recv()
                if self.via[h] == q and h not in hold:
                    self.pass_on(q, h)

        def pass_on(self, q, h):
            piece = self.at((before, after)[q][self.axis], h)
            start(piece, piece, self.ssem.at[self.j, 4 + h], self.rsem.at[self.j, 4 + h],
                  {self.axis: (after, before)[q][self.axis]})

        def arrive_across(self):
            for h in range(len(self.via)):
                piece = self.at(across[self.axis], h)
                copy(piece, piece, self.ssem.at[self.j, 4 + h], self.rsem.at[self.j, 4 + h],
                     {self.axis: before[self.axis]}).wait_recv()

    def chunk_of(axis, d, p):
        o = lax.rem((y if axis == "z" else z) + d, 4)
        return p * 4 + o if axis == "z" else o * 4 + p

    def panel_ring(axis, d, lo, j, via=(0, 1)):
        src = (lambda h: x_ref.at[pl.ds(lo + 4 * h, 4)]) if d == 0 else None
        return Ring(axis, lambda p, h: panel.at[chunk_of(axis, d, p), pl.ds(lo + 4 * h, 4)], psend, precv, j, via, src)

    def pmeta_ring(axis, d, j):
        src = (lambda h: m_ref) if d == 0 else None
        return Ring(axis, lambda p, h: pmeta.at[chunk_of(axis, d, p)], psend, precv, j, (0,), src)

    az, by = panel_ring("z", 0, 0, 0), panel_ring("y", 0, 8, 1)
    ay = {d: panel_ring("y", d, 0, j, v) for d, j, v in ((0, 2, (0, 1)), (1, 3, (0, 0)), (2, 4, (0, 1)), (3, 5, (1, 1)))}
    bz = {d: panel_ring("z", d, 8, j) for d, j in ((0, 6), (1, 7), (2, 8), (3, 9))}
    mz = pmeta_ring("z", 0, 10)
    my = {d: pmeta_ring("y", d, j) for d, j in ((0, 11), (1, 12), (2, 13), (3, 14))}
    xs = Ring("x", lambda p, h: strip.at[p * 2 + core, pl.ds(8 * h, 8)], xsend, xrecv, 0, (0, 1),
              lambda h: x_ref.at[pl.ds(8 * h, 8)])
    xm = Ring("x", lambda p, h: smeta.at[p * 2 + core], xsend, xrecv, 1, (0,), lambda h: m_ref)

    def swap(what, p, j, n):
        g = p * 2 + core
        start(what.at[g], what.at[g], csend.at[n, j], crecv.at[n, j], {"core": 1 - core})

    def swapped(what, p, j, n):
        g = p * 2 + 1 - core
        copy(what.at[g], what.at[g], csend.at[n, j], crecv.at[n, j], {"core": 1 - core}).wait_recv()

    source = (x == z) & (core == y // 2)
    low = lax.rem(y, 2) * 8

    def add_chunk(dz, dy):
        both = (dz, dy) not in ((0, 0), (0, 2), (2, 0), (2, 2))
        g = lax.rem(z + dz, 4) * 4 + lax.rem(y + dy, 4)
        group, base = g // 2, lax.rem(g, 2) * 8

        @pl.when(source)
        def _():
            def step(n, c):
                lefts, rights = [], []
                for u in range(8):
                    k, w = n * 4 + u // 2, u % 2
                    i = p_idx[g, w, k] - low
                    ok = (w < p_idx[g, 2, k]) & (i >= 0) & (i < ROWS)
                    i = jnp.clip(i, 0, ROWS - 1)
                    stored = s_idx[group, 2, i]
                    first = (s_idx[group, 0, i] == base + k) & (stored > 0)
                    second = (s_idx[group, 1, i] == base + k) & (stored > 1)
                    sign = 1 - 2 * p_idx[here, 4, i]
                    if both:
                        sign = jnp.where(p_idx[g, 4, k] == p_idx[here, 4, i], sign, 0)
                    weight = jnp.where(ok & (first | second), sign, 0).astype(jnp.float32)
                    left = strip[group, i * 2 + jnp.where(second, 1, 0)]
                    lefts.append((left.astype(jnp.float32) * weight).astype(jnp.bfloat16))
                    rights.append(panel[g, k * 2 + w])
                product = jnp.dot(jnp.concatenate(lefts, axis=1), jnp.concatenate(rights, axis=0),
                                  preferred_element_type=jnp.float32)
                acc[...] += 2.0 * product if both else product
                return c

            lax.fori_loop(0, 2, step, 0)

    def list_pairs():
        def row(i, c):
            for g in range(8):
                stored = s_idx[g, 2, i]
                for u in range(CAP):
                    k = s_idx[g, u, i]
                    chunk, r = 2 * g + k // 8, k % 8
                    inner = jnp.where(u < stored, p_idx[chunk, 2, r], 0)
                    for w in range(CAP):
                        col = jnp.where(w < inner, p_idx[chunk, w, r], 16)
                        place_b = (16 * g + k) * CAP + w
                        e_idx[i, (g * CAP + u) * CAP + w] = (place_b * 128 + g * OWN + i * CAP + u) * 32 + col
            return c

        lax.fori_loop(0, ROWS, row, 0)
        c = pltpu.make_async_copy(e_idx, entries, lsem.at[6])
        c.start()
        c.wait()

    def list_slots():
        lane = lax.broadcasted_iota(jnp.int32, (ROWS, BS), 1)
        sub = lax.broadcasted_iota(jnp.int32, (ROWS, BS), 0)
        entry = entries[...]
        col = jnp.where(lane < 32, entry % 32, 16)
        tab = jnp.zeros((ROWS, BS), jnp.int32)
        big = jnp.zeros((ROWS, 1), jnp.int32)
        by_row = [
            jnp.sum(jnp.where(lane == sub, jnp.broadcast_to(m_ref[f : f + 1, :], (ROWS, BS)), 0), axis=1, keepdims=True)
            for f in range(5)
        ]
        live = by_row[3]
        for t in range(YCAP):
            want = jnp.where(t < live, y_mem[:, t : t + 1], 17)
            hit = (col == want).astype(jnp.int32)
            upto = hit
            for shift in (1, 2, 4, 8, 16):
                upto = upto + jnp.where(lane >= shift, pltpu.roll(upto, shift, 1), 0)
            count = jnp.sum(hit, axis=1, keepdims=True)
            own = jnp.full((ROWS, 1), ZERO, jnp.int32)
            for u in range(CAP):
                mine_u = (by_row[u] == want) & (u < by_row[2])
                own = jnp.where(mine_u, here * OWN + sub[:, :1] * CAP + u, own)
            for n in range(PAIRS):
                found = jnp.sum(jnp.where((hit == 1) & (upto == n + 1), entry, 0), axis=1, keepdims=True)
                tab = jnp.where(lane == t * WIDTH + n, jnp.where(count > n, found, NONE), tab)
            tab = jnp.where(lane == t * WIDTH + PAIRS, count, tab)
            tab = jnp.where(lane == t * WIDTH + PAIRS + 1, own, tab)
            tab = jnp.where((lane == BIG + 1 + big) & (count > DIRECT), t, tab)
            big = big + jnp.where(count > DIRECT, 1, 0)
        tab = jnp.where(lane == FLAG, by_row[4], tab)
        table[...] = jnp.where(lane == BIG, big, tab)
        c = pltpu.make_async_copy(table, t_idx, lsem.at[8])
        c.start()
        c.wait()

    def multiply(first, last):
        def row(i, c):
            sign, twice = signs(t_idx, i)
            for t in range(YCAP):
                product = dot_pairs(strip, panel, [t_idx[i, t * WIDTH + n] for n in range(DIRECT)])
                own = t_idx[i, t * WIDTH + PAIRS + 1]
                updated = sign * product + twice * panel[own >> 4, own & 15].astype(jnp.float32)
                slots[i, t] = updated.astype(jnp.bfloat16)
            return c

        def rows(n, c):
            for u in range(4):
                row(n * 4 + u, c)
            return c

        lax.fori_loop(first // 4, last // 4, rows, 0)

    one, two = slice(0, 1), slice(1, 2)
    mz.own()
    my[0].own()
    xm.own()
    az.own(part=one)
    by.own(part=one)
    xs.own(part=one)
    for c in local:
        c.wait()
    swap(smeta, x, 0, 1)
    for q in (0, 1):
        mz.arrive(q)
    my[1].own()
    my[3].own()
    for q in (0, 1):
        my[0].arrive(q)
        xm.arrive(q)
    az.own(part=two)
    by.own(part=two)
    xs.own(part=two)
    for q in (0, 1):
        swap(smeta, (before, after)[q]["x"], 1 + q, 1)
    swap(strip, x, 0, 0)
    for part in (one, two):
        ay[0].own(part=part)
        bz[0].own(part=part)
        if part == one:
            mz.arrive_across()
            my[2].own()
            for q in (0, 1):
                az.arrive(q, one)
                by.arrive(q, one)
            for d in (1, 3):
                for q in (0, 1):
                    my[d].arrive(q)
    for q in (0, 1):
        az.arrive(q, two)
        by.arrive(q, two)
    ay[1].own()
    bz[1].own()
    my[0].arrive_across()
    for q in (0, 1):
        my[2].arrive(q)
    xm.arrive_across()
    swap(smeta, across["x"], 3, 1)
    for q in (0, 1):
        xs.arrive(q)
        swap(strip, (before, after)[q]["x"], 1 + q, 0)
    az.arrive_across()
    by.arrive_across()
    ay[2].own()
    bz[2].own()
    ay[3].own((1,))
    for d in (1, 3):
        my[d].arrive_across()
    xs.arrive_across()
    swap(strip, across["x"], 3, 0)
    for q in (0, 1):
        bz[0].arrive(q)
    ay[1].arrive(0)
    ay[1].arrive(1)
    ay[0].arrive(0)
    ay[0].arrive(1)
    for q in (0, 1):
        bz[1].arrive(q)
    my[2].arrive_across()
    for p, j in ((x, 0), (before["x"], 1), (after["x"], 2), (across["x"], 3)):
        swapped(smeta, p, j, 1)
        swapped(strip, p, j, 0)
    index_copies = [pltpu.make_async_copy(pmeta, p_idx, lsem.at[4]), pltpu.make_async_copy(smeta, s_idx, lsem.at[5])]
    for c in index_copies:
        c.start()
    for c in index_copies:
        c.wait()
    list_pairs()

    @pl.when(source)
    def _():
        for i in range(ROWS):
            flag = p_idx[here, 4, i]
            acc[...] += (2 * flag).astype(jnp.float32) * strip[line, i * 2].astype(jnp.float32)

    add_chunk(0, 0)
    add_chunk(1, 0)
    for q in (0, 1):
        ay[2].arrive(q)
        bz[2].arrive(q)
    ay[3].own((0,), one)
    bz[3].own()
    list_slots()
    add_chunk(0, 1)
    add_chunk(1, 1)
    bz[0].arrive_across()
    add_chunk(2, 0)
    ay[3].arrive(1, hold=(1,))
    add_chunk(3, 1)
    bz[1].arrive_across()
    add_chunk(2, 1)
    ay[1].arrive_across()
    add_chunk(1, 2)
    ay[0].arrive_across()
    add_chunk(0, 2)
    bz[2].arrive_across()
    ay[2].arrive_across()
    add_chunk(2, 2)

    @pl.when(source)
    def _():
        eye = lax.broadcasted_iota(jnp.int32, (BS, BS), 0) == lax.broadcasted_iota(jnp.int32, (BS, BS), 1)
        total = jnp.full((1, BS), jnp.sum(jnp.where(eye, acc[...], 0.0)))
        mine[0] = total
        plane_tr[lax.rem(y, 2)] = total

    far = [(dz, dy) for dz in (2, 1, 3, 0) for dy in (2, 1, 3, 0) if dz or dy]

    def tell_plane(n):
        dz, dy = far[n]
        return copy(mine.at[0], plane_tr.at[lax.rem(y, 2)], asend.at[n], arecv.at[lax.rem(y, 2)],
                    {"z": lax.rem(z + dz, 4), "y": lax.rem(y + dy, 4)})

    @pl.when(source)
    def _():
        for n in range(len(far)):
            tell_plane(n).start()

    ay[3].own((0,), two)
    ay[3].pass_on(1, 1)

    for part in (one, two):
        for q in (0, 1):
            bz[3].arrive(q, part)
    for t in range(2):
        @pl.when(jnp.logical_not(source & (lax.rem(y, 2) == t)))
        def _():
            copy(mine.at[0], plane_tr.at[t], asend.at[0], arecv.at[t], {"core": 1 - core}).wait_recv()

    total = plane_tr[0] + plane_tr[1]
    mine[1] = total
    line_tr[line] = total
    others = [(dx, dc) for dx in (2, 1, 3, 0) for dc in (1, 0) if dx or dc]
    for n, (dx, dc) in enumerate(others):
        start(mine.at[1], line_tr.at[line], bsend.at[n], brecv.at[line],
              {"x": lax.rem(x + dx, 4), "core": lax.rem(core + dc, 2)})
    ay[3].arrive(0)
    ay[3].arrive_across()
    bz[3].arrive_across()
    multiply(0, ROWS)
    @pl.when(source)
    def _():
        for n in range(len(far)):
            tell_plane(n).wait_send()

    for c in sends:
        c.wait_send()

    for dx, dc in others:
        g = lax.rem(x + dx, 4) * 2 + lax.rem(core + dc, 2)
        copy(mine.at[1], line_tr.at[g], bsend.at[0], brecv.at[g], {"core": 1 - core}).wait_recv()
    result = line_tr[0]
    for g in range(1, 8):
        result = result + line_tr[g]
    trace[...] = result


def finish_kernel(table, entries, strip, panel, slots, out, redone, found, osem):
    for i in range(ROWS):
        @pl.when(table[i, BIG] == 0)
        def _():
            pltpu.make_async_copy(slots.at[i], out.at[i], osem.at[i]).start()

    def redo(i, t):
        count = table[i, t * WIDTH + PAIRS]
        sign, twice = signs(table, i)
        own = table[i, t * WIDTH + PAIRS + 1]

        def store(product):
            updated = sign * product + twice * panel[own >> 4, own & 15].astype(jnp.float32)
            redone[i, t] = updated.astype(jnp.bfloat16)

        @pl.when(count <= PAIRS)
        def _():
            store(dot_pairs(strip, panel, [table[i, t * WIDTH + n] for n in range(PAIRS)]))

        @pl.when(count > PAIRS)
        def _():
            col = table[i, t * WIDTH] & 31
            n = 0
            for e in range(32):
                entry = entries[i, e]
                found[n] = entry
                n = n + jnp.where((entry & 31) == col, 1, 0)
            found[n] = NONE
            store(lax.fori_loop(
                1, (n + 1) // 2, lambda h, p: p + dot_pairs(strip, panel, [found[2 * h], found[2 * h + 1]]),
                dot_pairs(strip, panel, [found[0], found[1]])))

    def row(i, carry):
        @pl.when(table[i, BIG] > 0)
        def _():
            def again(n, c):
                redo(i, table[i, BIG + 1 + n])
                return c

            lax.fori_loop(0, table[i, BIG], again, 0)

            def send(t, c):
                big = table[i, t * WIDTH + PAIRS] > DIRECT

                @pl.when(big)
                def _():
                    pltpu.make_async_copy(redone.at[i, t], out.at[i, t], osem.at[i]).start()

                @pl.when(jnp.logical_not(big))
                def _():
                    pltpu.make_async_copy(slots.at[i, t], out.at[i, t], osem.at[i]).start()

                return c

            lax.fori_loop(0, YCAP, send, 0)

        return carry

    lax.fori_loop(0, ROWS, row, 0)
    for i in range(ROWS):
        pltpu.make_async_copy(slots.at[i], out.at[i], osem.at[i]).wait()


def on_device(x_blocks, x_cols, x_count, y_cols, y_count, branch_flag):
    x_blocks = pltpu.with_memory_space_constraint(x_blocks.reshape(OWN, BS, BS), pltpu.HBM)
    indices = [
        pltpu.with_memory_space_constraint(a, pltpu.HBM)
        for a in (x_cols.T, x_count.T, y_count.T, branch_flag[None, :], y_cols)
    ]
    vmem, hbm, smem = (pl.BlockSpec(memory_space=m) for m in (pltpu.VMEM, pltpu.HBM, pltpu.SMEM))
    dma = pltpu.SemaphoreType.DMA
    strip, panel, slots, trace, table, entries = pl.pallas_call(
        gather_kernel,
        out_shape=[
            pltpu.VMEM((8, OWN, BS, BS), jnp.bfloat16),
            pltpu.VMEM((17, OWN, BS, BS), jnp.bfloat16),
            pltpu.VMEM((ROWS, YCAP, BS, BS), jnp.bfloat16),
            jax.ShapeDtypeStruct((1, BS), jnp.float32),
            pltpu.VMEM((ROWS, BS), jnp.int32),
            pltpu.VMEM((ROWS, BS), jnp.int32),
        ],
        in_specs=[hbm] * 6,
        out_specs=[vmem] * 6,
        scratch_shapes=[
            pltpu.VMEM((8, ROWS, BS), jnp.int32),
            pltpu.VMEM((16, ROWS, BS), jnp.int32),
            pltpu.VMEM((ROWS, BS), jnp.int32),
            pltpu.VMEM((CAP, ROWS), jnp.int32),
            pltpu.VMEM((1, ROWS), jnp.int32),
            pltpu.VMEM((1, ROWS), jnp.int32),
            pltpu.VMEM((1, ROWS), jnp.int32),
            pltpu.VMEM((ROWS, YCAP), jnp.int32),
            pltpu.SMEM((8, ROWS, BS), jnp.int32),
            pltpu.SMEM((16, ROWS, BS), jnp.int32),
            pltpu.SMEM((ROWS, BS), jnp.int32),
            pltpu.SMEM((ROWS, BS), jnp.int32),
            pltpu.VMEM((BS, BS), jnp.float32),
            pltpu.VMEM((2, 1, BS), jnp.float32),
            pltpu.VMEM((2, 1, BS), jnp.float32),
            pltpu.VMEM((8, 1, BS), jnp.float32),
            dma((15, 6)),
            dma((15, 6)),
            dma((2, 6)),
            dma((2, 6)),
            dma((2, 4)),
            dma((2, 4)),
            dma((9,)),
            dma((4,)),
            dma((15,)),
            dma((2,)),
            dma((7,)),
            dma((8,)),
        ],
        compiler_params=pltpu.CompilerParams(collective_id=0, has_side_effects=True, vmem_limit_bytes=16 << 20),
    )(x_blocks, *indices)
    out = pl.pallas_call(
        finish_kernel,
        out_shape=jax.ShapeDtypeStruct((ROWS, YCAP, BS, BS), jnp.bfloat16),
        in_specs=[smem] * 2 + [vmem] * 3,
        out_specs=hbm,
        scratch_shapes=[
            pltpu.VMEM((ROWS, YCAP, BS, BS), jnp.bfloat16),
            pltpu.SMEM((40,), jnp.int32),
            dma((ROWS,)),
        ],
        compiler_params=pltpu.CompilerParams(vmem_limit_bytes=16 << 20),
    )(table, entries, strip, panel, slots)
    return out, trace[0, :1]


def solution(mesh):
    finer = Mesh(mesh.devices.reshape(4, 4, 4, 2), ALL)
    placed = (
        P(LINE, ("x", "core"), None, None),
        P(LINE, ("x", "core")),
        P(LINE, ("x", "core")),
        P(LINE, ("x", "core")),
        P(LINE, ("x", "core")),
        P(LINE),
    )
    return jax.shard_map(
        on_device,
        mesh=finer,
        in_specs=placed,
        out_specs=(P(LINE, ("x", "core"), None, None), P()),
        check_vma=False,
    )
```

```python
import jax
import jax.numpy as jnp
from jax import lax
from jax.experimental import pallas as pl
from jax.experimental.pallas import tpu as pltpu
from jax.sharding import Mesh
from jax.sharding import PartitionSpec as P

BS = 128
ROWS = 8
CAP = 2
YCAP = 12
OWN = ROWS * CAP
LINE = ("z", "y")
ALL = ("z", "y", "x", "core")
MESH_ID = pl.DeviceIdType.MESH
ZERO = 256
NONE = ZERO * 128 * 32 + 16
DIRECT = 3
PAIRS = 4
WIDTH = PAIRS + 2
FLAG = YCAP * WIDTH
BIG = FLAG + 1


def signs(table, i):
    flip = table[i, FLAG] == 1
    return jnp.where(flip, -1.0, 1.0), jnp.where(flip, 2.0, 0.0)


def dot_pairs(strip, panel, entries):
    a = jnp.concatenate([strip[(e >> 9) & 7, (e >> 5) & 15] for e in entries], axis=1)
    b = jnp.concatenate([panel[e >> 16, (e >> 12) & 15] for e in entries], axis=0)
    return jnp.dot(a, b, preferred_element_type=jnp.float32)


def gather_kernel(x_ref, *refs):
    (cols_ref, x_count_ref, y_count_ref, flag_ref, y_ref, strip, panel, slots, trace, table, entries, smeta, pmeta,
     m_ref, cols_mem, x_count_mem, y_count_mem, flag_mem, y_mem, s_idx, p_idx, e_idx, t_idx, acc, mine, plane_tr, line_tr,
     psend, precv, xsend, xrecv, csend, crecv, lsem, msem, asend, arecv, bsend, brecv) = refs
    place = {a: lax.axis_index(a) for a in ("z", "y", "x")}
    after = {a: lax.rem(v + 1, 4) for a, v in place.items()}
    before = {a: lax.rem(v + 3, 4) for a, v in place.items()}
    across = {a: lax.rem(v + 2, 4) for a, v in place.items()}
    core = lax.axis_index("core")
    z, y, x = place["z"], place["y"], place["x"]
    here, line = z * 4 + y, x * 2 + core

    barrier = pltpu.get_barrier_semaphore()
    peers = [{a: to[a]} for a in ("z", "y", "x") for to in (after, before)] + [{"core": 1 - core}]
    for peer in peers:
        pl.semaphore_signal(barrier, inc=1, device_id=peer, device_id_type=MESH_ID)

    local = [
        pltpu.make_async_copy(x_ref, panel.at[here], lsem.at[0]),
        pltpu.make_async_copy(x_ref, strip.at[line], lsem.at[1]),
        pltpu.make_async_copy(y_ref, y_mem, lsem.at[7]),
    ]
    fields = ((cols_ref, cols_mem), (x_count_ref, x_count_mem), (y_count_ref, y_count_mem), (flag_ref, flag_mem))
    small = [pltpu.make_async_copy(a, b, msem.at[n]) for n, (a, b) in enumerate(fields)]
    for c in small + local:
        c.start()
    for c in small:
        c.wait()
    for row, (_, b) in zip((0, 2, 3, 4), fields):
        for tile in (m_ref, smeta.at[line], pmeta.at[here]):
            tile[row : row + b.shape[0], :ROWS] = b[...]
    panel[16, 0] = jnp.zeros((BS, BS), jnp.bfloat16)
    acc[...] = jnp.zeros_like(acc)
    pl.semaphore_wait(barrier, len(peers))

    sends = []

    def copy(src, dst, ss, rs, peer):
        return pltpu.make_async_remote_copy(
            src_ref=src, dst_ref=dst, send_sem=ss, recv_sem=rs, device_id=peer, device_id_type=MESH_ID
        )

    def start(*args):
        c = copy(*args)
        c.start()
        sends.append(c)

    class Ring:
        def __init__(self, axis, at, ssem, rsem, j, via=(0, 1), src=None):
            self.axis, self.at, self.ssem, self.rsem, self.j, self.via = axis, at, ssem, rsem, j, via
            self.src = src or (lambda h: at(place[axis], h))

        def order(self, q):
            return sorted(range(len(self.via)), key=lambda h: self.via[h] != q)

        def own(self, qs=(0, 1), part=slice(None)):
            for q in qs:
                to = (after, before)[q][self.axis]
                for h in self.order(q)[part]:
                    n = q * 2 + h
                    start(self.src(h), self.at(place[self.axis], h), self.ssem.at[self.j, n], self.rsem.at[self.j, n],
                          {self.axis: to})

        def arrive(self, q, part=slice(None), hold=()):
            owner = (before, after)[q][self.axis]
            for h in self.order(q)[part]:
                n, piece = q * 2 + h, self.at(owner, h)
                copy(piece, piece, self.ssem.at[self.j, n], self.rsem.at[self.j, n], {self.axis: owner}).wait_recv()
                if self.via[h] == q and h not in hold:
                    self.pass_on(q, h)

        def pass_on(self, q, h):
            piece = self.at((before, after)[q][self.axis], h)
            start(piece, piece, self.ssem.at[self.j, 4 + h], self.rsem.at[self.j, 4 + h],
                  {self.axis: (after, before)[q][self.axis]})

        def arrive_across(self):
            for h in range(len(self.via)):
                piece = self.at(across[self.axis], h)
                copy(piece, piece, self.ssem.at[self.j, 4 + h], self.rsem.at[self.j, 4 + h],
                     {self.axis: before[self.axis]}).wait_recv()

    def chunk_of(axis, d, p):
        o = lax.rem((y if axis == "z" else z) + d, 4)
        return p * 4 + o if axis == "z" else o * 4 + p

    def panel_ring(axis, d, lo, j, via=(0, 1)):
        src = (lambda h: x_ref.at[pl.ds(lo + 4 * h, 4)]) if d == 0 else None
        return Ring(axis, lambda p, h: panel.at[chunk_of(axis, d, p), pl.ds(lo + 4 * h, 4)], psend, precv, j, via, src)

    def pmeta_ring(axis, d, j):
        src = (lambda h: m_ref) if d == 0 else None
        return Ring(axis, lambda p, h: pmeta.at[chunk_of(axis, d, p)], psend, precv, j, (0,), src)

    az, by = panel_ring("z", 0, 0, 0), panel_ring("y", 0, 8, 1)
    ay = {d: panel_ring("y", d, 0, j, v) for d, j, v in ((0, 2, (0, 1)), (1, 3, (0, 0)), (2, 4, (0, 1)), (3, 5, (1, 1)))}
    bz = {d: panel_ring("z", d, 8, j) for d, j in ((0, 6), (1, 7), (2, 8), (3, 9))}
    mz = pmeta_ring("z", 0, 10)
    my = {d: pmeta_ring("y", d, j) for d, j in ((0, 11), (1, 12), (2, 13), (3, 14))}
    xs = Ring("x", lambda p, h: strip.at[p * 2 + core, pl.ds(8 * h, 8)], xsend, xrecv, 0, (0, 1),
              lambda h: x_ref.at[pl.ds(8 * h, 8)])
    xm = Ring("x", lambda p, h: smeta.at[p * 2 + core], xsend, xrecv, 1, (0,), lambda h: m_ref)

    def swap(what, p, j, n):
        g = p * 2 + core
        start(what.at[g], what.at[g], csend.at[n, j], crecv.at[n, j], {"core": 1 - core})

    def swapped(what, p, j, n):
        g = p * 2 + 1 - core
        copy(what.at[g], what.at[g], csend.at[n, j], crecv.at[n, j], {"core": 1 - core}).wait_recv()

    source = (x == z) & (core == y // 2)
    low = lax.rem(y, 2) * 8

    def add_chunk(dz, dy):
        both = (dz, dy) not in ((0, 0), (0, 2), (2, 0), (2, 2))
        g = lax.rem(z + dz, 4) * 4 + lax.rem(y + dy, 4)
        group, base = g // 2, lax.rem(g, 2) * 8

        @pl.when(source)
        def _():
            def step(n, c):
                lefts, rights = [], []
                for u in range(8):
                    k, w = n * 4 + u // 2, u % 2
                    i = p_idx[g, w, k] - low
                    ok = (w < p_idx[g, 2, k]) & (i >= 0) & (i < ROWS)
                    i = jnp.clip(i, 0, ROWS - 1)
                    stored = s_idx[group, 2, i]
                    first = (s_idx[group, 0, i] == base + k) & (stored > 0)
                    second = (s_idx[group, 1, i] == base + k) & (stored > 1)
                    sign = 1 - 2 * p_idx[here, 4, i]
                    if both:
                        sign = jnp.where(p_idx[g, 4, k] == p_idx[here, 4, i], sign, 0)
                    weight = jnp.where(ok & (first | second), sign, 0).astype(jnp.float32)
                    left = strip[group, i * 2 + jnp.where(second, 1, 0)]
                    lefts.append((left.astype(jnp.float32) * weight).astype(jnp.bfloat16))
                    rights.append(panel[g, k * 2 + w])
                product = jnp.dot(jnp.concatenate(lefts, axis=1), jnp.concatenate(rights, axis=0),
                                  preferred_element_type=jnp.float32)
                acc[...] += 2.0 * product if both else product
                return c

            lax.fori_loop(0, 2, step, 0)

    def list_pairs():
        def row(i, c):
            for g in range(8):
                stored = s_idx[g, 2, i]
                for u in range(CAP):
                    k = s_idx[g, u, i]
                    chunk, r = 2 * g + k // 8, k % 8
                    inner = jnp.where(u < stored, p_idx[chunk, 2, r], 0)
                    for w in range(CAP):
                        col = jnp.where(w < inner, p_idx[chunk, w, r], 16)
                        place_b = (16 * g + k) * CAP + w
                        e_idx[i, (g * CAP + u) * CAP + w] = (place_b * 128 + g * OWN + i * CAP + u) * 32 + col
            return c

        lax.fori_loop(0, ROWS, row, 0)
        c = pltpu.make_async_copy(e_idx, entries, lsem.at[6])
        c.start()
        c.wait()

    def list_slots():
        lane = lax.broadcasted_iota(jnp.int32, (ROWS, BS), 1)
        sub = lax.broadcasted_iota(jnp.int32, (ROWS, BS), 0)
        entry = entries[...]
        col = jnp.where(lane < 32, entry % 32, 16)
        tab = jnp.zeros((ROWS, BS), jnp.int32)
        big = jnp.zeros((ROWS, 1), jnp.int32)
        by_row = [
            jnp.sum(jnp.where(lane == sub, jnp.broadcast_to(m_ref[f : f + 1, :], (ROWS, BS)), 0), axis=1, keepdims=True)
            for f in range(5)
        ]
        live = by_row[3]
        for t in range(YCAP):
            want = jnp.where(t < live, y_mem[:, t : t + 1], 17)
            hit = (col == want).astype(jnp.int32)
            upto = hit
            for shift in (1, 2, 4, 8, 16):
                upto = upto + jnp.where(lane >= shift, pltpu.roll(upto, shift, 1), 0)
            count = jnp.sum(hit, axis=1, keepdims=True)
            own = jnp.full((ROWS, 1), ZERO, jnp.int32)
            for u in range(CAP):
                mine_u = (by_row[u] == want) & (u < by_row[2])
                own = jnp.where(mine_u, here * OWN + sub[:, :1] * CAP + u, own)
            for n in range(PAIRS):
                found = jnp.sum(jnp.where((hit == 1) & (upto == n + 1), entry, 0), axis=1, keepdims=True)
                tab = jnp.where(lane == t * WIDTH + n, jnp.where(count > n, found, NONE), tab)
            tab = jnp.where(lane == t * WIDTH + PAIRS, count, tab)
            tab = jnp.where(lane == t * WIDTH + PAIRS + 1, own, tab)
            tab = jnp.where((lane == BIG + 1 + big) & (count > DIRECT), t, tab)
            big = big + jnp.where(count > DIRECT, 1, 0)
        tab = jnp.where(lane == FLAG, by_row[4], tab)
        table[...] = jnp.where(lane == BIG, big, tab)
        c = pltpu.make_async_copy(table, t_idx, lsem.at[8])
        c.start()
        c.wait()

    def multiply(first, last):
        def row(i, c):
            sign, twice = signs(t_idx, i)
            for t in range(YCAP):
                product = dot_pairs(strip, panel, [t_idx[i, t * WIDTH + n] for n in range(DIRECT)])
                own = t_idx[i, t * WIDTH + PAIRS + 1]
                updated = sign * product + twice * panel[own >> 4, own & 15].astype(jnp.float32)
                slots[i, t] = updated.astype(jnp.bfloat16)
            return c

        def rows(n, c):
            for u in range(4):
                row(n * 4 + u, c)
            return c

        lax.fori_loop(first // 4, last // 4, rows, 0)

    one, two = slice(0, 1), slice(1, 2)
    mz.own()
    my[0].own()
    xm.own()
    az.own(part=one)
    by.own(part=one)
    xs.own(part=one)
    for c in local:
        c.wait()
    swap(smeta, x, 0, 1)
    for q in (0, 1):
        mz.arrive(q)
    my[1].own()
    my[3].own()
    for q in (0, 1):
        my[0].arrive(q)
        xm.arrive(q)
    az.own(part=two)
    by.own(part=two)
    xs.own(part=two)
    for q in (0, 1):
        swap(smeta, (before, after)[q]["x"], 1 + q, 1)
    swap(strip, x, 0, 0)
    for part in (one, two):
        ay[0].own(part=part)
        bz[0].own(part=part)
        if part == one:
            mz.arrive_across()
            my[2].own()
            for q in (0, 1):
                az.arrive(q, one)
                by.arrive(q, one)
            for d in (1, 3):
                for q in (0, 1):
                    my[d].arrive(q)
    for q in (0, 1):
        az.arrive(q, two)
        by.arrive(q, two)
    ay[1].own()
    bz[1].own()
    my[0].arrive_across()
    for q in (0, 1):
        my[2].arrive(q)
    xm.arrive_across()
    swap(smeta, across["x"], 3, 1)
    for q in (0, 1):
        xs.arrive(q)
        swap(strip, (before, after)[q]["x"], 1 + q, 0)
    az.arrive_across()
    by.arrive_across()
    ay[2].own()
    bz[2].own()
    ay[3].own((1,))
    for d in (1, 3):
        my[d].arrive_across()
    xs.arrive_across()
    swap(strip, across["x"], 3, 0)
    for q in (0, 1):
        bz[0].arrive(q)
    ay[1].arrive(0)
    ay[1].arrive(1)
    ay[0].arrive(0)
    ay[0].arrive(1)
    for q in (0, 1):
        bz[1].arrive(q)
    my[2].arrive_across()
    for p, j in ((x, 0), (before["x"], 1), (after["x"], 2), (across["x"], 3)):
        swapped(smeta, p, j, 1)
        swapped(strip, p, j, 0)
    index_copies = [pltpu.make_async_copy(pmeta, p_idx, lsem.at[4]), pltpu.make_async_copy(smeta, s_idx, lsem.at[5])]
    for c in index_copies:
        c.start()
    for c in index_copies:
        c.wait()
    list_pairs()

    @pl.when(source)
    def _():
        for i in range(ROWS):
            flag = p_idx[here, 4, i]
            acc[...] += (2 * flag).astype(jnp.float32) * strip[line, i * 2].astype(jnp.float32)

    add_chunk(0, 0)
    add_chunk(1, 0)
    for q in (0, 1):
        ay[2].arrive(q)
        bz[2].arrive(q)
    bz[3].own()
    list_slots()
    add_chunk(0, 1)
    add_chunk(1, 1)
    bz[0].arrive_across()
    add_chunk(2, 0)
    ay[3].arrive(1, hold=(0, 1))
    add_chunk(3, 1)
    bz[1].arrive_across()
    add_chunk(2, 1)
    ay[1].arrive_across()
    add_chunk(1, 2)
    ay[0].arrive_across()
    add_chunk(0, 2)
    bz[2].arrive_across()
    ay[2].arrive_across()
    add_chunk(2, 2)

    @pl.when(source)
    def _():
        eye = lax.broadcasted_iota(jnp.int32, (BS, BS), 0) == lax.broadcasted_iota(jnp.int32, (BS, BS), 1)
        total = jnp.full((1, BS), jnp.sum(jnp.where(eye, acc[...], 0.0)))
        mine[0] = total
        plane_tr[lax.rem(y, 2)] = total

    far = [(dz, dy) for dz in (2, 1, 3, 0) for dy in (2, 1, 3, 0) if dz or dy]

    def tell_plane(n):
        dz, dy = far[n]
        return copy(mine.at[0], plane_tr.at[lax.rem(y, 2)], asend.at[n], arecv.at[lax.rem(y, 2)],
                    {"z": lax.rem(z + dz, 4), "y": lax.rem(y + dy, 4)})

    @pl.when(source)
    def _():
        for n in range(len(far)):
            tell_plane(n).start()

    ay[3].own((0,))
    ay[3].pass_on(1, 0)
    ay[3].pass_on(1, 1)

    for part in (one, two):
        for q in (0, 1):
            bz[3].arrive(q, part)
    for t in range(2):
        @pl.when(jnp.logical_not(source & (lax.rem(y, 2) == t)))
        def _():
            copy(mine.at[0], plane_tr.at[t], asend.at[0], arecv.at[t], {"core": 1 - core}).wait_recv()

    total = plane_tr[0] + plane_tr[1]
    mine[1] = total
    line_tr[line] = total
    others = [(dx, dc) for dx in (2, 1, 3, 0) for dc in (1, 0) if dx or dc]
    for n, (dx, dc) in enumerate(others):
        start(mine.at[1], line_tr.at[line], bsend.at[n], brecv.at[line],
              {"x": lax.rem(x + dx, 4), "core": lax.rem(core + dc, 2)})
    ay[3].arrive(0)
    ay[3].arrive_across()
    bz[3].arrive_across()
    multiply(0, ROWS)
    @pl.when(source)
    def _():
        for n in range(len(far)):
            tell_plane(n).wait_send()

    for c in sends:
        c.wait_send()

    for dx, dc in others:
        g = lax.rem(x + dx, 4) * 2 + lax.rem(core + dc, 2)
        copy(mine.at[1], line_tr.at[g], bsend.at[0], brecv.at[g], {"core": 1 - core}).wait_recv()
    result = line_tr[0]
    for g in range(1, 8):
        result = result + line_tr[g]
    trace[...] = result


def finish_kernel(table, entries, strip, panel, slots, out, redone, found, osem):
    for i in range(ROWS):
        @pl.when(table[i, BIG] == 0)
        def _():
            pltpu.make_async_copy(slots.at[i], out.at[i], osem.at[i]).start()

    def redo(i, t):
        count = table[i, t * WIDTH + PAIRS]
        sign, twice = signs(table, i)
        own = table[i, t * WIDTH + PAIRS + 1]

        def store(product):
            updated = sign * product + twice * panel[own >> 4, own & 15].astype(jnp.float32)
            redone[i, t] = updated.astype(jnp.bfloat16)

        @pl.when(count <= PAIRS)
        def _():
            store(dot_pairs(strip, panel, [table[i, t * WIDTH + n] for n in range(PAIRS)]))

        @pl.when(count > PAIRS)
        def _():
            col = table[i, t * WIDTH] & 31
            n = 0
            for e in range(32):
                entry = entries[i, e]
                found[n] = entry
                n = n + jnp.where((entry & 31) == col, 1, 0)
            found[n] = NONE
            store(lax.fori_loop(
                1, (n + 1) // 2, lambda h, p: p + dot_pairs(strip, panel, [found[2 * h], found[2 * h + 1]]),
                dot_pairs(strip, panel, [found[0], found[1]])))

    def row(i, carry):
        @pl.when(table[i, BIG] > 0)
        def _():
            def again(n, c):
                redo(i, table[i, BIG + 1 + n])
                return c

            lax.fori_loop(0, table[i, BIG], again, 0)

            def send(t, c):
                big = table[i, t * WIDTH + PAIRS] > DIRECT

                @pl.when(big)
                def _():
                    pltpu.make_async_copy(redone.at[i, t], out.at[i, t], osem.at[i]).start()

                @pl.when(jnp.logical_not(big))
                def _():
                    pltpu.make_async_copy(slots.at[i, t], out.at[i, t], osem.at[i]).start()

                return c

            lax.fori_loop(0, YCAP, send, 0)

        return carry

    lax.fori_loop(0, ROWS, row, 0)
    for i in range(ROWS):
        pltpu.make_async_copy(slots.at[i], out.at[i], osem.at[i]).wait()


def on_device(x_blocks, x_cols, x_count, y_cols, y_count, branch_flag):
    x_blocks = pltpu.with_memory_space_constraint(x_blocks.reshape(OWN, BS, BS), pltpu.HBM)
    indices = [
        pltpu.with_memory_space_constraint(a, pltpu.HBM)
        for a in (x_cols.T, x_count.T, y_count.T, branch_flag[None, :], y_cols)
    ]
    vmem, hbm, smem = (pl.BlockSpec(memory_space=m) for m in (pltpu.VMEM, pltpu.HBM, pltpu.SMEM))
    dma = pltpu.SemaphoreType.DMA
    strip, panel, slots, trace, table, entries = pl.pallas_call(
        gather_kernel,
        out_shape=[
            pltpu.VMEM((8, OWN, BS, BS), jnp.bfloat16),
            pltpu.VMEM((17, OWN, BS, BS), jnp.bfloat16),
            pltpu.VMEM((ROWS, YCAP, BS, BS), jnp.bfloat16),
            jax.ShapeDtypeStruct((1, BS), jnp.float32),
            pltpu.VMEM((ROWS, BS), jnp.int32),
            pltpu.VMEM((ROWS, BS), jnp.int32),
        ],
        in_specs=[hbm] * 6,
        out_specs=[vmem] * 6,
        scratch_shapes=[
            pltpu.VMEM((8, ROWS, BS), jnp.int32),
            pltpu.VMEM((16, ROWS, BS), jnp.int32),
            pltpu.VMEM((ROWS, BS), jnp.int32),
            pltpu.VMEM((CAP, ROWS), jnp.int32),
            pltpu.VMEM((1, ROWS), jnp.int32),
            pltpu.VMEM((1, ROWS), jnp.int32),
            pltpu.VMEM((1, ROWS), jnp.int32),
            pltpu.VMEM((ROWS, YCAP), jnp.int32),
            pltpu.SMEM((8, ROWS, BS), jnp.int32),
            pltpu.SMEM((16, ROWS, BS), jnp.int32),
            pltpu.SMEM((ROWS, BS), jnp.int32),
            pltpu.SMEM((ROWS, BS), jnp.int32),
            pltpu.VMEM((BS, BS), jnp.float32),
            pltpu.VMEM((2, 1, BS), jnp.float32),
            pltpu.VMEM((2, 1, BS), jnp.float32),
            pltpu.VMEM((8, 1, BS), jnp.float32),
            dma((15, 6)),
            dma((15, 6)),
            dma((2, 6)),
            dma((2, 6)),
            dma((2, 4)),
            dma((2, 4)),
            dma((9,)),
            dma((4,)),
            dma((15,)),
            dma((2,)),
            dma((7,)),
            dma((8,)),
        ],
        compiler_params=pltpu.CompilerParams(collective_id=0, has_side_effects=True, vmem_limit_bytes=16 << 20),
    )(x_blocks, *indices)
    out = pl.pallas_call(
        finish_kernel,
        out_shape=jax.ShapeDtypeStruct((ROWS, YCAP, BS, BS), jnp.bfloat16),
        in_specs=[smem] * 2 + [vmem] * 3,
        out_specs=hbm,
        scratch_shapes=[
            pltpu.VMEM((ROWS, YCAP, BS, BS), jnp.bfloat16),
            pltpu.SMEM((40,), jnp.int32),
            dma((ROWS,)),
        ],
        compiler_params=pltpu.CompilerParams(vmem_limit_bytes=16 << 20),
    )(table, entries, strip, panel, slots)
    return out, trace[0, :1]


def solution(mesh):
    finer = Mesh(mesh.devices.reshape(4, 4, 4, 2), ALL)
    placed = (
        P(LINE, ("x", "core"), None, None),
        P(LINE, ("x", "core")),
        P(LINE, ("x", "core")),
        P(LINE, ("x", "core")),
        P(LINE, ("x", "core")),
        P(LINE),
    )
    return jax.shard_map(
        on_device,
        mesh=finer,
        in_specs=placed,
        out_specs=(P(LINE, ("x", "core"), None, None), P()),
        check_vma=False,
    )
```
